128 devices in a mesh: blk: 16 (over x, z_hi, core), kvh: 4 (over y), section: 2 (over z_lo).
Axes of the slice: x: 4, y: 4, z: 4 (z_hi: 2, z_lo: 2; z = z_hi * 2 + z_lo), core: 2. Of those that a mesh axis runs over, the one named last changes fastest.
Arguments:
- query: bfloat16 [8192, 3072], P('blk', ('kvh', 'section')), may hold values from -110 to 110
- keys: bfloat16 [8192, 1024], P('blk', ('kvh', 'section')), may hold values from -6 to 6
- values: bfloat16 [8192, 1024], P('blk', ('kvh', 'section')), may hold values from -6 to 6
- out_grad: bfloat16 [8192, 3072], P('blk', ('kvh', 'section')), may hold values from -96 to 96
- visible_from: int32 [8192], P('blk'), may hold values from 0 to 8191, as said below
- kv_input: bfloat16 [8192, 3072], P('blk', ('kvh', 'section')), may hold values from -60 to 60
- residual_grad: bfloat16 [8192, 3072], P('blk', ('kvh', 'section')), may hold values from -3 to 3
- ffn_input: bfloat16 [8192, 3072], P('blk', ('kvh', 'section')), may hold values from -60 to 60
- kv_gain: float32 [3072], replicated, may hold values from 0.25 to 1.75
- ffn_gain: float32 [3072], replicated, may hold values from 0.25 to 1.75
- w_key: bfloat16 [3072, 1024], P(('kvh', 'section')), may hold values from -0.109375 to 0.109375
- w_value: bfloat16 [3072, 1024], P(('kvh', 'section')), may hold values from -0.109375 to 0.109375
- w_gate: bfloat16 [3072, 4096], P(None, ('kvh', 'section')), may hold values from -0.109375 to 0.109375
- w_up: bfloat16 [3072, 4096], P(None, ('kvh', 'section')), may hold values from -0.109375 to 0.109375
- w_down: bfloat16 [4096, 3072], P(('kvh', 'section')), may hold values from -0.09375 to 0.09375
Outputs:
- query_grad: bfloat16 [8192, 3072], P('blk', ('kvh', 'section'))
- input_grad: bfloat16 [8192, 3072], P('blk', ('kvh', 'section'))
- key_weight_grad: bfloat16 [16, 3072, 1024], P('blk', ('kvh', 'section'))
- value_weight_grad: bfloat16 [16, 3072, 1024], P('blk', ('kvh', 'section'))
- gate_grad: bfloat16 [16, 3072, 4096], P('blk', None, ('kvh', 'section'))
- up_grad: bfloat16 [16, 3072, 4096], P('blk', None, ('kvh', 'section'))
- down_grad: bfloat16 [16, 4096, 3072], P('blk', ('kvh', 'section'))
The draws below stay inside these ranges and needn't reach their ends.
Inputs may be any that keep to these rules, and one draw needn't show every extreme that they name: visible_from[t] is the first position of the document that holds position t: it is 0 at t = 0, never above t and never falling along t; the last position begins a document of its own.
All inputs are finite; a program needn't handle non-finite values.
Results may differ from the reference program's by a relative error of at most 0.02.
Values may be sent and summed in bfloat16 or wider, within the bound.
A program may use at most 192 MiB of HBM per device.

```python
import math
import jax
import jax.numpy as jnp
from jax import lax

D = 3072
HEAD = 128
KVHEADS = 8
GROUP = 3
FF = 4096
TOK_DEV = 512
QHEADS = 24
TOKENS = 8192
N_BLK = 16


def query_and_keys(key):
    base = jax.random.fold_in(key, 4127)
    query_seed = jax.random.fold_in(base, 1)
    keys_seed = jax.random.fold_in(base, 2)
    keys = jnp.clip(jax.random.normal(keys_seed, (TOKENS, KVHEADS * HEAD), jnp.float32), -6.0, 6.0)
    query = jnp.clip(jax.random.normal(query_seed, (TOKENS, QHEADS * HEAD), jnp.float32), -6.0, 6.0)
    return (query, keys)


def draw_query(key, part):
    return query_and_keys(key)[0].astype(jnp.bfloat16)


def draw_keys(key, part):
    return query_and_keys(key)[1].astype(jnp.bfloat16)


def draw_visible_from(key, part):
    base = jax.random.fold_in(key, 733)
    picks = jax.random.randint(base, (TOKENS,), 0, TOKENS)
    positions = jnp.arange(TOKENS, dtype=jnp.int32)
    starts = (picks < 3) | (positions == 0) | (positions == TOKENS - 1)
    return lax.cummax(jnp.where(starts, positions, 0), axis=0).astype(jnp.int32)


def scaled_rows(key, salt):
    base = jax.random.fold_in(key, salt)
    spread = math.log(10.0)
    lowest = 0.3
    row_scale = lowest * jnp.exp(jax.random.uniform(jax.random.fold_in(base, 1), (TOKENS, 1), jnp.float32, 0.0, spread))
    column_scale = lowest * jnp.exp(jax.random.uniform(jax.random.fold_in(base, 2), (1, D), jnp.float32, 0.0, spread))
    noise = jnp.clip(jax.random.normal(jax.random.fold_in(base, 3), (TOKENS, D), jnp.float32), -6.0, 6.0)
    return jnp.clip(row_scale * column_scale * noise, -60.0, 60.0).astype(jnp.bfloat16)


def draw_kv_input(key, part):
    return scaled_rows(key, 911)


def draw_ffn_input(key, part):
    return scaled_rows(key, 977)


def shard_levels(rng, extent, pieces, least, largest):
    factor_of, own = 1.0, jax.random.fold_in(rng, 6)
    for position, shards_of in pieces:
        steps = jnp.exp(jax.random.uniform(jax.random.fold_in(own, position), (shards_of,), jnp.float32, least / len(pieces), largest / len(pieces)))
        factor_of = factor_of * jnp.repeat(steps, extent[position] // shards_of).reshape([-1 if axis == position else 1 for axis in range(len(extent))])
    return factor_of


def centred(stream_key, dims, width, most, pieces=(), held_as=jnp.bfloat16):
    factor_of = shard_levels(stream_key, dims, pieces, -0.22, 0.18) if pieces else 1.0
    drawn = jax.random.normal(stream_key, dims, jnp.float32) * width * factor_of
    return jnp.minimum(jnp.maximum(drawn, -most), most).astype(held_as)


def setup_inputs(seed: int = 0) -> dict:
    splits = jax.random.split(jax.random.key(seed), 16)
    query = draw_query(jax.random.fold_in(splits[15], 71), 0)
    keys = draw_keys(jax.random.fold_in(splits[15], 71), 0)
    values = centred(splits[2], (TOKENS, KVHEADS * HEAD), 1.0, 6.0, ((0, 16), (1, 8)))
    out_grad = centred(splits[3], (TOKENS, QHEADS * HEAD), 16.0, 96.0, ((0, 16), (1, 8)))
    visible_from = draw_visible_from(jax.random.fold_in(splits[15], 71), 0)
    kv_input = draw_kv_input(jax.random.fold_in(splits[15], 71), 0)
    residual_grad = centred(splits[6], (TOKENS, D), 0.5, 3.0, ((0, 16), (1, 8)))
    ffn_input = draw_ffn_input(jax.random.fold_in(splits[15], 71), 0)
    kv_gain = jnp.clip(1.0 + 0.15 * jax.random.normal(splits[8], (D,), jnp.float32), 0.25, 1.75)
    ffn_gain = jnp.clip(1.0 + 0.15 * jax.random.normal(splits[9], (D,), jnp.float32), 0.25, 1.75)
    w_key = centred(splits[10], (D, KVHEADS * HEAD), D ** -0.5, 0.109375, ((0, 8),))
    w_value = centred(splits[11], (D, KVHEADS * HEAD), D ** -0.5, 0.109375, ((0, 8),))
    w_gate = centred(splits[12], (D, FF), D ** -0.5, 0.109375, ((1, 8),))
    w_up = centred(splits[13], (D, FF), D ** -0.5, 0.109375, ((1, 8),))
    w_down = centred(splits[14], (FF, D), FF ** -0.5, 0.09375, ((0, 8),))
    return {"query": query, "keys": keys, "values": values, "out_grad": out_grad, "visible_from": visible_from, "kv_input": kv_input, "residual_grad": residual_grad, "ffn_input": ffn_input, "kv_gain": kv_gain, "ffn_gain": ffn_gain, "w_key": w_key, "w_value": w_value, "w_gate": w_gate, "w_up": w_up, "w_down": w_down}


epsilon = 1e-06

def norm_rows(block):
    floats = block.astype(jnp.float32)
    inverse = lax.rsqrt(lax.optimization_barrier(jnp.mean(floats * floats, axis=-1, keepdims=True)) + epsilon)
    return (floats * inverse, inverse)

def rounded(entries):
    return lax.optimization_barrier(entries.astype(jnp.bfloat16)).astype(jnp.float32)

def block_product(pair):
    return jnp.dot(pair[0].T, pair[1], preferred_element_type=jnp.float32).astype(jnp.bfloat16)

def per_block(first, second):
    return lax.map(block_product, (first.reshape(N_BLK, TOK_DEV, -1), second.reshape(N_BLK, TOK_DEV, -1)))

def attention_grads(query, keys, values, out_grad, visible_from):
    scale = 1.0 / math.sqrt(HEAD)
    keys_all = keys.reshape(TOKENS, KVHEADS, HEAD).astype(jnp.float32).transpose(1, 0, 2)
    values_all = values.reshape(TOKENS, KVHEADS, HEAD).astype(jnp.float32).transpose(1, 0, 2)
    query_blocks = query.reshape(N_BLK, TOK_DEV, KVHEADS, GROUP, HEAD).transpose(0, 2, 1, 3, 4)
    grad_blocks = out_grad.reshape(N_BLK, TOK_DEV, KVHEADS, GROUP, HEAD).transpose(0, 2, 1, 3, 4)
    visible_blocks = visible_from.reshape(N_BLK, TOK_DEV)
    key_pos = jnp.arange(TOKENS, dtype=jnp.int32)

    def one_block(carry, inputs):
        query_block, grad_block, visible_block, index = inputs
        query_pos = index * TOK_DEV + jnp.arange(TOK_DEV, dtype=jnp.int32)
        visible = (key_pos[None, :] <= query_pos[:, None]) & (key_pos[None, :] >= visible_block[:, None])

        def one_head(args):
            query_head, grad_head, key_head, value_head = args
            query_float = query_head.astype(jnp.float32)
            grad_float = grad_head.astype(jnp.float32)
            scores = jnp.einsum('qsd,kd->sqk', query_float, key_head) * scale
            masked = jnp.where(visible[None], scores, -jnp.inf)
            row_max = lax.optimization_barrier(jnp.max(masked, axis=-1, keepdims=True))
            log_total = row_max + jnp.log(lax.optimization_barrier(jnp.sum(jnp.exp(masked - row_max), axis=-1, keepdims=True)))
            probs = jnp.exp(masked - log_total)
            dprobs = jnp.einsum('qsd,kd->sqk', grad_float, value_head)
            delta = lax.optimization_barrier(jnp.sum(probs * dprobs, axis=-1, keepdims=True))
            dscores = probs * (dprobs - delta)
            probs_b = rounded(probs)
            dscores_b = rounded(dscores)
            query_part = (jnp.einsum('sqk,kd->qsd', dscores_b, key_head) * scale).astype(jnp.bfloat16)
            key_part = jnp.einsum('sqk,qsd->kd', dscores_b, query_float) * scale
            value_part = jnp.einsum('sqk,qsd->kd', probs_b, grad_float)
            return (query_part, key_part, value_part)
        query_part, key_part, value_part = lax.map(one_head, (query_block, grad_block, keys_all, values_all))
        return ((carry[0] + key_part, carry[1] + value_part), query_part)
    start = (jnp.zeros((KVHEADS, TOKENS, HEAD), jnp.float32), jnp.zeros((KVHEADS, TOKENS, HEAD), jnp.float32))
    indices = jnp.arange(N_BLK, dtype=jnp.int32)
    sums, query_parts = lax.scan(one_block, start, (query_blocks, grad_blocks, visible_blocks, indices))
    query_grad = query_parts.transpose(0, 2, 1, 3, 4).reshape(TOKENS, QHEADS * HEAD)
    key_grad = sums[0].transpose(1, 0, 2).reshape(TOKENS, KVHEADS * HEAD).astype(jnp.bfloat16)
    value_grad = sums[1].transpose(1, 0, 2).reshape(TOKENS, KVHEADS * HEAD).astype(jnp.bfloat16)
    return (query_grad, key_grad, value_grad)

def reference(query, keys, values, out_grad, visible_from, kv_input, residual_grad, ffn_input, kv_gain, ffn_gain, w_key, w_value, w_gate, w_up, w_down):
    query_grad, key_grad, value_grad = attention_grads(query, keys, values, out_grad, visible_from)
    kv_hat, kv_inverse = norm_rows(kv_input)
    kv_normed = (kv_hat * kv_gain).astype(jnp.bfloat16)
    key_weight_grad = per_block(kv_normed, key_grad)
    value_weight_grad = per_block(kv_normed, value_grad)
    normed_grad = (jnp.dot(key_grad, w_key.T, preferred_element_type=jnp.float32) + jnp.dot(value_grad, w_value.T, preferred_element_type=jnp.float32)).astype(jnp.bfloat16)
    kv_scaled = kv_gain * normed_grad.astype(jnp.float32)
    y_grad = (residual_grad.astype(jnp.float32) + kv_inverse * (kv_scaled - kv_hat * lax.optimization_barrier(jnp.mean(kv_scaled * kv_hat, axis=-1, keepdims=True)))).astype(jnp.bfloat16)
    ffn_hat, ffn_inverse = norm_rows(ffn_input)
    act_in = (ffn_hat * ffn_gain).astype(jnp.bfloat16)
    gate = jnp.dot(act_in, w_gate, preferred_element_type=jnp.float32)
    upper = jnp.dot(act_in, w_up, preferred_element_type=jnp.float32)
    gate_sigmoid = jax.nn.sigmoid(gate)
    gate_silu = gate * gate_sigmoid
    hidden = (gate_silu * upper).astype(jnp.bfloat16)
    down_grad = per_block(hidden, y_grad)
    hidden_grad = jnp.dot(y_grad, w_down.T, preferred_element_type=jnp.float32)
    gate_act = (hidden_grad * upper * gate_sigmoid * (1.0 + gate * (1.0 - gate_sigmoid))).astype(jnp.bfloat16)
    up_act = (hidden_grad * gate_silu).astype(jnp.bfloat16)
    gate_grad = per_block(act_in, gate_act)
    up_grad = per_block(act_in, up_act)
    act_grad = jnp.dot(gate_act, w_gate.T, preferred_element_type=jnp.float32) + jnp.dot(up_act, w_up.T, preferred_element_type=jnp.float32)
    ffn_scaled = ffn_gain * act_grad
    input_grad = (y_grad.astype(jnp.float32) + ffn_inverse * (ffn_scaled - ffn_hat * lax.optimization_barrier(jnp.mean(ffn_scaled * ffn_hat, axis=-1, keepdims=True)))).astype(jnp.bfloat16)
    return (query_grad, input_grad, key_weight_grad, value_weight_grad, gate_grad, up_grad, down_grad)
```

```python
import functools
import math

import jax
import jax.numpy as jnp
from jax import lax
from jax.experimental import pallas as pl
from jax.experimental.pallas import tpu as pltpu
from jax.sharding import Mesh
from jax.sharding import PartitionSpec as P

HEAD = 128
BLK = ("bx", "bz", "bc")
FEAT = ("kvh", "section")
MESH = pl.DeviceIdType.MESH
LOG2E = 1.4426950408889634
VMEM = pltpu.VMEM
F32 = jnp.float32
BF16 = jnp.bfloat16

epsilon = 1e-06


def contract_rows(left, right):
    return lax.dot_general(left, right, (((0,), (0,)), ((), ())), preferred_element_type=F32)


def contract_cols(left, right):
    return lax.dot_general(left, right, (((1,), (1,)), ((), ())), preferred_element_type=F32)


def run_all(*plans):
    live = list(plans)
    while live:
        for plan in list(live):
            try:
                next(plan)
            except StopIteration:
                live.remove(plan)


def meet(peers):
    barrier = pltpu.get_barrier_semaphore()
    for peer in peers:
        pl.semaphore_signal(barrier, inc=1, device_id=peer, device_id_type=MESH)
    pl.semaphore_wait(barrier, len(peers))


class Wire:
    def __init__(self, send_sem, recv_sem):
        self.send_sem, self.recv_sem, self.sent = send_sem, recv_sem, []

    def send(self, i, src, dst, peer):
        copy = pltpu.make_async_remote_copy(
            src_ref=src,
            dst_ref=dst,
            send_sem=self.send_sem.at[i],
            recv_sem=self.recv_sem.at[i],
            device_id=peer,
            device_id_type=MESH,
        )
        copy.start()
        self.sent.append(copy)

    def got(self, i, dst, peer):
        pltpu.make_async_remote_copy(
            src_ref=dst,
            dst_ref=dst,
            send_sem=self.send_sem.at[i],
            recv_sem=self.recv_sem.at[i],
            device_id=peer,
            device_id_type=MESH,
        ).wait_recv()

    def finish(self):
        for copy in self.sent:
            copy.wait_send()


def feat_place():
    y, z = lax.axis_index("kvh"), lax.axis_index("section")
    return y, lax.rem(y + 1, 4), lax.rem(y + 3, 4), lax.rem(y + 2, 4), z, 1 - z


def feat_peers():
    y, yp, ym, y2, z, zo = feat_place()
    return [{"kvh": yp}, {"kvh": ym}, {"section": zo}]


def feat_others():
    y, yp, ym, y2, z, zo = feat_place()
    others = [{"section": zo}]
    for other in (yp, ym, y2):
        others.append({"kvh": other})
        others.append({"kvh": other, "section": zo})
    return others


def blk_place():
    x, z, c = lax.axis_index("bx"), lax.axis_index("bz"), lax.axis_index("bc")
    return x, lax.rem(x + 1, 4), lax.rem(x + 3, 4), lax.rem(x + 2, 4), z, 1 - z, c, 1 - c


def blk_peers():
    x, xp, xm, x2, z, zo, c, co = blk_place()
    return [{"bx": xp}, {"bx": xm}, {"bz": zo}, {"bc": co}]


GATHER8 = 18


def gather8(wire, x_ref, out_ref, cut):
    y, yp, ym, y2, z, zo = feat_place()
    rows, cols = x_ref.shape
    p_y, m_y, o_z = {"kvh": yp}, {"kvh": ym}, {"section": zo}
    full_a, low_a, high_a = (0, cut), (0, cut // 2), (cut // 2, cut // 2)
    rest = rows - cut
    full_b, low_b, high_b = (cut, rest), (cut, rest // 2), (cut + rest // 2, rest // 2)

    def at(sy, sz, part):
        start = pl.multiple_of((sy * 2 + sz) * cols, cols)
        return out_ref.at[pl.ds(part[0], part[1]), pl.ds(start, cols)]

    def own(i, part, peer):
        wire.send(i, x_ref.at[pl.ds(part[0], part[1]), :], at(y, z, part), peer)

    def on(i, sy, sz, part, peer):
        wire.send(i, at(sy, sz, part), at(sy, sz, part), peer)

    def got(i, sy, sz, part):
        wire.got(i, at(sy, sz, part), o_z)

    own(0, full_a, o_z)
    own(1, full_a, p_y)
    own(2, full_a, m_y)
    own(3, full_b, p_y)
    own(4, full_b, m_y)
    own(5, full_b, o_z)
    yield
    got(0, y, zo, full_a)
    on(6, y, zo, full_a, p_y)
    on(7, y, zo, full_a, m_y)
    yield
    got(1, ym, z, full_a)
    on(8, ym, z, low_a, p_y)
    yield
    got(2, yp, z, full_a)
    on(9, yp, z, high_a, m_y)
    yield
    got(3, ym, z, full_b)
    on(10, ym, z, low_b, p_y)
    on(12, ym, z, full_b, o_z)
    yield
    got(4, yp, z, full_b)
    on(11, yp, z, high_b, m_y)
    on(13, yp, z, full_b, o_z)
    yield
    got(6, ym, zo, full_a)
    on(14, ym, zo, low_a, p_y)
    yield
    got(7, yp, zo, full_a)
    on(15, yp, zo, high_a, m_y)
    yield
    got(10, y2, z, low_b)
    on(16, y2, z, low_b, o_z)
    yield
    got(11, y2, z, high_b)
    on(17, y2, z, high_b, o_z)
    yield
    got(5, y, zo, full_b)
    got(8, y2, z, low_a)
    got(9, y2, z, high_a)
    got(12, ym, zo, full_b)
    got(13, yp, zo, full_b)
    got(14, y2, zo, low_a)
    got(15, y2, zo, high_a)
    got(16, y2, zo, low_b)
    got(17, y2, zo, high_b)
    wire.finish()


GATHER16 = 19


def gather16(wire, kv_ref, out_ref):
    x, xp, xm, x2, z, zo, c, co = blk_place()
    rows = kv_ref.shape[1]
    p_x, m_x, o_z, o_c = {"bx": xp}, {"bx": xm}, {"bz": zo}, {"bc": co}
    full, low, high = (0, rows), (0, rows // 2), (rows // 2, rows // 2)

    def at(sx, sz, sc, part):
        return out_ref.at[:, sx * 4 + sz * 2 + sc, pl.ds(part[0], part[1]), :]

    def own(i, peer):
        wire.send(i, kv_ref, at(x, z, c, full), peer)

    def on(i, sx, sz, part, peer):
        wire.send(i, at(sx, sz, c, part), at(sx, sz, c, part), peer)

    def got(i, sx, sz, part, sc=None):
        wire.got(i, at(sx, sz, c if sc is None else sc, part), o_z)

    own(0, o_z)
    own(1, p_x)
    own(2, m_x)
    own(3, o_c)
    yield
    got(0, x, zo, full)
    on(4, x, zo, full, p_x)
    on(5, x, zo, full, m_x)
    on(6, x, zo, full, o_c)
    yield
    got(1, xm, z, full)
    on(7, xm, z, low, p_x)
    on(8, xm, z, full, o_c)
    yield
    got(2, xp, z, full)
    on(9, xp, z, high, m_x)
    on(10, xp, z, full, o_c)
    yield
    got(4, xm, zo, full)
    on(11, xm, zo, low, p_x)
    on(12, xm, zo, full, o_c)
    yield
    got(5, xp, zo, full)
    on(13, xp, zo, high, m_x)
    on(14, xp, zo, full, o_c)
    yield
    got(7, x2, z, low)
    on(15, x2, z, low, o_c)
    yield
    got(9, x2, z, high)
    on(16, x2, z, high, o_c)
    yield
    got(11, x2, zo, low)
    on(17, x2, zo, low, o_c)
    yield
    got(13, x2, zo, high)
    on(18, x2, zo, high, o_c)
    yield
    got(3, x, z, full, co)
    got(6, x, zo, full, co)
    got(8, xm, z, full, co)
    got(10, xp, z, full, co)
    got(12, xm, zo, full, co)
    got(14, xp, zo, full, co)
    got(15, x2, z, low, co)
    got(16, x2, z, high, co)
    got(17, x2, zo, low, co)
    got(18, x2, zo, high, co)
    wire.finish()


def first_kernel(kv_ref, ffn_ref, kv_out, ffn_out, s0, r0, s1, r1, local):
    x, xp, xm, x2, z, zo, c, co = blk_place()
    y, yp, ym, y2, sz, szo = feat_place()
    cols = ffn_ref.shape[1]
    meet(blk_peers() + feat_peers())
    keep_kv = pltpu.make_async_copy(kv_ref, kv_out.at[:, x * 4 + z * 2 + c], local.at[0])
    keep_ffn = pltpu.make_async_copy(
        ffn_ref,
        ffn_out.at[:, pl.ds(pl.multiple_of((y * 2 + sz) * cols, cols), cols)],
        local.at[1],
    )
    wire_kv, wire_ffn = Wire(s0, r0), Wire(s1, r1)
    kv_plan = gather16(wire_kv, kv_ref, kv_out)
    ffn_plan = gather8(wire_ffn, ffn_ref, ffn_out, ffn_ref.shape[0] * 3 // 4)
    next(kv_plan)
    next(ffn_plan)
    keep_kv.start()
    keep_ffn.start()
    run_all(kv_plan, ffn_plan)
    keep_kv.wait()
    keep_ffn.wait()


def gather_first(kv, ffn):
    rows, cols = ffn.shape
    return pl.pallas_call(
        first_kernel,
        name="gather_first",
        out_shape=(
            jax.ShapeDtypeStruct((2, 16, *kv.shape[1:]), kv.dtype),
            jax.ShapeDtypeStruct((rows, 8 * cols), ffn.dtype),
        ),
        in_specs=[pl.BlockSpec(memory_space=VMEM)] * 2,
        out_specs=(pl.BlockSpec(memory_space=pl.ANY),) * 2,
        scratch_shapes=[
            pltpu.SemaphoreType.DMA((GATHER16,)),
            pltpu.SemaphoreType.DMA((GATHER16,)),
            pltpu.SemaphoreType.DMA((GATHER8,)),
            pltpu.SemaphoreType.DMA((GATHER8,)),
            pltpu.SemaphoreType.DMA((2,)),
        ],
        compiler_params=pltpu.CompilerParams(collective_id=1, has_side_effects=True),
    )(kv, ffn)


def gather_kernel(x_ref, out_ref, s0, r0, local):
    y, yp, ym, y2, z, zo = feat_place()
    rows, cols = x_ref.shape
    meet(feat_peers())
    keep = pltpu.make_async_copy(
        x_ref,
        out_ref.at[:, pl.ds(pl.multiple_of((y * 2 + z) * cols, cols), cols)],
        local.at[0],
    )
    plan = gather8(Wire(s0, r0), x_ref, out_ref, rows // 2)
    next(plan)
    keep.start()
    run_all(plan)
    keep.wait()


def gather_features(x, collective_id):
    rows, cols = x.shape
    return pl.pallas_call(
        gather_kernel,
        name=f"gather_{collective_id}",
        out_shape=jax.ShapeDtypeStruct((rows, 8 * cols), x.dtype),
        in_specs=[pl.BlockSpec(memory_space=VMEM)],
        out_specs=pl.BlockSpec(memory_space=pl.ANY),
        scratch_shapes=[
            pltpu.SemaphoreType.DMA((GATHER8,)),
            pltpu.SemaphoreType.DMA((GATHER8,)),
            pltpu.SemaphoreType.DMA((1,)),
        ],
        compiler_params=pltpu.CompilerParams(collective_id=collective_id, has_side_effects=True),
    )(x)


def add(*terms):
    total = terms[0].astype(F32)
    for term in terms[1:]:
        total = total + term.astype(F32)
    return total


def ring_plan(wire, first, far, plus, minus, half, ring, near_p, near_m, far_p, far_m, p, m):
    low, high = half
    wire.send(first + 0, high(far), high(far_m), p)
    wire.send(first + 1, low(far), low(far_p), m)
    wire.send(first + 2, low(plus), low(near_m), p)
    wire.send(first + 3, high(minus), high(near_p), m)
    yield
    wire.got(first + 0, high(far_m), p)
    high(plus)[...] = add(high(plus)[...], high(far_m)[...]).astype(BF16)
    wire.send(first + 4, high(plus), high(near_m), p)
    yield
    wire.got(first + 1, low(far_p), p)
    low(minus)[...] = add(low(minus)[...], low(far_p)[...]).astype(BF16)
    wire.send(first + 5, low(minus), low(near_p), m)
    yield
    wire.got(first + 2, low(near_m), p)
    wire.got(first + 3, high(near_p), p)
    wire.got(first + 4, high(near_m), p)
    wire.got(first + 5, low(near_p), p)


SCATTER16 = 8 + 6 + 6 + 1


def scatter16_kernel(part_ref, out_ref, twin, acc, near, far, zsend, zrecv, ssem, rsem):
    x, xp, xm, x2, z, zo, c, co = blk_place()
    rows = part_ref.shape[2]
    half_rows = rows // 2
    wire = Wire(ssem, rsem)
    meet(blk_peers())
    order = [(tx, tz) for tz in (zo, z) for tx in (x2, xp, xm, x)]
    for i, (tx, tz) in enumerate(order):
        wire.send(i, part_ref.at[:, tx * 4 + tz * 2 + co], twin.at[i], {"bc": co})

    def merge(i):
        tx, tz = order[i]
        wire.got(i, twin.at[i], {"bc": co})
        acc[i] = add(part_ref[:, tx * 4 + tz * 2 + c], twin[i]).astype(BF16)

    def low(ref):
        return ref.at[:, pl.ds(0, half_rows), :]

    def high(ref):
        return ref.at[:, pl.ds(half_rows, half_rows), :]

    def ring(plane):
        base = plane * 4
        return ring_plan(
            wire,
            8 + plane * 6,
            acc.at[base],
            acc.at[base + 1],
            acc.at[base + 2],
            (low, high),
            None,
            near.at[plane, 0],
            near.at[plane, 1],
            far.at[plane, 0],
            far.at[plane, 1],
            {"bx": xp},
            {"bx": xm},
        )

    for i in range(3):
        merge(i)
    outer = ring(0)
    next(outer)
    for i in range(4, 7):
        merge(i)
    inner = ring(1)
    next(inner)
    merge(3)
    merge(7)
    run_all(outer)
    zsend[...] = add(acc[3], near[0, 0], near[0, 1]).astype(BF16)
    wire.send(20, zsend, zrecv, {"bz": zo})
    run_all(inner)
    total = add(acc[7], near[1, 0], near[1, 1])
    wire.got(20, zrecv, {"bz": zo})
    out_ref[...] = (total + zrecv[...].astype(F32)).astype(BF16)
    wire.finish()


def scatter_blocks(parts):
    _, _, rows, width = parts.shape
    shard = (2, rows, width)
    return pl.pallas_call(
        scatter16_kernel,
        name="scatter_blocks",
        out_shape=jax.ShapeDtypeStruct(shard, BF16),
        in_specs=[pl.BlockSpec(memory_space=VMEM)],
        out_specs=pl.BlockSpec(memory_space=VMEM),
        scratch_shapes=[
            VMEM((8, *shard), BF16),
            VMEM((8, *shard), BF16),
            VMEM((2, 2, *shard), BF16),
            VMEM((2, 2, *shard), BF16),
            VMEM(shard, BF16),
            VMEM(shard, BF16),
            pltpu.SemaphoreType.DMA((SCATTER16,)),
            pltpu.SemaphoreType.DMA((SCATTER16,)),
        ],
        compiler_params=pltpu.CompilerParams(collective_id=2, has_side_effects=True),
    )(parts)


def sum_stat_kernel(x_ref, out_ref, slots, ssem, rsem):
    others = feat_others()
    meet(others)
    wire = Wire(ssem, rsem)
    for i, peer in enumerate(others):
        wire.send(i, x_ref, slots.at[i], peer)
    total = x_ref[...]
    for i, peer in enumerate(others):
        wire.got(i, slots.at[i], peer)
        total = total + slots[i]
    out_ref[...] = total
    wire.finish()


def sum_stat(x, collective_id):
    return pl.pallas_call(
        sum_stat_kernel,
        name=f"sum_stat_{collective_id}",
        out_shape=jax.ShapeDtypeStruct(x.shape, F32),
        in_specs=[pl.BlockSpec(memory_space=VMEM)],
        out_specs=pl.BlockSpec(memory_space=VMEM),
        scratch_shapes=[
            VMEM((7, *x.shape), F32),
            pltpu.SemaphoreType.DMA((7,)),
            pltpu.SemaphoreType.DMA((7,)),
        ],
        compiler_params=pltpu.CompilerParams(collective_id=collective_id, has_side_effects=True),
    )(x)


SCATTER8 = 13 + 4 + 6


def scatter8_kernel(
    part_ref, stat_ref, out_ref, stat_out, acc, zbuf, near, far, zsend, zrecv, slots, ssem, rsem, s1, r1
):
    y, yp, ym, y2, z, zo = feat_place()
    rows, cols = out_ref.shape
    cut = rows // 2
    quarter = cut // 2
    others = feat_others()
    meet(others)
    wire, stat_wire = Wire(ssem, rsem), Wire(s1, r1)
    for i, peer in enumerate(others):
        stat_wire.send(i, stat_ref, slots.at[i], peer)

    def cols_of(ty, tz):
        return pl.ds(pl.multiple_of((ty * 2 + tz) * cols, cols), cols)

    def low(ref):
        return ref.at[pl.ds(0, quarter), :]

    def high(ref):
        return ref.at[pl.ds(quarter, quarter), :]

    def ring(plane, first):
        return ring_plan(
            wire,
            first,
            acc.at[plane, 0],
            acc.at[plane, 1],
            acc.at[plane, 2],
            (low, high),
            None,
            near.at[plane, 0],
            near.at[plane, 1],
            far.at[plane, 0],
            far.at[plane, 1],
            {"kvh": yp},
            {"kvh": ym},
        )

    turn = (y2, yp, ym, y)
    for i, ty in enumerate(turn):
        wire.send(i, part_ref.at[pl.ds(cut, cut), cols_of(ty, zo)], zbuf.at[i], {"section": zo})
    for i, ty in enumerate(turn):
        acc[0, i] = part_ref[pl.ds(0, cut), cols_of(ty, zo)]
    outer = ring(0, 4)
    next(outer)
    for i, ty in enumerate(turn):
        acc[1, i] = part_ref[pl.ds(0, cut), cols_of(ty, z)]
    inner = ring(1, 10)
    next(inner)
    for i, ty in enumerate(turn):
        wire.got(i, zbuf.at[i], {"section": zo})
        acc[2, i] = add(part_ref[pl.ds(cut, cut), cols_of(ty, z)], zbuf[i]).astype(BF16)
    last = ring(2, 16)
    next(last)
    run_all(outer)
    zsend[...] = add(acc[0, 3], near[0, 0], near[0, 1]).astype(BF16)
    wire.send(22, zsend, zrecv, {"section": zo})
    run_all(inner)
    total = add(acc[1, 3], near[1, 0], near[1, 1])
    run_all(last)
    out_ref[pl.ds(cut, cut), :] = add(acc[2, 3], near[2, 0], near[2, 1])
    stat = stat_ref[...]
    for i, peer in enumerate(others):
        stat_wire.got(i, slots.at[i], peer)
        stat = stat + slots[i]
    stat_out[...] = stat
    wire.got(22, zrecv, {"section": zo})
    out_ref[pl.ds(0, cut), :] = total + zrecv[...].astype(F32)
    wire.finish()
    stat_wire.finish()


def scatter_features(part, stat, collective_id):
    rows, width = part.shape
    cols = width // 8
    cut = rows // 2
    return pl.pallas_call(
        scatter8_kernel,
        name="scatter_features",
        out_shape=(
            jax.ShapeDtypeStruct((rows, cols), F32),
            jax.ShapeDtypeStruct(stat.shape, F32),
        ),
        in_specs=[pl.BlockSpec(memory_space=VMEM)] * 2,
        out_specs=(pl.BlockSpec(memory_space=VMEM),) * 2,
        scratch_shapes=[
            VMEM((3, 4, cut, cols), BF16),
            VMEM((4, cut, cols), BF16),
            VMEM((3, 2, cut, cols), BF16),
            VMEM((3, 2, cut, cols), BF16),
            VMEM((cut, cols), BF16),
            VMEM((cut, cols), BF16),
            VMEM((7, *stat.shape), F32),
            pltpu.SemaphoreType.DMA((SCATTER8,)),
            pltpu.SemaphoreType.DMA((SCATTER8,)),
            pltpu.SemaphoreType.DMA((7,)),
            pltpu.SemaphoreType.DMA((7,)),
        ],
        compiler_params=pltpu.CompilerParams(collective_id=collective_id, has_side_effects=True),
    )(part, stat)


MASKED = -1e30
START = -1e29


def attention_kernel(
    span_ref, seen_ref, q_ref, g_ref, kv_ref, dq_ref, dkv_ref,
    q_cat, g_cat, q_t, g_t, run_max, run_sum, run_dot, dq_t, *, tile, scale
):
    rows = q_ref.shape[0]
    group = q_ref.shape[1] // HEAD
    own, lowest, highest = span_ref[0], span_ref[1], span_ref[2]
    to_log2 = scale * LOG2E
    for h in range(group):
        for src, cat, turned in ((q_ref, q_cat, q_t), (g_ref, g_cat, g_t)):
            block = src[:, h * HEAD : (h + 1) * HEAD]
            cat[h * rows : (h + 1) * rows, :] = block
            turned[:, h * rows : (h + 1) * rows] = block.astype(F32).T.astype(BF16)
    run_max[...] = jnp.full_like(run_max, START)
    run_sum[...] = jnp.zeros_like(run_sum)
    run_dot[...] = jnp.zeros_like(run_dot)
    dq_t[...] = jnp.zeros_like(dq_t)

    tiles = dkv_ref.shape[1] // tile
    first = lowest // tile
    last = ((own + 1) * rows) // tile
    whole_from = jnp.minimum((highest + tile - 1) // tile, (own * rows) // tile)
    whole_to = (own * rows) // tile

    def part(j):
        return pl.ds(pl.multiple_of(j * tile, tile), tile)

    def lanes(h):
        return pl.ds(h * rows, rows)

    def scores(j, h, masked):
        keys = kv_ref[0, part(j), :]
        value = jnp.dot(keys, q_t[:, lanes(h)], preferred_element_type=F32) * to_log2
        if masked:
            key_pos = j * tile + lax.broadcasted_iota(jnp.int32, (tile, rows), 0)
            query_pos = own * rows + lax.broadcasted_iota(jnp.int32, (tile, rows), 1)
            visible = (key_pos <= query_pos) & (key_pos >= seen_ref[...])
            value = jnp.where(visible, value, MASKED)
        return value

    def products(j, h):
        return jnp.dot(kv_ref[1, part(j), :], g_t[:, lanes(h)], preferred_element_type=F32)

    def stats(j, masked):
        for h in range(group):
            value = scores(j, h, masked).reshape(tile // 8, 8, rows)
            dprobs = products(j, h).reshape(tile // 8, 8, rows)
            before = run_max[:, lanes(h)]
            now = jnp.maximum(before, jnp.max(value, axis=0))
            shrink = jnp.exp2(before - now)
            probs = jnp.exp2(value - now[None])
            run_max[:, lanes(h)] = now
            run_sum[:, lanes(h)] = run_sum[:, lanes(h)] * shrink + jnp.sum(probs, axis=0)
            run_dot[:, lanes(h)] = run_dot[:, lanes(h)] * shrink + jnp.sum(probs * dprobs, axis=0)

    def grads(j, masked):
        keys = kv_ref[0, part(j), :]
        value_part = jnp.zeros((tile, HEAD), F32)
        key_part = jnp.zeros((tile, HEAD), F32)
        for h in range(group):
            value = scores(j, h, masked)
            probs = jnp.exp2(value - run_max[0:1, lanes(h)])
            dscores = (probs * (products(j, h) - run_dot[0:1, lanes(h)])).astype(BF16)
            value_part = value_part + jnp.dot(
                probs.astype(BF16), g_cat[lanes(h), :], preferred_element_type=F32
            )
            key_part = key_part + jnp.dot(dscores, q_cat[lanes(h), :], preferred_element_type=F32)
            dq_t[:, lanes(h)] += contract_rows(keys, dscores)
        dkv_ref[0, part(j), :] = (key_part * scale).astype(BF16)
        dkv_ref[1, part(j), :] = value_part.astype(BF16)

    def sweep(body):
        lax.fori_loop(first, whole_from, lambda j, _: (body(j, True), 0)[1], 0)
        lax.fori_loop(jnp.maximum(whole_from, first), whole_to, lambda j, _: (body(j, False), 0)[1], 0)
        lax.fori_loop(jnp.maximum(whole_to, first), last, lambda j, _: (body(j, True), 0)[1], 0)

    sweep(stats)
    peak = jnp.max(run_max[...], axis=0, keepdims=True)
    factor = jnp.exp2(run_max[...] - peak)
    total = jnp.sum(run_sum[...] * factor, axis=0, keepdims=True)
    delta = jnp.sum(run_dot[...] * factor, axis=0, keepdims=True) / total
    run_max[0:1, :] = peak + jnp.log(total) * LOG2E
    run_dot[0:1, :] = delta

    def clear(j, _):
        dkv_ref[:, part(j), :] = jnp.zeros((2, tile, HEAD), BF16)
        return 0

    lax.fori_loop(0, first, clear, 0)
    lax.fori_loop(last, tiles, clear, 0)
    sweep(grads)
    for h in range(group):
        dq_ref[:, h * HEAD : (h + 1) * HEAD] = (dq_t[:, lanes(h)] * scale).T.astype(BF16)


def attention(query, out_grad, kv, visible_from, own, tile=256):
    rows, width = query.shape
    group = width // HEAD
    span = jnp.stack((own, visible_from[0], visible_from[-1])).astype(jnp.int32)
    cat = VMEM((group * rows, HEAD), BF16)
    turned = VMEM((HEAD, group * rows), BF16)
    stat = VMEM((8, group * rows), F32)
    return pl.pallas_call(
        functools.partial(attention_kernel, tile=tile, scale=1.0 / math.sqrt(HEAD)),
        name="attention",
        out_shape=(
            jax.ShapeDtypeStruct((rows, width), BF16),
            jax.ShapeDtypeStruct(kv.shape, BF16),
        ),
        in_specs=[pl.BlockSpec(memory_space=pltpu.SMEM)] + [pl.BlockSpec(memory_space=VMEM)] * 4,
        out_specs=(pl.BlockSpec(memory_space=VMEM),) * 2,
        scratch_shapes=[
            cat, cat, turned, turned, stat, stat, stat, VMEM((HEAD, group * rows), F32),
        ],
    )(span, visible_from.reshape(1, rows), query, out_grad, kv)


def inverse_of(squares, width):
    return lax.rsqrt(squares / width + epsilon)


def on_device(
    query, keys, values, out_grad, visible_from, kv_input, residual_grad, ffn_input,
    kv_gain, ffn_gain, w_key, w_value, w_gate, w_up, w_down,
):
    rows, part_width = query.shape
    width = kv_gain.shape[0]
    own = lax.axis_index(BLK)
    offset = lax.axis_index(FEAT) * part_width

    def mine(vector):
        return lax.dynamic_slice_in_dim(vector, offset, part_width, 0)

    every, ffn_full = gather_first(jnp.stack((keys, values)), ffn_input)
    blocks = every.shape[1]
    query_grad, dkv = attention(
        query, out_grad, every.reshape(2, blocks * rows, HEAD), visible_from, own
    )
    key_value = scatter_blocks(dkv.reshape(2, blocks, rows, HEAD))
    all_heads = gather_features(key_value.reshape(2 * rows, HEAD), 3)
    key_heads, value_heads = all_heads[:rows], all_heads[rows:]
    normed = (contract_cols(key_heads, w_key) + contract_cols(value_heads, w_value)).astype(BF16)
    kv_floats = kv_input.astype(F32)
    kv_scaled = mine(kv_gain) * normed.astype(F32)
    squares = jnp.sum(kv_floats * kv_floats, axis=-1)
    dots = jnp.sum(kv_scaled * kv_floats, axis=-1)
    sums = sum_stat(jnp.stack((squares, dots)).reshape(8, -1), 4).reshape(2, rows, 1)
    kv_inverse = inverse_of(sums[0], width)
    kv_hat = kv_floats * kv_inverse
    y_slice = (
        residual_grad.astype(F32)
        + kv_inverse * (kv_scaled - kv_hat * (sums[1] * kv_inverse / width))
    ).astype(BF16)
    y_full = gather_features(y_slice, 5)
    kv_normed = (kv_hat * mine(kv_gain)).astype(BF16)
    key_weight_grad = contract_rows(kv_normed, key_heads).astype(BF16)[None]
    value_weight_grad = contract_rows(kv_normed, value_heads).astype(BF16)[None]

    ffn_floats = ffn_full.astype(F32)
    ffn_inverse = inverse_of(jnp.sum(ffn_floats * ffn_floats, axis=-1, keepdims=True), width)
    ffn_scale = ffn_floats * ffn_inverse * ffn_gain
    act_in = ffn_scale.astype(BF16)
    gate = jnp.dot(act_in, w_gate, preferred_element_type=F32)
    upper = jnp.dot(act_in, w_up, preferred_element_type=F32)
    gate_sigmoid = jax.nn.sigmoid(gate)
    gate_silu = gate * gate_sigmoid
    hidden = (gate_silu * upper).astype(BF16)
    down_grad = contract_rows(hidden, y_full).astype(BF16)[None]
    hidden_grad = contract_cols(y_full, w_down)
    gate_act = (hidden_grad * upper * gate_sigmoid * (1.0 + gate * (1.0 - gate_sigmoid))).astype(BF16)
    up_act = (hidden_grad * gate_silu).astype(BF16)
    gate_grad = contract_rows(act_in, gate_act).astype(BF16)[None]
    up_grad = contract_rows(act_in, up_act).astype(BF16)[None]
    partial_value = contract_cols(gate_act, w_gate) + contract_cols(up_act, w_up)
    row_part = jnp.sum(partial_value * ffn_scale, axis=-1).reshape(-1, HEAD)
    row_part = jnp.concatenate((row_part, jnp.zeros_like(row_part)), axis=0)
    act_slice, row_total = scatter_features(partial_value.astype(BF16), row_part, 6)
    correction = row_total[: rows // HEAD].reshape(rows, 1) / width
    hat_slice = ffn_input.astype(F32) * ffn_inverse
    input_grad = (
        y_slice.astype(F32) + ffn_inverse * (mine(ffn_gain) * act_slice - hat_slice * correction)
    ).astype(BF16)
    return (
        query_grad, input_grad, key_weight_grad, value_weight_grad, gate_grad, up_grad, down_grad,
    )


def solution(mesh):
    finer = Mesh(
        mesh.devices.reshape(4, 2, 2, mesh.shape["kvh"], mesh.shape["section"]),
        (*BLK, *FEAT),
    )
    tokens = P(BLK, FEAT)
    placed = (
        tokens, tokens, tokens, tokens, P(BLK), tokens, tokens, tokens, P(), P(),
        P(FEAT, None), P(FEAT, None), P(None, FEAT), P(None, FEAT), P(FEAT, None),
    )
    return jax.shard_map(
        on_device,
        mesh=finer,
        in_specs=placed,
        out_specs=(
            tokens,
            tokens,
            P(BLK, FEAT, None),
            P(BLK, FEAT, None),
            P(BLK, None, FEAT),
            P(BLK, None, FEAT),
            P(BLK, FEAT, None),
        ),
        check_vma=False,
    )
```

```python
import functools
import math

import jax
import jax.numpy as jnp
from jax import lax
from jax.experimental import pallas as pl
from jax.experimental.pallas import tpu as pltpu
from jax.sharding import Mesh
from jax.sharding import PartitionSpec as P

HEAD = 128
BLK = ("bx", "bz", "bc")
FEAT = ("kvh", "section")
MESH = pl.DeviceIdType.MESH
LOG2E = 1.4426950408889634
VMEM = pltpu.VMEM
F32 = jnp.float32
BF16 = jnp.bfloat16

epsilon = 1e-06


def contract_rows(left, right):
    return lax.dot_general(left, right, (((0,), (0,)), ((), ())), preferred_element_type=F32)


def contract_cols(left, right):
    return lax.dot_general(left, right, (((1,), (1,)), ((), ())), preferred_element_type=F32)


def run_all(*plans):
    live = list(plans)
    while live:
        for plan in list(live):
            try:
                next(plan)
            except StopIteration:
                live.remove(plan)


def run_some(plan):
    try:
        next(plan)
    except StopIteration:
        pass


def run_first(main, *others):
    for _ in main:
        for other in others:
            run_some(other)


def chain(*plans):
    for plan in plans:
        yield from plan


def meet(peers):
    barrier = pltpu.get_barrier_semaphore()
    for peer in peers:
        pl.semaphore_signal(barrier, inc=1, device_id=peer, device_id_type=MESH)
    pl.semaphore_wait(barrier, len(peers))


class Wire:
    def __init__(self, send_sem, recv_sem):
        self.send_sem, self.recv_sem, self.sent = send_sem, recv_sem, []

    def send(self, i, src, dst, peer):
        copy = pltpu.make_async_remote_copy(
            src_ref=src,
            dst_ref=dst,
            send_sem=self.send_sem.at[i],
            recv_sem=self.recv_sem.at[i],
            device_id=peer,
            device_id_type=MESH,
        )
        copy.start()
        self.sent.append(copy)

    def got(self, i, dst, peer):
        pltpu.make_async_remote_copy(
            src_ref=dst,
            dst_ref=dst,
            send_sem=self.send_sem.at[i],
            recv_sem=self.recv_sem.at[i],
            device_id=peer,
            device_id_type=MESH,
        ).wait_recv()

    def finish(self):
        for copy in self.sent:
            copy.wait_send()


def feat_place():
    y, z = lax.axis_index("kvh"), lax.axis_index("section")
    return y, lax.rem(y + 1, 4), lax.rem(y + 3, 4), lax.rem(y + 2, 4), z, 1 - z


def feat_peers():
    y, yp, ym, y2, z, zo = feat_place()
    return [{"kvh": yp}, {"kvh": ym}, {"section": zo}]


def feat_others():
    y, yp, ym, y2, z, zo = feat_place()
    others = [{"section": zo}]
    for other in (yp, ym, y2):
        others.append({"kvh": other})
        others.append({"kvh": other, "section": zo})
    return others


def blk_place():
    x, z, c = lax.axis_index("bx"), lax.axis_index("bz"), lax.axis_index("bc")
    return x, lax.rem(x + 1, 4), lax.rem(x + 3, 4), lax.rem(x + 2, 4), z, 1 - z, c, 1 - c


def blk_peers():
    x, xp, xm, x2, z, zo, c, co = blk_place()
    return [{"bx": xp}, {"bx": xm}, {"bz": zo}, {"bc": co}]


GATHER8 = 18


def gather8(wire, x_ref, out_ref, cut):
    y, yp, ym, y2, z, zo = feat_place()
    rows, cols = x_ref.shape
    p_y, m_y, o_z = {"kvh": yp}, {"kvh": ym}, {"section": zo}
    full_a, low_a, high_a = (0, cut), (0, cut // 2), (cut // 2, cut // 2)
    rest = rows - cut
    full_b, low_b, high_b = (cut, rest), (cut, rest // 2), (cut + rest // 2, rest // 2)

    def at(sy, sz, part):
        start = pl.multiple_of((sy * 2 + sz) * cols, cols)
        return out_ref.at[pl.ds(part[0], part[1]), pl.ds(start, cols)]

    def own(i, part, peer):
        wire.send(i, x_ref.at[pl.ds(part[0], part[1]), :], at(y, z, part), peer)

    def on(i, sy, sz, part, peer):
        wire.send(i, at(sy, sz, part), at(sy, sz, part), peer)

    def got(i, sy, sz, part):
        wire.got(i, at(sy, sz, part), o_z)

    own(0, full_a, o_z)
    own(1, full_a, p_y)
    own(2, full_a, m_y)
    own(3, full_b, p_y)
    own(4, full_b, m_y)
    own(5, full_b, o_z)
    yield
    got(0, y, zo, full_a)
    on(6, y, zo, full_a, p_y)
    on(7, y, zo, full_a, m_y)
    yield
    got(1, ym, z, full_a)
    on(8, ym, z, low_a, p_y)
    yield
    got(2, yp, z, full_a)
    on(9, yp, z, high_a, m_y)
    yield
    got(3, ym, z, full_b)
    on(10, ym, z, low_b, p_y)
    on(12, ym, z, full_b, o_z)
    yield
    got(4, yp, z, full_b)
    on(11, yp, z, high_b, m_y)
    on(13, yp, z, full_b, o_z)
    yield
    got(5, y, zo, full_b)
    yield y, False
    got(6, ym, zo, full_a)
    on(14, ym, zo, low_a, p_y)
    yield
    got(7, yp, zo, full_a)
    on(15, yp, zo, high_a, m_y)
    yield
    got(12, ym, zo, full_b)
    yield ym, False
    got(10, y2, z, low_b)
    on(16, y2, z, low_b, o_z)
    yield
    got(11, y2, z, high_b)
    on(17, y2, z, high_b, o_z)
    yield
    got(13, yp, zo, full_b)
    yield yp, False
    got(8, y2, z, low_a)
    got(9, y2, z, high_a)
    got(14, y2, zo, low_a)
    got(15, y2, zo, high_a)
    got(16, y2, zo, low_b)
    got(17, y2, zo, high_b)
    wire.finish()
    yield y2, True


GATHER16 = 19


def gather16(wire, kv_ref, out_ref):
    x, xp, xm, x2, z, zo, c, co = blk_place()
    rows = kv_ref.shape[1]
    p_x, m_x, o_z, o_c = {"bx": xp}, {"bx": xm}, {"bz": zo}, {"bc": co}
    full, low, high = (0, rows), (0, rows // 2), (rows // 2, rows // 2)

    def at(sx, sz, sc, part):
        return out_ref.at[:, sx * 4 + sz * 2 + sc, pl.ds(part[0], part[1]), :]

    def own(i, peer):
        wire.send(i, kv_ref, at(x, z, c, full), peer)

    def on(i, sx, sz, part, peer):
        wire.send(i, at(sx, sz, c, part), at(sx, sz, c, part), peer)

    def got(i, sx, sz, part, sc=None):
        wire.got(i, at(sx, sz, c if sc is None else sc, part), o_z)

    own(0, o_z)
    own(1, p_x)
    own(2, m_x)
    own(3, o_c)
    yield
    got(0, x, zo, full)
    on(4, x, zo, full, p_x)
    on(5, x, zo, full, m_x)
    on(6, x, zo, full, o_c)
    yield
    got(1, xm, z, full)
    on(7, xm, z, low, p_x)
    on(8, xm, z, full, o_c)
    yield
    got(2, xp, z, full)
    on(9, xp, z, high, m_x)
    on(10, xp, z, full, o_c)
    yield
    got(4, xm, zo, full)
    on(11, xm, zo, low, p_x)
    on(12, xm, zo, full, o_c)
    yield
    got(5, xp, zo, full)
    on(13, xp, zo, high, m_x)
    on(14, xp, zo, full, o_c)
    yield
    got(7, x2, z, low)
    on(15, x2, z, low, o_c)
    yield
    got(9, x2, z, high)
    on(16, x2, z, high, o_c)
    yield
    got(11, x2, zo, low)
    on(17, x2, zo, low, o_c)
    yield
    got(13, x2, zo, high)
    on(18, x2, zo, high, o_c)
    yield
    got(3, x, z, full, co)
    got(6, x, zo, full, co)
    got(8, xm, z, full, co)
    got(10, xp, z, full, co)
    got(12, xm, zo, full, co)
    got(14, xp, zo, full, co)
    got(15, x2, z, low, co)
    got(16, x2, z, high, co)
    got(17, x2, zo, low, co)
    got(18, x2, zo, high, co)
    wire.finish()


def first_kernel(key_ref, value_ref, kv_out, own, s0, r0, local):
    x, xp, xm, x2, z, zo, c, co = blk_place()
    loads = [
        pltpu.make_async_copy(key_ref, own.at[0], local.at[0]),
        pltpu.make_async_copy(value_ref, own.at[1], local.at[1]),
    ]
    for load in loads:
        load.start()
    meet(blk_peers())
    for load in loads:
        load.wait()
    keep = pltpu.make_async_copy(own, kv_out.at[:, x * 4 + z * 2 + c], local.at[2])
    plan = gather16(Wire(s0, r0), own, kv_out)
    next(plan)
    keep.start()
    run_all(plan)
    keep.wait()


def gather_first(keys, values):
    rows, width = keys.shape
    return pl.pallas_call(
        first_kernel,
        name="gather_first",
        out_shape=VMEM((2, 16, rows, width), keys.dtype),
        in_specs=[pl.BlockSpec(memory_space=pltpu.HBM)] * 2,
        out_specs=pl.BlockSpec(memory_space=VMEM),
        scratch_shapes=[
            VMEM((2, rows, width), keys.dtype),
            pltpu.SemaphoreType.DMA((GATHER16,)),
            pltpu.SemaphoreType.DMA((GATHER16,)),
            pltpu.SemaphoreType.DMA((3,)),
        ],
        compiler_params=pltpu.CompilerParams(
            collective_id=1, has_side_effects=True, vmem_limit_bytes=16_000_000
        ),
    )(
        pltpu.with_memory_space_constraint(keys, pltpu.HBM),
        pltpu.with_memory_space_constraint(values, pltpu.HBM),
    )


def add(*terms):
    total = terms[0].astype(F32)
    for term in terms[1:]:
        total = total + term.astype(F32)
    return total


class Ring:
    SIZE = 6

    def __init__(self, wire, first, terms, halves, near, far, p, m):
        self.wire, self.first, self.p, self.m = wire, first, p, m
        self.far, self.plus, self.minus, self.own = terms
        self.low, self.high = halves
        self.near_p, self.near_m = near
        self.far_p, self.far_m = far

    def send_far(self):
        self.wire.send(self.first, self.high(self.far), self.high(self.far_m), self.p)
        self.wire.send(self.first + 1, self.low(self.far), self.low(self.far_p), self.m)

    def send_plus(self):
        self.wire.send(self.first + 2, self.low(self.plus), self.low(self.near_m), self.p)

    def send_minus(self):
        self.wire.send(self.first + 3, self.high(self.minus), self.high(self.near_p), self.m)

    def relay_plus(self):
        self.wire.got(self.first, self.high(self.far_m), self.p)
        ref = self.high(self.plus)
        ref[...] = add(ref[...], self.high(self.far_m)[...]).astype(BF16)
        self.wire.send(self.first + 4, ref, self.high(self.near_m), self.p)

    def relay_minus(self):
        self.wire.got(self.first + 1, self.low(self.far_p), self.p)
        ref = self.low(self.minus)
        ref[...] = add(ref[...], self.low(self.far_p)[...]).astype(BF16)
        self.wire.send(self.first + 5, ref, self.low(self.near_p), self.m)

    def collect(self):
        self.wire.got(self.first + 2, self.low(self.near_m), self.p)
        self.wire.got(self.first + 3, self.high(self.near_p), self.p)
        self.wire.got(self.first + 4, self.high(self.near_m), self.p)
        self.wire.got(self.first + 5, self.low(self.near_p), self.p)
        return add(self.own[...], self.near_p[...], self.near_m[...])


SCATTER16 = 8 + 6 + 6 + 1


def scatter16(wire, part_ref, out_ref, acc, near, far, zsend, zrecv):
    x, xp, xm, x2, z, zo, c, co = blk_place()
    rows = part_ref.shape[2]
    half_rows = rows // 2
    order = [(tx, tz) for tz in (zo, z) for tx in (x2, xp, xm, x)]
    for i, (tx, tz) in enumerate(order):
        wire.send(i, part_ref.at[:, tx * 4 + tz * 2 + co], acc.at[i], {"bc": co})

    def merge(i):
        tx, tz = order[i]
        wire.got(i, acc.at[i], {"bc": co})
        acc[i] = add(part_ref[:, tx * 4 + tz * 2 + c], acc[i]).astype(BF16)

    def low(ref):
        return ref.at[:, pl.ds(0, half_rows), :]

    def high(ref):
        return ref.at[:, pl.ds(half_rows, half_rows), :]

    def ring(plane):
        return Ring(
            wire,
            8 + plane * Ring.SIZE,
            [acc.at[plane * 4 + i] for i in range(4)],
            (low, high),
            [near.at[plane, 0], near.at[plane, 1]],
            [far.at[plane, 0], far.at[plane, 1]],
            {"bx": xp},
            {"bx": xm},
        )

    outer, inner = ring(0), ring(1)
    yield
    for plane, one in enumerate((outer, inner)):
        merge(plane * 4)
        one.send_far()
        yield
        merge(plane * 4 + 1)
        one.send_plus()
        merge(plane * 4 + 2)
        one.send_minus()
        yield
    outer.relay_plus()
    yield
    outer.relay_minus()
    yield
    merge(3)
    merge(7)
    inner.relay_plus()
    yield
    inner.relay_minus()
    yield
    zsend[...] = outer.collect().astype(BF16)
    wire.send(20, zsend, zrecv, {"bz": zo})
    yield
    total = inner.collect()
    yield
    wire.got(20, zrecv, {"bz": zo})
    sums = (total + zrecv[...].astype(F32)).astype(BF16)
    out_ref[pl.ds(0, rows), :] = sums[0]
    out_ref[pl.ds(rows, rows), :] = sums[1]
    wire.finish()


SCATTER8 = 4 + 3 * Ring.SIZE + 1


def fold(value):
    total = value[:, :HEAD]
    for k in range(1, value.shape[1] // HEAD):
        total = total + value[:, k * HEAD : (k + 1) * HEAD]
    return total


def to_row(folded):
    return jnp.sum(folded.T, axis=0, keepdims=True)


def to_column(row):
    return jnp.broadcast_to(row, (HEAD, row.shape[1])).T


def wide(column, width):
    return jnp.concatenate([column] * (width // HEAD), axis=1)


def tail_kernel(
    dkv_ref, ffn_ref, kv_ref, res_ref, kv_gain, ffn_gain, wk_ref, wv_ref, wg_ref, wu_ref, wd_ref,
    input_grad, key_grad, value_grad, gate_grad, up_grad, down_grad,
    shard, ffn_own, heads, ffn, kv_in, res, wk, wv, wg, wu, wd,
    act, gate, upper, hidden_t, inv_col, kv_scaled, kv_n, y_own, y_full, hidden_grad, acts,
    row_acc, final, acc16, near16, far16, zsend16, zrecv16,
    stat_send, stat_slots, zbuf, near, far, zsend, zrecv,
    load_sem, ss, sr, fs, fr, hs, hr, ys, yr, rs, rr, ts, tr,
):
    y, yp, ym, y2, z, zo = feat_place()
    rows, cols = y_own.shape
    width = ffn.shape[1]
    pair = 2 * cols
    others = feat_others()
    loads = [
        pltpu.make_async_copy(src, dst, load_sem.at[i])
        for i, (src, dst) in enumerate(
            (
                (ffn_ref, ffn_own), (kv_ref, kv_in), (wg_ref, wg), (wu_ref, wu), (wk_ref, wk),
                (wv_ref, wv), (res_ref, res), (wd_ref, wd),
            )
        )
    ]
    for load in loads:
        load.start()
    meet(others + blk_peers())
    offset = pl.multiple_of((y * 2 + z) * cols, cols)
    stat_wire = Wire(ts, tr)

    def share(k, row):
        stat_send[k] = jnp.broadcast_to(row, (8, rows))
        for i, peer in enumerate(others):
            stat_wire.send(7 * k + i, stat_send.at[k], stat_slots.at[k, i], peer)

    def total_of(k):
        total = stat_send[k]
        for i, peer in enumerate(others):
            stat_wire.got(7 * k + i, stat_slots.at[k, i], peer)
            total = total + stat_slots[k, i]
        return total[0:1, :]

    def group(ref, i):
        return ref[:, pl.ds(pl.multiple_of(i * pair, pair), pair)]

    def forward():
        loads[1].wait()
        floats = kv_in[...].astype(F32)
        share(0, to_row(fold(floats * floats)))
        yield
        squares = jnp.zeros((rows, HEAD), F32)
        for i in range(4):
            floats = ffn[:, i * pair : (i + 1) * pair].astype(F32)
            squares = squares + fold(floats * floats)
        inverse = lax.rsqrt(jnp.sum(squares, axis=-1, keepdims=True) / width + epsilon)
        inv_col[...] = jnp.broadcast_to(inverse, (rows, HEAD))
        gate[...] = jnp.zeros_like(gate)
        upper[...] = jnp.zeros_like(upper)
        yield
        for i in range(4):
            span = slice(i * pair, (i + 1) * pair)
            scaled = ffn[:, span].astype(F32) * wide(inv_col[...], pair) * ffn_gain[:, span]
            act[:, span] = scaled.astype(BF16)
            yield
            if i == 0:
                loads[2].wait()
                loads[3].wait()
            gate[...] += jnp.dot(act[:, span], wg[span, :], preferred_element_type=F32)
            yield
            upper[...] += jnp.dot(act[:, span], wu[span, :], preferred_element_type=F32)
            yield
        value = gate[...]
        sigmoid = jax.nn.sigmoid(value)
        silu = value * sigmoid
        up_value = upper[...]
        hidden_t[...] = (silu * up_value).T.astype(BF16)
        gate[...] = up_value * sigmoid * (1.0 + value * (1.0 - sigmoid))
        upper[...] = silu

    loads[0].wait()
    kv_sums = scatter16(Wire(ss, sr), dkv_ref, shard, acc16, near16, far16, zsend16, zrecv16)
    ffn_plan = gather8(Wire(fs, fr), ffn_own, ffn, rows * 7 // 8)
    ahead = forward()
    next(kv_sums)
    next(ffn_plan)
    ffn[:, pl.ds(offset, cols)] = ffn_own[...]
    next(ahead)
    run_first(kv_sums, ffn_plan)
    plan = gather8(Wire(hs, hr), shard, heads, rows * 9 // 8)
    next(plan)
    heads[:, pl.ds(pl.multiple_of((y * 2 + z) * HEAD, HEAD), HEAD)] = shard[...]
    run_all(plan, chain(ffn_plan, ahead))

    for load in loads[4:]:
        load.wait()
    normed = contract_cols(heads[:rows, :], wk[...]) + contract_cols(heads[rows:, :], wv[...])
    gain = kv_gain[:, pl.ds(offset, cols)]
    scaled = gain * normed.astype(BF16).astype(F32)
    kv_scaled[...] = scaled
    kv_floats = kv_in[...].astype(F32)
    share(1, to_row(fold(scaled * kv_floats)))
    kv_inv = wide(to_column(lax.rsqrt(total_of(0) / width + epsilon)), cols)
    kv_hat = kv_in[...].astype(F32) * kv_inv
    kv_n[...] = (kv_hat * kv_gain[:, pl.ds(offset, cols)]).astype(BF16)
    key_grad[0] = contract_rows(kv_n[...], heads[:rows, :]).astype(BF16)
    mean = wide(to_column(total_of(1) / width), cols) * kv_inv
    y_own[...] = (res[...].astype(F32) + kv_inv * (kv_scaled[...] - kv_hat * mean)).astype(BF16)

    plan = gather8(Wire(ys, yr), y_own, y_full, rows * 9 // 16)
    next(plan)
    y_full[:, pl.ds(offset, cols)] = y_own[...]
    hidden_grad[...] = jnp.zeros_like(hidden_grad)

    def other_kv():
        value_grad[0] = contract_rows(kv_n[...], heads[rows:, :]).astype(BF16)
        yield

    def down(i):
        down_grad[0, :, pl.ds(pl.multiple_of(i * pair, pair), pair)] = jnp.dot(
            hidden_t[...], group(y_full, i), preferred_element_type=F32
        ).astype(BF16)

    def back(i):
        hidden_grad[...] += contract_cols(group(y_full, i), group(wd, i))

    filler = other_kv()
    for stage in plan:
        if stage is None:
            run_some(filler)
            continue
        i, is_last = stage
        back(i)
        if not is_last:
            down(i)

    value = hidden_grad[...]
    hidden = gate.shape[1]
    acts[:, :hidden] = (value * gate[...]).astype(BF16)
    acts[:, hidden:] = (value * upper[...]).astype(BF16)
    cut = near.shape[2]
    rest = rows - cut
    wire = Wire(rs, rr)

    def term(i, tz, first, size):
        return wd.at[pl.ds(first, size), pl.ds(pl.multiple_of(i * pair + tz * cols, cols), cols)]

    def ring(plane, tz, first, size):
        return Ring(
            wire,
            4 + plane * Ring.SIZE,
            [term(i, tz, first, size) for i in range(4)],
            (
                lambda ref: ref.at[pl.ds(0, size // 2), :],
                lambda ref: ref.at[pl.ds(size // 2, size // 2), :],
            ),
            [near.at[plane, k, pl.ds(0, size), :] for k in range(2)],
            [far.at[plane, k, pl.ds(0, size), :] for k in range(2)],
            {"kvh": yp},
            {"kvh": ym},
        )

    outer, inner, last = ring(0, zo, 0, cut), ring(1, z, 0, cut), ring(2, z, cut, rest)
    row_acc[...] = jnp.zeros_like(row_acc)
    for i, ty in enumerate((y2, yp, ym, y)):
        span = pl.ds(pl.multiple_of(ty * pair, pair), pair)
        value = contract_cols(acts[:, :hidden], wg[span, :]) + contract_cols(acts[:, hidden:], wu[span, :])
        wd[:, i * pair : (i + 1) * pair] = value.astype(BF16)
        wire.send(i, term(i, zo, cut, rest), zbuf.at[i], {"section": zo})
        for one in (outer, inner):
            (one.send_far, one.send_plus, one.send_minus, lambda: None)[i]()
        row_acc[...] += fold(value * ffn[:, span].astype(F32) * ffn_gain[:, span])
    share(2, to_row(row_acc[...] * inv_col[...]))

    def weights():
        for i in range(4):
            span = slice(i * pair, (i + 1) * pair)
            value = contract_rows(act[:, span], acts[:, :hidden])
            gate_grad[0, span, :] = value.astype(BF16)
            yield
            value = contract_rows(act[:, span], acts[:, hidden:])
            up_grad[0, span, :] = value.astype(BF16)
            yield
        down(y2)

    def blend(i):
        wire.got(i, zbuf.at[i], {"section": zo})
        ref = term(i, z, cut, rest)
        ref[...] = add(ref[...], zbuf[i]).astype(BF16)

    def sums():
        outer.relay_plus()
        outer.relay_minus()
        yield
        blend(0)
        last.send_far()
        inner.relay_plus()
        inner.relay_minus()
        yield
        blend(1)
        last.send_plus()
        blend(2)
        last.send_minus()
        yield
        zsend[...] = outer.collect().astype(BF16)
        wire.send(SCATTER8 - 1, zsend, zrecv, {"section": zo})
        yield
        last.relay_plus()
        last.relay_minus()
        yield
        blend(3)
        final[pl.ds(0, cut), :] = inner.collect()
        yield
        final[pl.ds(cut, rest), :] = last.collect()
        yield
        wire.got(SCATTER8 - 1, zrecv, {"section": zo})
        final[pl.ds(0, cut), :] += zrecv[...].astype(F32)

    run_all(weights(), sums())
    inverse = wide(inv_col[...], cols)
    correction = wide(to_column(total_of(2) / width), cols)
    hat = ffn[:, pl.ds(offset, cols)].astype(F32) * inverse
    input_grad[...] = (
        y_own[...].astype(F32)
        + inverse * (ffn_gain[:, pl.ds(offset, cols)] * final[...] - hat * correction)
    ).astype(BF16)
    wire.finish()
    stat_wire.finish()


def tail(dkv, ffn_input, kv_input, residual, kv_gain, ffn_gain, w_key, w_value, w_gate, w_up, w_down):
    rows, cols = kv_input.shape
    width, hidden = w_gate.shape
    cut = rows * 9 // 16
    rest = rows - cut
    any_space = pl.BlockSpec(memory_space=pl.ANY)
    in_vmem = pl.BlockSpec(memory_space=VMEM)
    dma = pltpu.SemaphoreType.DMA
    heads = w_key.shape[1]
    return pl.pallas_call(
        tail_kernel,
        name="tail",
        out_shape=(
            VMEM((rows, cols), BF16),
            VMEM((1, cols, heads), BF16),
            VMEM((1, cols, heads), BF16),
            VMEM((1, width, hidden), BF16),
            VMEM((1, width, hidden), BF16),
            VMEM((1, hidden, width), BF16),
        ),
        in_specs=[in_vmem] + [any_space] * 3 + [in_vmem] * 2 + [any_space] * 5,
        out_specs=(in_vmem,) * 6,
        scratch_shapes=[
            VMEM((2 * rows, HEAD), BF16),
            VMEM((rows, cols), BF16),
            VMEM((2 * rows, heads), BF16),
            VMEM((rows, width), BF16),
            VMEM((rows, cols), BF16),
            VMEM((rows, cols), BF16),
            VMEM((cols, heads), BF16),
            VMEM((cols, heads), BF16),
            VMEM((width, hidden), BF16),
            VMEM((width, hidden), BF16),
            VMEM((hidden, width), BF16),
            VMEM((rows, width), BF16),
            VMEM((rows, hidden), F32),
            VMEM((rows, hidden), F32),
            VMEM((hidden, rows), BF16),
            VMEM((rows, HEAD), F32),
            VMEM((rows, cols), F32),
            VMEM((rows, cols), BF16),
            VMEM((rows, cols), BF16),
            VMEM((rows, width), BF16),
            VMEM((rows, hidden), F32),
            VMEM((rows, 2 * hidden), BF16),
            VMEM((rows, HEAD), F32),
            VMEM((rows, cols), F32),
            VMEM((8, 2, rows, HEAD), BF16),
            VMEM((2, 2, 2, rows, HEAD), BF16),
            VMEM((2, 2, 2, rows, HEAD), BF16),
            VMEM((2, rows, HEAD), BF16),
            VMEM((2, rows, HEAD), BF16),
            VMEM((3, 8, rows), F32),
            VMEM((3, 7, 8, rows), F32),
            VMEM((4, rest, cols), BF16),
            VMEM((3, 2, cut, cols), BF16),
            VMEM((3, 2, cut, cols), BF16),
            VMEM((cut, cols), BF16),
            VMEM((cut, cols), BF16),
            dma((8,)), dma((SCATTER16,)), dma((SCATTER16,)), dma((GATHER8,)), dma((GATHER8,)),
            dma((GATHER8,)), dma((GATHER8,)), dma((GATHER8,)), dma((GATHER8,)),
            dma((SCATTER8,)), dma((SCATTER8,)), dma((21,)), dma((21,)),
        ],
        compiler_params=pltpu.CompilerParams(
            collective_id=3, has_side_effects=True, vmem_limit_bytes=44_000_000
        ),
    )(
        pltpu.with_memory_space_constraint(dkv, VMEM),
        ffn_input, kv_input, residual, kv_gain.reshape(1, -1), ffn_gain.reshape(1, -1),
        w_key, w_value, w_gate, w_up, w_down,
    )


MASKED = -1e30
START = -1e29


def attention_kernel(
    bound_ref, seen_ref, q_ref, g_ref, kv_ref, dq_ref, dkv_ref,
    q_cat, g_cat, q_t, g_t, run_max, run_sum, run_dot, dq_t, *, tile, scale
):
    rows = q_ref.shape[0]
    group = q_ref.shape[1] // HEAD
    own = lax.axis_index(BLK)
    lowest, highest = bound_ref[0], bound_ref[rows - 1]
    to_log2 = scale * LOG2E
    for h in range(group):
        for src, cat, turned in ((q_ref, q_cat, q_t), (g_ref, g_cat, g_t)):
            block = src[:, h * HEAD : (h + 1) * HEAD]
            cat[h * rows : (h + 1) * rows, :] = block
            turned[:, h * rows : (h + 1) * rows] = block.astype(F32).T.astype(BF16)
    run_max[...] = jnp.full_like(run_max, START)
    run_sum[...] = jnp.zeros_like(run_sum)
    run_dot[...] = jnp.zeros_like(run_dot)
    dq_t[...] = jnp.zeros_like(dq_t)

    tiles = dkv_ref.shape[1] // tile
    first = lowest // tile
    last = ((own + 1) * rows) // tile
    whole_from = jnp.minimum((highest + tile - 1) // tile, (own * rows) // tile)
    whole_to = (own * rows) // tile

    def part(j):
        return pl.ds(pl.multiple_of(j * tile, tile), tile)

    def lanes(h):
        return pl.ds(h * rows, rows)

    def scores(j, h, masked):
        keys = kv_ref[0, part(j), :]
        value = jnp.dot(keys, q_t[:, lanes(h)], preferred_element_type=F32) * to_log2
        if masked:
            key_pos = j * tile + lax.broadcasted_iota(jnp.int32, (tile, rows), 0)
            query_pos = own * rows + lax.broadcasted_iota(jnp.int32, (tile, rows), 1)
            visible = (key_pos <= query_pos) & (key_pos >= seen_ref[...])
            value = jnp.where(visible, value, MASKED)
        return value

    def products(j, h):
        return jnp.dot(kv_ref[1, part(j), :], g_t[:, lanes(h)], preferred_element_type=F32)

    def stats(j, masked):
        for h in range(group):
            value = scores(j, h, masked).reshape(tile // 8, 8, rows)
            dprobs = products(j, h).reshape(tile // 8, 8, rows)
            before = run_max[:, lanes(h)]
            now = jnp.maximum(before, jnp.max(value, axis=0))
            shrink = jnp.exp2(before - now)
            probs = jnp.exp2(value - now[None])
            run_max[:, lanes(h)] = now
            run_sum[:, lanes(h)] = run_sum[:, lanes(h)] * shrink + jnp.sum(probs, axis=0)
            run_dot[:, lanes(h)] = run_dot[:, lanes(h)] * shrink + jnp.sum(probs * dprobs, axis=0)

    def grads(j, masked):
        keys = kv_ref[0, part(j), :]
        value_part = jnp.zeros((tile, HEAD), F32)
        key_part = jnp.zeros((tile, HEAD), F32)
        for h in range(group):
            value = scores(j, h, masked)
            probs = jnp.exp2(value - run_max[0:1, lanes(h)])
            dscores = (probs * (products(j, h) - run_dot[0:1, lanes(h)])).astype(BF16)
            value_part = value_part + jnp.dot(
                probs.astype(BF16), g_cat[lanes(h), :], preferred_element_type=F32
            )
            key_part = key_part + jnp.dot(dscores, q_cat[lanes(h), :], preferred_element_type=F32)
            dq_t[:, lanes(h)] += contract_rows(keys, dscores)
        dkv_ref[0, part(j), :] = (key_part * scale).astype(BF16)
        dkv_ref[1, part(j), :] = value_part.astype(BF16)

    def sweep(body):
        lax.fori_loop(first, whole_from, lambda j, _: (body(j, True), 0)[1], 0)
        lax.fori_loop(jnp.maximum(whole_from, first), whole_to, lambda j, _: (body(j, False), 0)[1], 0)
        lax.fori_loop(jnp.maximum(whole_to, first), last, lambda j, _: (body(j, True), 0)[1], 0)

    sweep(stats)
    peak = jnp.max(run_max[...], axis=0, keepdims=True)
    factor = jnp.exp2(run_max[...] - peak)
    total = jnp.sum(run_sum[...] * factor, axis=0, keepdims=True)
    delta = jnp.sum(run_dot[...] * factor, axis=0, keepdims=True) / total
    run_max[0:1, :] = peak + jnp.log(total) * LOG2E
    run_dot[0:1, :] = delta

    def clear(j, _):
        dkv_ref[:, part(j), :] = jnp.zeros((2, tile, HEAD), BF16)
        return 0

    lax.fori_loop(0, first, clear, 0)
    lax.fori_loop(last, tiles, clear, 0)
    sweep(grads)
    for h in range(group):
        dq_ref[:, h * HEAD : (h + 1) * HEAD] = (dq_t[:, lanes(h)] * scale).T.astype(BF16)


def attention(query, out_grad, kv, visible_from, tile=256):
    rows, width = query.shape
    group = width // HEAD
    cat = VMEM((group * rows, HEAD), BF16)
    turned = VMEM((HEAD, group * rows), BF16)
    stat = VMEM((8, group * rows), F32)
    return pl.pallas_call(
        functools.partial(attention_kernel, tile=tile, scale=1.0 / math.sqrt(HEAD)),
        name="attention",
        out_shape=(
            jax.ShapeDtypeStruct((rows, width), BF16),
            VMEM(kv.shape, BF16),
        ),
        in_specs=[pl.BlockSpec(memory_space=pltpu.SMEM)] + [pl.BlockSpec(memory_space=VMEM)] * 4,
        out_specs=(pl.BlockSpec(memory_space=VMEM),) * 2,
        scratch_shapes=[
            cat, cat, turned, turned, stat, stat, stat, VMEM((HEAD, group * rows), F32),
        ],
        compiler_params=pltpu.CompilerParams(vmem_limit_bytes=32_000_000),
    )(visible_from, visible_from.reshape(1, rows), query, out_grad, kv)


def on_device(
    query, keys, values, out_grad, visible_from, kv_input, residual_grad, ffn_input,
    kv_gain, ffn_gain, w_key, w_value, w_gate, w_up, w_down,
):
    rows = query.shape[0]
    every = gather_first(keys, values)
    blocks = every.shape[1]
    query_grad, dkv = attention(query, out_grad, every.reshape(2, blocks * rows, HEAD), visible_from)
    rest = tail(
        dkv.reshape(2, blocks, rows, HEAD), ffn_input, kv_input, residual_grad, kv_gain, ffn_gain,
        w_key, w_value, w_gate, w_up, w_down,
    )
    return (query_grad, *rest)


def solution(mesh):
    finer = Mesh(
        mesh.devices.reshape(4, 2, 2, mesh.shape["kvh"], mesh.shape["section"]),
        (*BLK, *FEAT),
    )
    tokens = P(BLK, FEAT)
    placed = (
        tokens, tokens, tokens, tokens, P(BLK), tokens, tokens, tokens, P(), P(),
        P(FEAT, None), P(FEAT, None), P(None, FEAT), P(None, FEAT), P(FEAT, None),
    )
    return jax.shard_map(
        on_device,
        mesh=finer,
        in_specs=placed,
        out_specs=(
            tokens,
            tokens,
            P(BLK, FEAT, None),
            P(BLK, FEAT, None),
            P(BLK, None, FEAT),
            P(BLK, None, FEAT),
            P(BLK, FEAT, None),
        ),
        check_vma=False,
    )
```

```python
import functools
import math

import jax
import jax.numpy as jnp
from jax import lax
from jax.experimental import pallas as pl
from jax.experimental.pallas import tpu as pltpu
from jax.sharding import Mesh
from jax.sharding import PartitionSpec as P

HEAD = 128
BLK = ("bx", "bz", "bc")
FEAT = ("kvh", "section")
MESH = pl.DeviceIdType.MESH
LOG2E = 1.4426950408889634
VMEM = pltpu.VMEM
F32 = jnp.float32
BF16 = jnp.bfloat16

epsilon = 1e-06


def contract_rows(left, right):
    return lax.dot_general(left, right, (((0,), (0,)), ((), ())), preferred_element_type=F32)


def contract_cols(left, right):
    return lax.dot_general(left, right, (((1,), (1,)), ((), ())), preferred_element_type=F32)


def run_all(*plans):
    live = list(plans)
    while live:
        for plan in list(live):
            try:
                next(plan)
            except StopIteration:
                live.remove(plan)


def run_some(plan):
    try:
        next(plan)
    except StopIteration:
        pass


def run_first(main, *others):
    for _ in main:
        for other in others:
            run_some(other)


def chain(*plans):
    for plan in plans:
        yield from plan


def meet(peers):
    barrier = pltpu.get_barrier_semaphore()
    for peer in peers:
        pl.semaphore_signal(barrier, inc=1, device_id=peer, device_id_type=MESH)
    pl.semaphore_wait(barrier, len(peers))


class Wire:
    def __init__(self, send_sem, recv_sem):
        self.send_sem, self.recv_sem, self.sent = send_sem, recv_sem, []

    def send(self, i, src, dst, peer):
        copy = pltpu.make_async_remote_copy(
            src_ref=src,
            dst_ref=dst,
            send_sem=self.send_sem.at[i],
            recv_sem=self.recv_sem.at[i],
            device_id=peer,
            device_id_type=MESH,
        )
        copy.start()
        self.sent.append(copy)

    def got(self, i, dst, peer):
        pltpu.make_async_remote_copy(
            src_ref=dst,
            dst_ref=dst,
            send_sem=self.send_sem.at[i],
            recv_sem=self.recv_sem.at[i],
            device_id=peer,
            device_id_type=MESH,
        ).wait_recv()

    def finish(self):
        for copy in self.sent:
            copy.wait_send()


def feat_place():
    y, z = lax.axis_index("kvh"), lax.axis_index("section")
    return y, lax.rem(y + 1, 4), lax.rem(y + 3, 4), lax.rem(y + 2, 4), z, 1 - z


def feat_peers():
    y, yp, ym, y2, z, zo = feat_place()
    return [{"kvh": yp}, {"kvh": ym}, {"section": zo}]


def feat_others():
    y, yp, ym, y2, z, zo = feat_place()
    others = [{"section": zo}]
    for other in (yp, ym, y2):
        others.append({"kvh": other})
        others.append({"kvh": other, "section": zo})
    return others


def blk_place():
    x, z, c = lax.axis_index("bx"), lax.axis_index("bz"), lax.axis_index("bc")
    return x, lax.rem(x + 1, 4), lax.rem(x + 3, 4), lax.rem(x + 2, 4), z, 1 - z, c, 1 - c


def blk_peers():
    x, xp, xm, x2, z, zo, c, co = blk_place()
    return [{"bx": xp}, {"bx": xm}, {"bz": zo}, {"bc": co}]


GATHER8 = 18


def gather8(wire, x_ref, out_ref, cut):
    y, yp, ym, y2, z, zo = feat_place()
    rows, cols = x_ref.shape
    p_y, m_y, o_z = {"kvh": yp}, {"kvh": ym}, {"section": zo}
    full_a, low_a, high_a = (0, cut), (0, cut // 2), (cut // 2, cut // 2)
    rest = rows - cut
    full_b, low_b, high_b = (cut, rest), (cut, rest // 2), (cut + rest // 2, rest // 2)

    def at(sy, sz, part):
        start = pl.multiple_of((sy * 2 + sz) * cols, cols)
        return out_ref.at[pl.ds(part[0], part[1]), pl.ds(start, cols)]

    def own(i, part, peer):
        wire.send(i, x_ref.at[pl.ds(part[0], part[1]), :], at(y, z, part), peer)

    def on(i, sy, sz, part, peer):
        wire.send(i, at(sy, sz, part), at(sy, sz, part), peer)

    def got(i, sy, sz, part):
        wire.got(i, at(sy, sz, part), o_z)

    own(0, full_a, o_z)
    own(1, full_a, p_y)
    own(2, full_a, m_y)
    own(3, full_b, p_y)
    own(4, full_b, m_y)
    own(5, full_b, o_z)
    yield
    got(0, y, zo, full_a)
    on(6, y, zo, full_a, p_y)
    on(7, y, zo, full_a, m_y)
    yield
    got(1, ym, z, full_a)
    on(8, ym, z, low_a, p_y)
    yield
    got(2, yp, z, full_a)
    on(9, yp, z, high_a, m_y)
    yield
    got(3, ym, z, full_b)
    on(10, ym, z, low_b, p_y)
    on(12, ym, z, full_b, o_z)
    yield
    got(4, yp, z, full_b)
    on(11, yp, z, high_b, m_y)
    on(13, yp, z, full_b, o_z)
    yield
    got(5, y, zo, full_b)
    yield y, False
    got(6, ym, zo, full_a)
    on(14, ym, zo, low_a, p_y)
    yield
    got(7, yp, zo, full_a)
    on(15, yp, zo, high_a, m_y)
    yield
    got(12, ym, zo, full_b)
    yield ym, False
    got(10, y2, z, low_b)
    on(16, y2, z, low_b, o_z)
    yield
    got(11, y2, z, high_b)
    on(17, y2, z, high_b, o_z)
    yield
    got(13, yp, zo, full_b)
    yield yp, False
    got(8, y2, z, low_a)
    got(9, y2, z, high_a)
    got(14, y2, zo, low_a)
    got(15, y2, zo, high_a)
    got(16, y2, zo, low_b)
    got(17, y2, zo, high_b)
    wire.finish()
    yield y2, True


GATHER16 = 25


def gather16(wire, kv_ref, out_ref):
    x, xp, xm, x2, z, zo, c, co = blk_place()
    rows = kv_ref.shape[1]
    p_x, m_x, o_z, o_c = {"bx": xp}, {"bx": xm}, {"bz": zo}, {"bc": co}
    full, low, high = (0, rows), (0, rows // 2), (rows // 2, rows // 2)

    def at(sx, sz, sc, part):
        return out_ref.at[:, sx * 4 + sz * 2 + sc, pl.ds(part[0], part[1]), :]

    def own(i, part, peer):
        wire.send(i, kv_ref.at[:, pl.ds(part[0], part[1]), :], at(x, z, c, part), peer)

    def on(i, sx, sz, part, peer):
        wire.send(i, at(sx, sz, c, part), at(sx, sz, c, part), peer)

    def got(i, sx, sz, part, sc=None):
        wire.got(i, at(sx, sz, c if sc is None else sc, part), o_z)

    own(0, low, o_z)
    own(1, full, p_x)
    own(2, full, m_x)
    own(19, high, o_z)
    own(3, full, o_c)
    yield
    got(0, x, zo, low)
    on(4, x, zo, low, p_x)
    on(5, x, zo, low, m_x)
    on(6, x, zo, low, o_c)
    yield
    got(1, xm, z, full)
    on(7, xm, z, low, p_x)
    on(8, xm, z, full, o_c)
    yield
    got(2, xp, z, full)
    on(9, xp, z, high, m_x)
    on(10, xp, z, full, o_c)
    yield
    got(19, x, zo, high)
    on(20, x, zo, high, p_x)
    on(21, x, zo, high, m_x)
    on(22, x, zo, high, o_c)
    yield
    got(4, xm, zo, low)
    on(11, xm, zo, low, p_x)
    on(12, xm, zo, low, o_c)
    yield
    got(5, xp, zo, low)
    on(14, xp, zo, low, o_c)
    yield
    got(7, x2, z, low)
    on(15, x2, z, low, o_c)
    yield
    got(9, x2, z, high)
    on(16, x2, z, high, o_c)
    yield
    got(21, xp, zo, high)
    on(13, xp, zo, high, m_x)
    on(24, xp, zo, high, o_c)
    yield
    got(20, xm, zo, high)
    on(23, xm, zo, high, o_c)
    yield
    got(11, x2, zo, low)
    on(17, x2, zo, low, o_c)
    yield
    got(13, x2, zo, high)
    on(18, x2, zo, high, o_c)
    yield
    got(3, x, z, full, co)
    got(6, x, zo, low, co)
    got(22, x, zo, high, co)
    got(8, xm, z, full, co)
    got(10, xp, z, full, co)
    got(12, xm, zo, low, co)
    got(23, xm, zo, high, co)
    got(14, xp, zo, low, co)
    got(24, xp, zo, high, co)
    got(15, x2, z, low, co)
    got(16, x2, z, high, co)
    got(17, x2, zo, low, co)
    got(18, x2, zo, high, co)
    wire.finish()


def first_kernel(key_ref, value_ref, kv_out, own, s0, r0, local):
    x, xp, xm, x2, z, zo, c, co = blk_place()
    loads = [
        pltpu.make_async_copy(key_ref, own.at[0], local.at[0]),
        pltpu.make_async_copy(value_ref, own.at[1], local.at[1]),
    ]
    for load in loads:
        load.start()
    meet(blk_peers())
    for load in loads:
        load.wait()
    keep = pltpu.make_async_copy(own, kv_out.at[:, x * 4 + z * 2 + c], local.at[2])
    plan = gather16(Wire(s0, r0), own, kv_out)
    next(plan)
    keep.start()
    run_all(plan)
    keep.wait()


def gather_first(keys, values):
    rows, width = keys.shape
    return pl.pallas_call(
        first_kernel,
        name="gather_first",
        out_shape=VMEM((2, 16, rows, width), keys.dtype),
        in_specs=[pl.BlockSpec(memory_space=pltpu.HBM)] * 2,
        out_specs=pl.BlockSpec(memory_space=VMEM),
        scratch_shapes=[
            VMEM((2, rows, width), keys.dtype),
            pltpu.SemaphoreType.DMA((GATHER16,)),
            pltpu.SemaphoreType.DMA((GATHER16,)),
            pltpu.SemaphoreType.DMA((3,)),
        ],
        compiler_params=pltpu.CompilerParams(
            collective_id=1, has_side_effects=True, vmem_limit_bytes=16_000_000
        ),
    )(
        pltpu.with_memory_space_constraint(keys, pltpu.HBM),
        pltpu.with_memory_space_constraint(values, pltpu.HBM),
    )


def add(*terms):
    total = terms[0].astype(F32)
    for term in terms[1:]:
        total = total + term.astype(F32)
    return total


class Ring:
    SIZE = 6

    def __init__(self, wire, first, terms, halves, near, far, p, m):
        self.wire, self.first, self.p, self.m = wire, first, p, m
        self.far, self.plus, self.minus, self.own = terms
        self.low, self.high = halves
        self.near_p, self.near_m = near
        self.far_p, self.far_m = far

    def send_far(self):
        self.wire.send(self.first, self.high(self.far), self.high(self.far_m), self.p)
        self.wire.send(self.first + 1, self.low(self.far), self.low(self.far_p), self.m)

    def send_plus(self):
        self.wire.send(self.first + 2, self.low(self.plus), self.low(self.near_m), self.p)

    def send_minus(self):
        self.wire.send(self.first + 3, self.high(self.minus), self.high(self.near_p), self.m)

    def relay_plus(self):
        self.wire.got(self.first, self.high(self.far_m), self.p)
        ref = self.high(self.plus)
        ref[...] = add(ref[...], self.high(self.far_m)[...]).astype(BF16)
        self.wire.send(self.first + 4, ref, self.high(self.near_m), self.p)

    def relay_minus(self):
        self.wire.got(self.first + 1, self.low(self.far_p), self.p)
        ref = self.low(self.minus)
        ref[...] = add(ref[...], self.low(self.far_p)[...]).astype(BF16)
        self.wire.send(self.first + 5, ref, self.low(self.near_p), self.m)

    def collect(self):
        self.wire.got(self.first + 2, self.low(self.near_m), self.p)
        self.wire.got(self.first + 3, self.high(self.near_p), self.p)
        self.wire.got(self.first + 4, self.high(self.near_m), self.p)
        self.wire.got(self.first + 5, self.low(self.near_p), self.p)
        return add(self.own[...], self.near_p[...], self.near_m[...])


SCATTER16 = 16 + 4 * Ring.SIZE + 2


def scatter16(wire, part_ref, out_ref, acc, near, far, zsend, zrecv):
    x, xp, xm, x2, z, zo, c, co = blk_place()
    rows = part_ref.shape[2]
    half_rows = rows // 2
    spots = [(tz, kind) for tz in (zo, z) for kind in range(2)]
    turn = (x2, xp, xm, x)
    for r, (tz, kind) in enumerate(spots):
        for i, tx in enumerate(turn):
            wire.send(4 * r + i, part_ref.at[kind, tx * 4 + tz * 2 + co], acc.at[r, i], {"bc": co})

    def merge(r, i):
        tz, kind = spots[r]
        wire.got(4 * r + i, acc.at[r, i], {"bc": co})
        acc[r, i] = add(part_ref[kind, turn[i] * 4 + tz * 2 + c], acc[r, i]).astype(BF16)

    def low(ref):
        return ref.at[pl.ds(0, half_rows), :]

    def high(ref):
        return ref.at[pl.ds(half_rows, half_rows), :]

    rings = [
        Ring(
            wire,
            16 + r * Ring.SIZE,
            [acc.at[r, i] for i in range(4)],
            (low, high),
            [near.at[r, 0], near.at[r, 1]],
            [far.at[r, 0], far.at[r, 1]],
            {"bx": xp},
            {"bx": xm},
        )
        for r in range(4)
    ]

    def launch(r):
        merge(r, 0)
        rings[r].send_far()
        merge(r, 1)
        rings[r].send_plus()
        merge(r, 2)
        rings[r].send_minus()

    def relay(r):
        rings[r].relay_plus()
        rings[r].relay_minus()

    def across(r):
        merge(r, 3)
        zsend[r] = rings[r].collect().astype(BF16)
        wire.send(16 + 4 * Ring.SIZE + r, zsend.at[r], zrecv.at[r], {"bz": zo})

    def settle(r):
        total = rings[r].collect()
        wire.got(16 + 4 * Ring.SIZE + r - 2, zrecv.at[r - 2], {"bz": zo})
        total = total + zrecv[r - 2].astype(F32)
        out_ref[pl.ds((r - 2) * rows, rows), :] = total.astype(BF16)

    yield
    launch(0)
    yield
    launch(1)
    yield
    relay(0)
    yield
    launch(2)
    yield
    relay(1)
    yield
    across(0)
    yield
    launch(3)
    yield
    relay(2)
    yield
    across(1)
    yield
    relay(3)
    yield
    merge(2, 3)
    settle(2)
    yield
    merge(3, 3)
    settle(3)
    wire.finish()


SCATTER8 = 4 + 3 * Ring.SIZE + 1


def fold(value):
    total = value[:, :HEAD]
    for k in range(1, value.shape[1] // HEAD):
        total = total + value[:, k * HEAD : (k + 1) * HEAD]
    return total


def to_row(folded):
    return jnp.sum(folded.T, axis=0, keepdims=True)


def to_column(row):
    return jnp.broadcast_to(row, (HEAD, row.shape[1])).T


def wide(column, width):
    return jnp.concatenate([column] * (width // HEAD), axis=1)


def tail_kernel(
    dkv_ref, ffn_ref, kv_ref, res_ref, kv_gain, ffn_gain, wk_ref, wv_ref, wg_ref, wu_ref, wd_ref,
    input_grad, key_grad, value_grad, gate_grad, up_grad, down_grad,
    shard, ffn_own, heads, ffn, kv_in, res, wk, wv, wg, wu, wd,
    act, gate, upper, hidden_t, inv_col, kv_scaled, kv_n, y_own, y_full, hidden_grad, acts,
    row_acc, final, acc16, near16, far16, zsend16, zrecv16,
    stat_send, stat_slots, zbuf, near, far, zsend, zrecv,
    load_sem, ss, sr, fs, fr, hs, hr, ys, yr, rs, rr, ts, tr,
):
    y, yp, ym, y2, z, zo = feat_place()
    rows, cols = y_own.shape
    width = ffn.shape[1]
    pair = 2 * cols
    others = feat_others()
    loads = [
        pltpu.make_async_copy(src, dst, load_sem.at[i])
        for i, (src, dst) in enumerate(
            (
                (ffn_ref, ffn_own), (kv_ref, kv_in), (wg_ref, wg), (wu_ref, wu), (wk_ref, wk),
                (wv_ref, wv), (res_ref, res), (wd_ref, wd),
            )
        )
    ]
    for load in loads:
        load.start()
    meet(others + blk_peers())
    offset = pl.multiple_of((y * 2 + z) * cols, cols)
    stat_wire = Wire(ts, tr)

    def share(k, row):
        stat_send[k] = jnp.broadcast_to(row, (8, rows))
        for i, peer in enumerate(others):
            stat_wire.send(7 * k + i, stat_send.at[k], stat_slots.at[k, i], peer)

    def total_of(k):
        total = stat_send[k]
        for i, peer in enumerate(others):
            stat_wire.got(7 * k + i, stat_slots.at[k, i], peer)
            total = total + stat_slots[k, i]
        return total[0:1, :]

    def group(ref, i):
        return ref[:, pl.ds(pl.multiple_of(i * pair, pair), pair)]

    def forward():
        loads[1].wait()
        floats = kv_in[...].astype(F32)
        share(0, to_row(fold(floats * floats)))
        yield
        squares = jnp.zeros((rows, HEAD), F32)
        for i in range(4):
            floats = ffn[:, i * pair : (i + 1) * pair].astype(F32)
            squares = squares + fold(floats * floats)
        inverse = lax.rsqrt(jnp.sum(squares, axis=-1, keepdims=True) / width + epsilon)
        inv_col[...] = jnp.broadcast_to(inverse, (rows, HEAD))
        gate[...] = jnp.zeros_like(gate)
        upper[...] = jnp.zeros_like(upper)
        yield
        for i in range(4):
            span = slice(i * pair, (i + 1) * pair)
            scaled = ffn[:, span].astype(F32) * wide(inv_col[...], pair) * ffn_gain[:, span]
            act[:, span] = scaled.astype(BF16)
            yield
            if i == 0:
                loads[2].wait()
                loads[3].wait()
            gate[...] += jnp.dot(act[:, span], wg[span, :], preferred_element_type=F32)
            yield
            upper[...] += jnp.dot(act[:, span], wu[span, :], preferred_element_type=F32)
            yield

    loads[0].wait()
    kv_sums = scatter16(Wire(ss, sr), dkv_ref, shard, acc16, near16, far16, zsend16, zrecv16)
    ffn_plan = gather8(Wire(fs, fr), ffn_own, ffn, rows * 7 // 8)
    ahead = forward()
    next(kv_sums)
    next(ffn_plan)
    ffn[:, pl.ds(offset, cols)] = ffn_own[...]
    next(ahead)
    run_first(kv_sums, ffn_plan)
    plan = gather8(Wire(hs, hr), shard, heads, rows * 9 // 8)
    next(plan)
    heads[:, pl.ds(pl.multiple_of((y * 2 + z) * HEAD, HEAD), HEAD)] = shard[...]
    run_all(plan, chain(ffn_plan, ahead))

    for load in loads[4:]:
        load.wait()
    normed = contract_cols(heads[:rows, :], wk[...]) + contract_cols(heads[rows:, :], wv[...])
    gain = kv_gain[:, pl.ds(offset, cols)]
    scaled = gain * normed.astype(BF16).astype(F32)
    kv_scaled[...] = scaled
    kv_floats = kv_in[...].astype(F32)
    share(1, to_row(fold(scaled * kv_floats)))
    kv_inv = wide(to_column(lax.rsqrt(total_of(0) / width + epsilon)), cols)
    kv_hat = kv_in[...].astype(F32) * kv_inv
    kv_n[...] = (kv_hat * kv_gain[:, pl.ds(offset, cols)]).astype(BF16)
    key_grad[0] = contract_rows(kv_n[...], heads[:rows, :]).astype(BF16)
    mean = wide(to_column(total_of(1) / width), cols) * kv_inv
    y_own[...] = (res[...].astype(F32) + kv_inv * (kv_scaled[...] - kv_hat * mean)).astype(BF16)

    plan = gather8(Wire(ys, yr), y_own, y_full, rows * 9 // 16)
    next(plan)
    y_full[:, pl.ds(offset, cols)] = y_own[...]
    hidden_grad[...] = jnp.zeros_like(hidden_grad)

    def other_kv():
        value_grad[0] = contract_rows(kv_n[...], heads[rows:, :]).astype(BF16)
        yield
        hidden_t[...] = (gate[...] * jax.nn.sigmoid(gate[...]) * upper[...]).T.astype(BF16)
        yield
        value = gate[...]
        sigmoid = jax.nn.sigmoid(value)
        gate[...] = upper[...] * sigmoid * (1.0 + value * (1.0 - sigmoid))
        upper[...] = value * sigmoid

    def down(i):
        down_grad[0, :, pl.ds(pl.multiple_of(i * pair, pair), pair)] = jnp.dot(
            hidden_t[...], group(y_full, i), preferred_element_type=F32
        ).astype(BF16)

    def back(i):
        hidden_grad[...] += contract_cols(group(y_full, i), group(wd, i))

    filler = other_kv()
    for stage in plan:
        if stage is None:
            run_some(filler)
            continue
        i, is_last = stage
        back(i)
        if not is_last:
            down(i)

    value = hidden_grad[...]
    hidden = gate.shape[1]
    acts[:, :hidden] = (value * gate[...]).astype(BF16)
    acts[:, hidden:] = (value * upper[...]).astype(BF16)
    cut = near.shape[2]
    rest = rows - cut
    wire = Wire(rs, rr)

    def term(i, tz, first, size):
        return wd.at[pl.ds(first, size), pl.ds(pl.multiple_of(i * pair + tz * cols, cols), cols)]

    def ring(plane, tz, first, size):
        return Ring(
            wire,
            4 + plane * Ring.SIZE,
            [term(i, tz, first, size) for i in range(4)],
            (
                lambda ref: ref.at[pl.ds(0, size // 2), :],
                lambda ref: ref.at[pl.ds(size // 2, size // 2), :],
            ),
            [near.at[plane, k, pl.ds(0, size), :] for k in range(2)],
            [far.at[plane, k, pl.ds(0, size), :] for k in range(2)],
            {"kvh": yp},
            {"kvh": ym},
        )

    outer, inner, last = ring(0, zo, 0, cut), ring(1, z, 0, cut), ring(2, z, cut, rest)
    row_acc[...] = jnp.zeros_like(row_acc)
    for i, ty in enumerate((y2, yp, ym, y)):
        span = pl.ds(pl.multiple_of(ty * pair, pair), pair)
        value = contract_cols(acts[:, :hidden], wg[span, :]) + contract_cols(acts[:, hidden:], wu[span, :])
        wd[:, i * pair : (i + 1) * pair] = value.astype(BF16)
        wire.send(i, term(i, zo, cut, rest), zbuf.at[i], {"section": zo})
        for one in (outer, inner):
            (one.send_far, one.send_plus, one.send_minus, lambda: None)[i]()
        row_acc[...] += fold(value * ffn[:, span].astype(F32) * ffn_gain[:, span])
    share(2, to_row(row_acc[...] * inv_col[...]))

    def weights():
        for i in range(4):
            span = slice(i * pair, (i + 1) * pair)
            value = contract_rows(act[:, span], acts[:, :hidden])
            gate_grad[0, span, :] = value.astype(BF16)
            yield
            value = contract_rows(act[:, span], acts[:, hidden:])
            up_grad[0, span, :] = value.astype(BF16)
            yield
        down(y2)

    def blend(i):
        wire.got(i, zbuf.at[i], {"section": zo})
        ref = term(i, z, cut, rest)
        ref[...] = add(ref[...], zbuf[i]).astype(BF16)

    def sums():
        outer.relay_plus()
        outer.relay_minus()
        yield
        blend(0)
        last.send_far()
        inner.relay_plus()
        inner.relay_minus()
        yield
        blend(1)
        last.send_plus()
        blend(2)
        last.send_minus()
        yield
        zsend[...] = outer.collect().astype(BF16)
        wire.send(SCATTER8 - 1, zsend, zrecv, {"section": zo})
        yield
        last.relay_plus()
        last.relay_minus()
        yield
        blend(3)
        final[pl.ds(0, cut), :] = inner.collect()
        yield
        final[pl.ds(cut, rest), :] = last.collect()
        yield
        wire.got(SCATTER8 - 1, zrecv, {"section": zo})
        final[pl.ds(0, cut), :] += zrecv[...].astype(F32)

    run_all(weights(), sums())
    inverse = wide(inv_col[...], cols)
    correction = wide(to_column(total_of(2) / width), cols)
    hat = ffn[:, pl.ds(offset, cols)].astype(F32) * inverse
    input_grad[...] = (
        y_own[...].astype(F32)
        + inverse * (ffn_gain[:, pl.ds(offset, cols)] * final[...] - hat * correction)
    ).astype(BF16)
    wire.finish()
    stat_wire.finish()


def tail(dkv, ffn_input, kv_input, residual, kv_gain, ffn_gain, w_key, w_value, w_gate, w_up, w_down):
    rows, cols = kv_input.shape
    width, hidden = w_gate.shape
    cut = rows * 9 // 16
    rest = rows - cut
    any_space = pl.BlockSpec(memory_space=pl.ANY)
    in_vmem = pl.BlockSpec(memory_space=VMEM)
    dma = pltpu.SemaphoreType.DMA
    heads = w_key.shape[1]
    return pl.pallas_call(
        tail_kernel,
        name="tail",
        out_shape=(
            VMEM((rows, cols), BF16),
            VMEM((1, cols, heads), BF16),
            VMEM((1, cols, heads), BF16),
            VMEM((1, width, hidden), BF16),
            VMEM((1, width, hidden), BF16),
            VMEM((1, hidden, width), BF16),
        ),
        in_specs=[in_vmem] + [any_space] * 3 + [in_vmem] * 2 + [any_space] * 5,
        out_specs=(in_vmem,) * 6,
        scratch_shapes=[
            VMEM((2 * rows, HEAD), BF16),
            VMEM((rows, cols), BF16),
            VMEM((2 * rows, heads), BF16),
            VMEM((rows, width), BF16),
            VMEM((rows, cols), BF16),
            VMEM((rows, cols), BF16),
            VMEM((cols, heads), BF16),
            VMEM((cols, heads), BF16),
            VMEM((width, hidden), BF16),
            VMEM((width, hidden), BF16),
            VMEM((hidden, width), BF16),
            VMEM((rows, width), BF16),
            VMEM((rows, hidden), F32),
            VMEM((rows, hidden), F32),
            VMEM((hidden, rows), BF16),
            VMEM((rows, HEAD), F32),
            VMEM((rows, cols), F32),
            VMEM((rows, cols), BF16),
            VMEM((rows, cols), BF16),
            VMEM((rows, width), BF16),
            VMEM((rows, hidden), F32),
            VMEM((rows, 2 * hidden), BF16),
            VMEM((rows, HEAD), F32),
            VMEM((rows, cols), F32),
            VMEM((4, 4, rows, HEAD), BF16),
            VMEM((4, 2, rows, HEAD), BF16),
            VMEM((4, 2, rows, HEAD), BF16),
            VMEM((2, rows, HEAD), BF16),
            VMEM((2, rows, HEAD), BF16),
            VMEM((3, 8, rows), F32),
            VMEM((3, 7, 8, rows), F32),
            VMEM((4, rest, cols), BF16),
            VMEM((3, 2, cut, cols), BF16),
            VMEM((3, 2, cut, cols), BF16),
            VMEM((cut, cols), BF16),
            VMEM((cut, cols), BF16),
            dma((8,)), dma((SCATTER16,)), dma((SCATTER16,)), dma((GATHER8,)), dma((GATHER8,)),
            dma((GATHER8,)), dma((GATHER8,)), dma((GATHER8,)), dma((GATHER8,)),
            dma((SCATTER8,)), dma((SCATTER8,)), dma((21,)), dma((21,)),
        ],
        compiler_params=pltpu.CompilerParams(
            collective_id=3, has_side_effects=True, vmem_limit_bytes=44_000_000
        ),
    )(
        pltpu.with_memory_space_constraint(dkv, VMEM),
        ffn_input, kv_input, residual, kv_gain.reshape(1, -1), ffn_gain.reshape(1, -1),
        w_key, w_value, w_gate, w_up, w_down,
    )


MASKED = -1e30
START = -1e29


def attention_kernel(
    bound_ref, seen_ref, q_ref, g_ref, kv_ref, dq_ref, dkv_ref,
    q_cat, g_cat, q_t, g_t, run_max, run_sum, run_dot, dq_t, p_all, d_all, *, tile, scale
):
    rows = q_ref.shape[0]
    group = q_ref.shape[1] // HEAD
    own = lax.axis_index(BLK)
    lowest, highest = bound_ref[0], bound_ref[rows - 1]
    to_log2 = scale * LOG2E
    for h in range(group):
        for src, cat, turned in ((q_ref, q_cat, q_t), (g_ref, g_cat, g_t)):
            block = src[:, h * HEAD : (h + 1) * HEAD]
            cat[h * rows : (h + 1) * rows, :] = block
            turned[:, h * rows : (h + 1) * rows] = block.astype(F32).T.astype(BF16)
    run_max[...] = jnp.full_like(run_max, START)
    run_sum[...] = jnp.zeros_like(run_sum)
    run_dot[...] = jnp.zeros_like(run_dot)
    dq_t[...] = jnp.zeros_like(dq_t)

    tiles = dkv_ref.shape[1] // tile
    first = lowest // tile
    last = ((own + 1) * rows) // tile
    whole_from = jnp.minimum((highest + tile - 1) // tile, (own * rows) // tile)
    whole_to = (own * rows) // tile

    def part(j):
        return pl.ds(pl.multiple_of(j * tile, tile), tile)

    def lanes(h):
        return pl.ds(h * rows, rows)

    def scores(j, h, masked):
        keys = kv_ref[0, part(j), :]
        value = jnp.dot(keys, q_t[:, lanes(h)], preferred_element_type=F32) * to_log2
        if masked:
            key_pos = j * tile + lax.broadcasted_iota(jnp.int32, (tile, rows), 0)
            query_pos = own * rows + lax.broadcasted_iota(jnp.int32, (tile, rows), 1)
            visible = (key_pos <= query_pos) & (key_pos >= seen_ref[...])
            value = jnp.where(visible, value, MASKED)
        return value

    def products(j, h):
        return jnp.dot(kv_ref[1, part(j), :], g_t[:, lanes(h)], preferred_element_type=F32)

    def stats(j, masked):
        for h in range(group):
            value = scores(j, h, masked).reshape(tile // 8, 8, rows)
            dprobs = products(j, h).reshape(tile // 8, 8, rows)
            before = run_max[:, lanes(h)]
            now = jnp.maximum(before, jnp.max(value, axis=0))
            shrink = jnp.exp2(before - now)
            probs = jnp.exp2(value - now[None])
            run_max[:, lanes(h)] = now
            run_sum[:, lanes(h)] = run_sum[:, lanes(h)] * shrink + jnp.sum(probs, axis=0)
            run_dot[:, lanes(h)] = run_dot[:, lanes(h)] * shrink + jnp.sum(probs * dprobs, axis=0)

    def grads(j, masked):
        keys = kv_ref[0, part(j), :]
        for h in range(group):
            value = scores(j, h, masked)
            probs = jnp.exp2(value - run_max[0:1, lanes(h)])
            p_all[:, lanes(h)] = probs.astype(BF16)
            d_all[:, lanes(h)] = (probs * (products(j, h) - run_dot[0:1, lanes(h)])).astype(BF16)
        dkv_ref[1, part(j), :] = jnp.dot(p_all[...], g_cat[...], preferred_element_type=F32).astype(BF16)
        dkv_ref[0, part(j), :] = (
            jnp.dot(d_all[...], q_cat[...], preferred_element_type=F32) * scale
        ).astype(BF16)
        dq_t[...] += contract_rows(keys, d_all[...])

    def sweep(body):
        lax.fori_loop(first, whole_from, lambda j, _: (body(j, True), 0)[1], 0)
        lax.fori_loop(jnp.maximum(whole_from, first), whole_to, lambda j, _: (body(j, False), 0)[1], 0)
        lax.fori_loop(jnp.maximum(whole_to, first), last, lambda j, _: (body(j, True), 0)[1], 0)

    sweep(stats)
    peak = jnp.max(run_max[...], axis=0, keepdims=True)
    factor = jnp.exp2(run_max[...] - peak)
    total = jnp.sum(run_sum[...] * factor, axis=0, keepdims=True)
    delta = jnp.sum(run_dot[...] * factor, axis=0, keepdims=True) / total
    run_max[0:1, :] = peak + jnp.log(total) * LOG2E
    run_dot[0:1, :] = delta

    def clear(j, _):
        dkv_ref[:, part(j), :] = jnp.zeros((2, tile, HEAD), BF16)
        return 0

    lax.fori_loop(0, first, clear, 0)
    lax.fori_loop(last, tiles, clear, 0)
    sweep(grads)
    for h in range(group):
        dq_ref[:, h * HEAD : (h + 1) * HEAD] = (dq_t[:, lanes(h)] * scale).T.astype(BF16)


def attention(query, out_grad, kv, visible_from, tile=512):
    rows, width = query.shape
    group = width // HEAD
    cat = VMEM((group * rows, HEAD), BF16)
    turned = VMEM((HEAD, group * rows), BF16)
    stat = VMEM((8, group * rows), F32)
    return pl.pallas_call(
        functools.partial(attention_kernel, tile=tile, scale=1.0 / math.sqrt(HEAD)),
        name="attention",
        out_shape=(
            jax.ShapeDtypeStruct((rows, width), BF16),
            VMEM(kv.shape, BF16),
        ),
        in_specs=[pl.BlockSpec(memory_space=pltpu.SMEM)] + [pl.BlockSpec(memory_space=VMEM)] * 4,
        out_specs=(pl.BlockSpec(memory_space=VMEM),) * 2,
        scratch_shapes=[
            cat, cat, turned, turned, stat, stat, stat, VMEM((HEAD, group * rows), F32),
            VMEM((tile, group * rows), BF16), VMEM((tile, group * rows), BF16),
        ],
        compiler_params=pltpu.CompilerParams(vmem_limit_bytes=32_000_000),
    )(visible_from, visible_from.reshape(1, rows), query, out_grad, kv)


def write_kernel(*refs):
    count = len(refs) // 2
    sem = refs[-1]
    copies = []
    for k in range(count):
        src, dst = refs[k], refs[count + k]
        rows = src.shape[-2]
        for piece in range(2):
            span = pl.ds(piece * rows // 2, rows // 2)
            at = (span,) if len(src.shape) == 2 else (0, span)
            copies.append(pltpu.make_async_copy(src.at[at], dst.at[at], sem.at[2 * k + piece]))
    for copy in copies:
        copy.start()
    for copy in copies:
        copy.wait()


def write_out(arrays):
    return pl.pallas_call(
        write_kernel,
        name="write_out",
        out_shape=tuple(jax.ShapeDtypeStruct(a.shape, a.dtype) for a in arrays),
        in_specs=[pl.BlockSpec(memory_space=VMEM)] * len(arrays),
        out_specs=(pl.BlockSpec(memory_space=pl.ANY),) * len(arrays),
        scratch_shapes=[pltpu.SemaphoreType.DMA((2 * len(arrays),))],
        compiler_params=pltpu.CompilerParams(vmem_limit_bytes=8_000_000),
    )(*[pltpu.with_memory_space_constraint(a, VMEM) for a in arrays])


def on_device(
    query, keys, values, out_grad, visible_from, kv_input, residual_grad, ffn_input,
    kv_gain, ffn_gain, w_key, w_value, w_gate, w_up, w_down,
):
    rows = query.shape[0]
    every = gather_first(keys, values)
    blocks = every.shape[1]
    query_grad, dkv = attention(query, out_grad, every.reshape(2, blocks * rows, HEAD), visible_from)
    rest = tail(
        dkv.reshape(2, blocks, rows, HEAD), ffn_input, kv_input, residual_grad, kv_gain, ffn_gain,
        w_key, w_value, w_gate, w_up, w_down,
    )
    return (query_grad, *write_out(rest))


def solution(mesh):
    finer = Mesh(
        mesh.devices.reshape(4, 2, 2, mesh.shape["kvh"], mesh.shape["section"]),
        (*BLK, *FEAT),
    )
    tokens = P(BLK, FEAT)
    placed = (
        tokens, tokens, tokens, tokens, P(BLK), tokens, tokens, tokens, P(), P(),
        P(FEAT, None), P(FEAT, None), P(None, FEAT), P(None, FEAT), P(FEAT, None),
    )
    return jax.shard_map(
        on_device,
        mesh=finer,
        in_specs=placed,
        out_specs=(
            tokens,
            tokens,
            P(BLK, FEAT, None),
            P(BLK, FEAT, None),
            P(BLK, None, FEAT),
            P(BLK, None, FEAT),
            P(BLK, FEAT, None),
        ),
        check_vma=False,
    )
```

```python
import functools
import math

import jax
import jax.numpy as jnp
from jax import lax
from jax.experimental import pallas as pl
from jax.experimental.pallas import tpu as pltpu
from jax.sharding import Mesh
from jax.sharding import PartitionSpec as P

HEAD = 128
BLK = ("bx", "bz", "bc")
FEAT = ("kvh", "section")
MESH = pl.DeviceIdType.MESH
LOG2E = 1.4426950408889634
VMEM = pltpu.VMEM
F32 = jnp.float32
BF16 = jnp.bfloat16

epsilon = 1e-06


def contract_rows(left, right):
    return lax.dot_general(left, right, (((0,), (0,)), ((), ())), preferred_element_type=F32)


def contract_cols(left, right):
    return lax.dot_general(left, right, (((1,), (1,)), ((), ())), preferred_element_type=F32)


def run_all(*plans):
    live = list(plans)
    while live:
        for plan in list(live):
            try:
                next(plan)
            except StopIteration:
                live.remove(plan)


def run_some(plan):
    try:
        next(plan)
    except StopIteration:
        pass


def run_first(main, *others):
    for _ in main:
        for other in others:
            run_some(other)


def chain(*plans):
    for plan in plans:
        yield from plan


def meet(peers):
    barrier = pltpu.get_barrier_semaphore()
    for peer in peers:
        pl.semaphore_signal(barrier, inc=1, device_id=peer, device_id_type=MESH)
    pl.semaphore_wait(barrier, len(peers))


class Wire:
    def __init__(self, send_sem, recv_sem):
        self.send_sem, self.recv_sem, self.sent = send_sem, recv_sem, []

    def send(self, i, src, dst, peer):
        copy = pltpu.make_async_remote_copy(
            src_ref=src,
            dst_ref=dst,
            send_sem=self.send_sem.at[i],
            recv_sem=self.recv_sem.at[i],
            device_id=peer,
            device_id_type=MESH,
        )
        copy.start()
        self.sent.append(copy)

    def got(self, i, dst, peer):
        pltpu.make_async_remote_copy(
            src_ref=dst,
            dst_ref=dst,
            send_sem=self.send_sem.at[i],
            recv_sem=self.recv_sem.at[i],
            device_id=peer,
            device_id_type=MESH,
        ).wait_recv()

    def finish(self):
        for copy in self.sent:
            copy.wait_send()


def feat_place():
    y, z = lax.axis_index("kvh"), lax.axis_index("section")
    return y, lax.rem(y + 1, 4), lax.rem(y + 3, 4), lax.rem(y + 2, 4), z, 1 - z


def feat_peers():
    y, yp, ym, y2, z, zo = feat_place()
    return [{"kvh": yp}, {"kvh": ym}, {"section": zo}]


def feat_others():
    y, yp, ym, y2, z, zo = feat_place()
    others = [{"section": zo}]
    for other in (yp, ym, y2):
        others.append({"kvh": other})
        others.append({"kvh": other, "section": zo})
    return others


def blk_place():
    x, z, c = lax.axis_index("bx"), lax.axis_index("bz"), lax.axis_index("bc")
    return x, lax.rem(x + 1, 4), lax.rem(x + 3, 4), lax.rem(x + 2, 4), z, 1 - z, c, 1 - c


def blk_peers():
    x, xp, xm, x2, z, zo, c, co = blk_place()
    return [{"bx": xp}, {"bx": xm}, {"bz": zo}, {"bc": co}]


GATHER8 = 18


def tree(place, rows, cut, own, on, got):
    y, yp, ym, y2, z, zo = place
    rest = rows - cut
    full_a, low_a, high_a = (0, cut), (0, cut // 2), (cut // 2, cut // 2)
    full_b, low_b, high_b = (cut, rest), (cut, rest // 2), (cut + rest // 2, rest // 2)
    own(0, full_a, "o")
    own(1, full_a, "p")
    own(2, full_a, "m")
    own(3, full_b, "p")
    own(4, full_b, "m")
    own(5, full_b, "o")
    yield
    got(0, y, zo, full_a)
    on(6, y, zo, full_a, "p")
    on(7, y, zo, full_a, "m")
    yield
    got(1, ym, z, full_a)
    on(8, ym, z, low_a, "p")
    yield
    got(2, yp, z, full_a)
    on(9, yp, z, high_a, "m")
    yield
    got(3, ym, z, full_b)
    on(10, ym, z, low_b, "p")
    on(12, ym, z, full_b, "o")
    yield
    got(4, yp, z, full_b)
    on(11, yp, z, high_b, "m")
    on(13, yp, z, full_b, "o")
    yield
    got(5, y, zo, full_b)
    yield y, False
    got(6, ym, zo, full_a)
    on(14, ym, zo, low_a, "p")
    yield
    got(7, yp, zo, full_a)
    on(15, yp, zo, high_a, "m")
    yield
    got(10, y2, z, low_b)
    on(16, y2, z, low_b, "o")
    yield
    got(11, y2, z, high_b)
    on(17, y2, z, high_b, "o")
    yield
    got(12, ym, zo, full_b)
    yield ym, False
    got(13, yp, zo, full_b)
    yield yp, False
    got(8, y2, z, low_a)
    got(9, y2, z, high_a)
    got(14, y2, zo, low_a)
    got(15, y2, zo, high_a)
    got(16, y2, zo, low_b)
    got(17, y2, zo, high_b)
    yield y2, True


def gather8(wire, x_ref, out_ref, cut):
    place = y, yp, ym, y2, z, zo = feat_place()
    rows, cols = x_ref.shape
    peers = {"p": {"kvh": yp}, "m": {"kvh": ym}, "o": {"section": zo}}

    def at(sy, sz, part):
        start = pl.multiple_of((sy * 2 + sz) * cols, cols)
        return out_ref.at[pl.ds(part[0], part[1]), pl.ds(start, cols)]

    def own(i, part, way):
        wire.send(i, x_ref.at[pl.ds(part[0], part[1]), :], at(y, z, part), peers[way])

    def on(i, sy, sz, part, way):
        wire.send(i, at(sy, sz, part), at(sy, sz, part), peers[way])

    def got(i, sy, sz, part):
        wire.got(i, at(sy, sz, part), peers["o"])

    for stage in tree(place, rows, cut, own, on, got):
        if stage is not None and stage[1]:
            wire.finish()
        yield stage


GATHER16 = 2 * GATHER8 + 1


def gather16(wire, kv_ref, out_ref, cut):
    x, xp, xm, x2, z, zo, c, co = blk_place()
    rows = kv_ref.shape[1]
    peers = {"p": {"bx": xp}, "m": {"bx": xm}, "o": {"bz": zo}}
    twin = {"bc": co}
    arrived = []

    def at(sx, sz, part, sc):
        return out_ref.at[:, sx * 4 + sz * 2 + sc, pl.ds(part[0], part[1]), :]

    def own(i, part, way):
        wire.send(i, kv_ref.at[:, pl.ds(part[0], part[1]), :], at(x, z, part, c), peers[way])

    def on(i, sx, sz, part, way):
        wire.send(i, at(sx, sz, part, c), at(sx, sz, part, c), peers[way])

    def got(i, sx, sz, part):
        wire.got(i, at(sx, sz, part, c), peers["o"])
        wire.send(GATHER8 + i, at(sx, sz, part, c), at(sx, sz, part, c), twin)
        arrived.append((GATHER8 + i, sx, sz, part))

    first = True
    for _ in tree((x, xp, xm, x2, z, zo), rows, cut, own, on, got):
        if first:
            wire.send(2 * GATHER8, kv_ref, at(x, z, (0, rows), c), twin)
            arrived.append((2 * GATHER8, x, z, (0, rows)))
            first = False
        yield
    for i, sx, sz, part in arrived:
        wire.got(i, at(sx, sz, part, co), twin)
    wire.finish()


def first_kernel(key_ref, value_ref, kv_out, own, s0, r0, local):
    x, xp, xm, x2, z, zo, c, co = blk_place()
    loads = [
        pltpu.make_async_copy(key_ref, own.at[0], local.at[0]),
        pltpu.make_async_copy(value_ref, own.at[1], local.at[1]),
    ]
    for load in loads:
        load.start()
    meet(blk_peers())
    for load in loads:
        load.wait()
    keep = pltpu.make_async_copy(own, kv_out.at[:, x * 4 + z * 2 + c], local.at[2])
    plan = gather16(Wire(s0, r0), own, kv_out, own.shape[1] * 9 // 16)
    next(plan)
    keep.start()
    run_all(plan)
    keep.wait()


def gather_first(keys, values):
    rows, width = keys.shape
    return pl.pallas_call(
        first_kernel,
        name="gather_first",
        out_shape=VMEM((2, 16, rows, width), keys.dtype),
        in_specs=[pl.BlockSpec(memory_space=pltpu.HBM)] * 2,
        out_specs=pl.BlockSpec(memory_space=VMEM),
        scratch_shapes=[
            VMEM((2, rows, width), keys.dtype),
            pltpu.SemaphoreType.DMA((GATHER16,)),
            pltpu.SemaphoreType.DMA((GATHER16,)),
            pltpu.SemaphoreType.DMA((3,)),
        ],
        compiler_params=pltpu.CompilerParams(
            collective_id=1, has_side_effects=True, vmem_limit_bytes=16_000_000
        ),
    )(
        pltpu.with_memory_space_constraint(keys, pltpu.HBM),
        pltpu.with_memory_space_constraint(values, pltpu.HBM),
    )


def add(*terms):
    total = terms[0].astype(F32)
    for term in terms[1:]:
        total = total + term.astype(F32)
    return total


class Ring:
    SIZE = 6

    def __init__(self, wire, first, terms, halves, near, far, p, m):
        self.wire, self.first, self.p, self.m = wire, first, p, m
        self.far, self.plus, self.minus, self.own = terms
        self.low, self.high = halves
        self.near_p, self.near_m = near
        self.far_p, self.far_m = far

    def send_far(self):
        self.wire.send(self.first, self.high(self.far), self.high(self.far_m), self.p)
        self.wire.send(self.first + 1, self.low(self.far), self.low(self.far_p), self.m)

    def send_plus(self):
        self.wire.send(self.first + 2, self.low(self.plus), self.low(self.near_m), self.p)

    def send_minus(self):
        self.wire.send(self.first + 3, self.high(self.minus), self.high(self.near_p), self.m)

    def relay_plus(self):
        self.wire.got(self.first, self.high(self.far_m), self.p)
        ref = self.high(self.plus)
        ref[...] = add(ref[...], self.high(self.far_m)[...]).astype(BF16)
        self.wire.send(self.first + 4, ref, self.high(self.near_m), self.p)

    def relay_minus(self):
        self.wire.got(self.first + 1, self.low(self.far_p), self.p)
        ref = self.low(self.minus)
        ref[...] = add(ref[...], self.low(self.far_p)[...]).astype(BF16)
        self.wire.send(self.first + 5, ref, self.low(self.near_p), self.m)

    def collect(self):
        self.wire.got(self.first + 2, self.low(self.near_m), self.p)
        self.wire.got(self.first + 3, self.high(self.near_p), self.p)
        self.wire.got(self.first + 4, self.high(self.near_m), self.p)
        self.wire.got(self.first + 5, self.low(self.near_p), self.p)
        return add(self.own[...], self.near_p[...], self.near_m[...])


SCATTER16 = 8 + 4 + 3 * Ring.SIZE + 1


def scatter16(wire, part_ref, out_ref, acc, zbuf, near, far, zsend, zrecv):
    x, xp, xm, x2, z, zo, c, co = blk_place()
    rows = part_ref.shape[2]
    rest = zbuf.shape[2]
    cut = rows - rest
    across = {"bz": zo}
    turn = (x2, xp, xm, x)
    for p, tz in enumerate((zo, z)):
        for i, tx in enumerate(turn):
            wire.send(4 * p + i, part_ref.at[:, tx * 4 + tz * 2 + co], acc.at[p, i], {"bc": co})

    def merge(p, i):
        wire.got(4 * p + i, acc.at[p, i], {"bc": co})
        mine = part_ref[:, turn[i] * 4 + (zo, z)[p] * 2 + c]
        acc[p, i] = add(mine, acc[p, i]).astype(BF16)

    def term(p, i, first, size):
        return acc.at[p, i, :, pl.ds(first, size), :]

    def ring(k, p, first, size):
        return Ring(
            wire,
            12 + k * Ring.SIZE,
            [term(p, i, first, size) for i in range(4)],
            (
                lambda ref: ref.at[:, pl.ds(0, size // 2), :],
                lambda ref: ref.at[:, pl.ds(size // 2, size // 2), :],
            ),
            [near.at[k, n, :, pl.ds(0, size), :] for n in range(2)],
            [far.at[k, n, :, pl.ds(0, size), :] for n in range(2)],
            {"bx": xp},
            {"bx": xm},
        )

    outer, inner, last = ring(0, 0, 0, cut), ring(1, 1, 0, cut), ring(2, 1, cut, rest)

    def blend(i):
        wire.got(8 + i, zbuf.at[i], across)
        ref = term(1, i, cut, rest)
        ref[...] = add(ref[...], zbuf[i]).astype(BF16)

    def put(first, total):
        size = total.shape[1]
        out_ref[pl.ds(first, size), :] = total[0].astype(BF16)
        out_ref[pl.ds(rows + first, size), :] = total[1].astype(BF16)

    yield
    for p, one in enumerate((outer, inner)):
        for i in range(4):
            merge(p, i)
            if p == 0:
                wire.send(8 + i, term(0, i, cut, rest), zbuf.at[i], across)
            (one.send_far, one.send_plus, one.send_minus, lambda: None)[i]()
            yield
        if p == 0:
            outer.relay_plus()
            outer.relay_minus()
            yield
    blend(0)
    last.send_far()
    yield
    inner.relay_plus()
    inner.relay_minus()
    yield
    blend(1)
    last.send_plus()
    blend(2)
    last.send_minus()
    yield
    zsend[...] = outer.collect().astype(BF16)
    wire.send(SCATTER16 - 1, zsend, zrecv, across)
    yield
    last.relay_plus()
    last.relay_minus()
    yield
    blend(3)
    total = inner.collect()
    yield
    put(cut, last.collect())
    yield
    wire.got(SCATTER16 - 1, zrecv, across)
    put(0, total + zrecv[...].astype(F32))
    wire.finish()


SCATTER8 = 4 + 3 * Ring.SIZE + 1


def fold(value):
    total = value[:, :HEAD]
    for k in range(1, value.shape[1] // HEAD):
        total = total + value[:, k * HEAD : (k + 1) * HEAD]
    return total


def to_row(folded):
    return jnp.sum(folded.T, axis=0, keepdims=True)


def to_column(row):
    return jnp.broadcast_to(row, (HEAD, row.shape[1])).T


def wide(column, width):
    return jnp.concatenate([column] * (width // HEAD), axis=1)


def tail_kernel(
    dkv_ref, ffn_ref, kv_ref, res_ref, kv_gain, ffn_gain, wk_ref, wv_ref, wg_ref, wu_ref, wd_ref,
    input_grad, key_grad, value_grad, gate_grad, up_grad, down_grad,
    shard, ffn_own, heads, ffn, kv_in, res, wk, wv, wg, wu, wd,
    act, gate, upper, hidden_t, inv_col, kv_scaled, kv_n, y_own, y_full, hidden_grad, acts,
    row_acc, final, acc16, zbuf16, near16, far16, zsend16, zrecv16,
    stat_send, stat_slots, zbuf, near, far, zsend, zrecv,
    load_sem, ss, sr, fs, fr, hs, hr, ys, yr, rs, rr, ts, tr,
):
    y, yp, ym, y2, z, zo = feat_place()
    rows, cols = y_own.shape
    width = ffn.shape[1]
    pair = 2 * cols
    others = feat_others()
    loads = [
        pltpu.make_async_copy(src, dst, load_sem.at[i])
        for i, (src, dst) in enumerate(
            (
                (ffn_ref, ffn_own), (kv_ref, kv_in), (wg_ref, wg), (wu_ref, wu), (wk_ref, wk),
                (wv_ref, wv), (res_ref, res), (wd_ref, wd),
            )
        )
    ]
    for load in loads:
        load.start()
    meet(others + blk_peers())
    offset = pl.multiple_of((y * 2 + z) * cols, cols)
    stat_wire = Wire(ts, tr)

    def share(k, row):
        stat_send[k] = jnp.broadcast_to(row, (8, rows))
        for i, peer in enumerate(others):
            stat_wire.send(7 * k + i, stat_send.at[k], stat_slots.at[k, i], peer)

    def total_of(k):
        total = stat_send[k]
        for i, peer in enumerate(others):
            stat_wire.got(7 * k + i, stat_slots.at[k, i], peer)
            total = total + stat_slots[k, i]
        return total[0:1, :]

    def group(ref, i):
        return ref[:, pl.ds(pl.multiple_of(i * pair, pair), pair)]

    def forward():
        loads[1].wait()
        floats = kv_in[...].astype(F32)
        share(0, to_row(fold(floats * floats)))
        yield
        squares = jnp.zeros((rows, HEAD), F32)
        for i in range(4):
            floats = ffn[:, i * pair : (i + 1) * pair].astype(F32)
            squares = squares + fold(floats * floats)
        inverse = lax.rsqrt(jnp.sum(squares, axis=-1, keepdims=True) / width + epsilon)
        inv_col[...] = jnp.broadcast_to(inverse, (rows, HEAD))
        gate[...] = jnp.zeros_like(gate)
        upper[...] = jnp.zeros_like(upper)
        yield
        for i in range(4):
            span = slice(i * pair, (i + 1) * pair)
            scaled = ffn[:, span].astype(F32) * wide(inv_col[...], pair) * ffn_gain[:, span]
            act[:, span] = scaled.astype(BF16)
            yield
            if i == 0:
                loads[2].wait()
                loads[3].wait()
            gate[...] += jnp.dot(act[:, span], wg[span, :], preferred_element_type=F32)
            yield
            upper[...] += jnp.dot(act[:, span], wu[span, :], preferred_element_type=F32)
            yield

    loads[0].wait()
    kv_sums = scatter16(Wire(ss, sr), dkv_ref, shard, acc16, zbuf16, near16, far16, zsend16, zrecv16)
    ffn_plan = gather8(Wire(fs, fr), ffn_own, ffn, rows * 7 // 8)
    ahead = forward()
    next(kv_sums)
    next(ffn_plan)
    ffn[:, pl.ds(offset, cols)] = ffn_own[...]
    next(ahead)
    run_first(kv_sums, ffn_plan)
    plan = gather8(Wire(hs, hr), shard, heads, rows * 9 // 8)
    next(plan)
    heads[:, pl.ds(pl.multiple_of((y * 2 + z) * HEAD, HEAD), HEAD)] = shard[...]
    run_all(plan, chain(ffn_plan, ahead))

    for load in loads[4:]:
        load.wait()
    normed = contract_cols(heads[:rows, :], wk[...]) + contract_cols(heads[rows:, :], wv[...])
    gain = kv_gain[:, pl.ds(offset, cols)]
    scaled = gain * normed.astype(BF16).astype(F32)
    kv_scaled[...] = scaled
    kv_floats = kv_in[...].astype(F32)
    share(1, to_row(fold(scaled * kv_floats)))
    kv_inv = wide(to_column(lax.rsqrt(total_of(0) / width + epsilon)), cols)
    kv_hat = kv_in[...].astype(F32) * kv_inv
    kv_n[...] = (kv_hat * kv_gain[:, pl.ds(offset, cols)]).astype(BF16)
    key_grad[0] = contract_rows(kv_n[...], heads[:rows, :]).astype(BF16)
    mean = wide(to_column(total_of(1) / width), cols) * kv_inv
    y_own[...] = (res[...].astype(F32) + kv_inv * (kv_scaled[...] - kv_hat * mean)).astype(BF16)

    plan = gather8(Wire(ys, yr), y_own, y_full, rows * 9 // 16)
    next(plan)
    y_full[:, pl.ds(offset, cols)] = y_own[...]
    hidden_grad[...] = jnp.zeros_like(hidden_grad)

    def other_kv():
        value_grad[0] = contract_rows(kv_n[...], heads[rows:, :]).astype(BF16)
        yield
        hidden_t[...] = (gate[...] * jax.nn.sigmoid(gate[...]) * upper[...]).T.astype(BF16)
        yield
        value = gate[...]
        sigmoid = jax.nn.sigmoid(value)
        gate[...] = upper[...] * sigmoid * (1.0 + value * (1.0 - sigmoid))
        upper[...] = value * sigmoid

    def down(i):
        down_grad[0, :, pl.ds(pl.multiple_of(i * pair, pair), pair)] = jnp.dot(
            hidden_t[...], group(y_full, i), preferred_element_type=F32
        ).astype(BF16)

    def back(i):
        hidden_grad[...] += contract_cols(group(y_full, i), group(wd, i))

    filler = other_kv()
    for stage in plan:
        if stage is None:
            run_some(filler)
            continue
        i, is_last = stage
        back(i)
        if not is_last:
            down(i)

    value = hidden_grad[...]
    hidden = gate.shape[1]
    acts[:, :hidden] = (value * gate[...]).astype(BF16)
    acts[:, hidden:] = (value * upper[...]).astype(BF16)
    cut = near.shape[2]
    rest = rows - cut
    wire = Wire(rs, rr)

    def term(i, tz, first, size):
        return wd.at[pl.ds(first, size), pl.ds(pl.multiple_of(i * pair + tz * cols, cols), cols)]

    def ring(plane, tz, first, size):
        return Ring(
            wire,
            4 + plane * Ring.SIZE,
            [term(i, tz, first, size) for i in range(4)],
            (
                lambda ref: ref.at[pl.ds(0, size // 2), :],
                lambda ref: ref.at[pl.ds(size // 2, size // 2), :],
            ),
            [near.at[plane, k, pl.ds(0, size), :] for k in range(2)],
            [far.at[plane, k, pl.ds(0, size), :] for k in range(2)],
            {"kvh": yp},
            {"kvh": ym},
        )

    outer, inner, last = ring(0, zo, 0, cut), ring(1, z, 0, cut), ring(2, z, cut, rest)
    row_acc[...] = jnp.zeros_like(row_acc)
    for i, ty in enumerate((y2, yp, ym, y)):
        span = pl.ds(pl.multiple_of(ty * pair, pair), pair)
        value = contract_cols(acts[:, :hidden], wg[span, :]) + contract_cols(acts[:, hidden:], wu[span, :])
        wd[:, i * pair : (i + 1) * pair] = value.astype(BF16)
        wire.send(i, term(i, zo, cut, rest), zbuf.at[i], {"section": zo})
        for one in (outer, inner):
            (one.send_far, one.send_plus, one.send_minus, lambda: None)[i]()
        row_acc[...] += fold(value * ffn[:, span].astype(F32) * ffn_gain[:, span])
    share(2, to_row(row_acc[...] * inv_col[...]))

    def weights():
        for i in range(4):
            span = slice(i * pair, (i + 1) * pair)
            value = contract_rows(act[:, span], acts[:, :hidden])
            gate_grad[0, span, :] = value.astype(BF16)
            yield
            value = contract_rows(act[:, span], acts[:, hidden:])
            up_grad[0, span, :] = value.astype(BF16)
            yield
        down(y2)

    def blend(i):
        wire.got(i, zbuf.at[i], {"section": zo})
        ref = term(i, z, cut, rest)
        ref[...] = add(ref[...], zbuf[i]).astype(BF16)

    def sums():
        outer.relay_plus()
        outer.relay_minus()
        yield
        blend(0)
        last.send_far()
        inner.relay_plus()
        inner.relay_minus()
        yield
        blend(1)
        last.send_plus()
        blend(2)
        last.send_minus()
        yield
        zsend[...] = outer.collect().astype(BF16)
        wire.send(SCATTER8 - 1, zsend, zrecv, {"section": zo})
        yield
        last.relay_plus()
        last.relay_minus()
        yield
        blend(3)
        final[pl.ds(0, cut), :] = inner.collect()
        yield
        final[pl.ds(cut, rest), :] = last.collect()
        yield
        wire.got(SCATTER8 - 1, zrecv, {"section": zo})
        final[pl.ds(0, cut), :] += zrecv[...].astype(F32)

    run_all(weights(), sums())
    inverse = wide(inv_col[...], cols)
    correction = wide(to_column(total_of(2) / width), cols)
    hat = ffn[:, pl.ds(offset, cols)].astype(F32) * inverse
    input_grad[...] = (
        y_own[...].astype(F32)
        + inverse * (ffn_gain[:, pl.ds(offset, cols)] * final[...] - hat * correction)
    ).astype(BF16)
    wire.finish()
    stat_wire.finish()


def tail(dkv, ffn_input, kv_input, residual, kv_gain, ffn_gain, w_key, w_value, w_gate, w_up, w_down):
    rows, cols = kv_input.shape
    width, hidden = w_gate.shape
    cut = rows * 9 // 16
    rest = rows - cut
    any_space = pl.BlockSpec(memory_space=pl.ANY)
    in_vmem = pl.BlockSpec(memory_space=VMEM)
    dma = pltpu.SemaphoreType.DMA
    heads = w_key.shape[1]
    return pl.pallas_call(
        tail_kernel,
        name="tail",
        out_shape=(
            VMEM((rows, cols), BF16),
            VMEM((1, cols, heads), BF16),
            VMEM((1, cols, heads), BF16),
            VMEM((1, width, hidden), BF16),
            VMEM((1, width, hidden), BF16),
            VMEM((1, hidden, width), BF16),
        ),
        in_specs=[in_vmem] + [any_space] * 3 + [in_vmem] * 2 + [any_space] * 5,
        out_specs=(in_vmem,) * 6,
        scratch_shapes=[
            VMEM((2 * rows, HEAD), BF16),
            VMEM((rows, cols), BF16),
            VMEM((2 * rows, heads), BF16),
            VMEM((rows, width), BF16),
            VMEM((rows, cols), BF16),
            VMEM((rows, cols), BF16),
            VMEM((cols, heads), BF16),
            VMEM((cols, heads), BF16),
            VMEM((width, hidden), BF16),
            VMEM((width, hidden), BF16),
            VMEM((hidden, width), BF16),
            VMEM((rows, width), BF16),
            VMEM((rows, hidden), F32),
            VMEM((rows, hidden), F32),
            VMEM((hidden, rows), BF16),
            VMEM((rows, HEAD), F32),
            VMEM((rows, cols), F32),
            VMEM((rows, cols), BF16),
            VMEM((rows, cols), BF16),
            VMEM((rows, width), BF16),
            VMEM((rows, hidden), F32),
            VMEM((rows, 2 * hidden), BF16),
            VMEM((rows, HEAD), F32),
            VMEM((rows, cols), F32),
            VMEM((2, 4, 2, rows, HEAD), BF16),
            VMEM((4, 2, rest, HEAD), BF16),
            VMEM((3, 2, 2, cut, HEAD), BF16),
            VMEM((3, 2, 2, cut, HEAD), BF16),
            VMEM((2, cut, HEAD), BF16),
            VMEM((2, cut, HEAD), BF16),
            VMEM((3, 8, rows), F32),
            VMEM((3, 7, 8, rows), F32),
            VMEM((4, rest, cols), BF16),
            VMEM((3, 2, cut, cols), BF16),
            VMEM((3, 2, cut, cols), BF16),
            VMEM((cut, cols), BF16),
            VMEM((cut, cols), BF16),
            dma((8,)), dma((SCATTER16,)), dma((SCATTER16,)), dma((GATHER8,)), dma((GATHER8,)),
            dma((GATHER8,)), dma((GATHER8,)), dma((GATHER8,)), dma((GATHER8,)),
            dma((SCATTER8,)), dma((SCATTER8,)), dma((21,)), dma((21,)),
        ],
        compiler_params=pltpu.CompilerParams(
            collective_id=3, has_side_effects=True, vmem_limit_bytes=44_000_000
        ),
    )(
        pltpu.with_memory_space_constraint(dkv, VMEM),
        ffn_input, kv_input, residual, kv_gain.reshape(1, -1), ffn_gain.reshape(1, -1),
        w_key, w_value, w_gate, w_up, w_down,
    )


MASKED = -1e30
START = -1e29


def attention_kernel(
    bound_ref, seen_ref, q_ref, g_ref, kv_ref, dq_ref, dkv_ref,
    q_cat, g_cat, q_t, g_t, run_max, run_sum, run_dot, dq_t, p_all, d_all, *, tile, scale
):
    rows = q_ref.shape[0]
    group = q_ref.shape[1] // HEAD
    own = lax.axis_index(BLK)
    lowest = bound_ref[0]
    to_log2 = scale * LOG2E
    for h in range(group):
        for src, cat, turned in ((q_ref, q_cat, q_t), (g_ref, g_cat, g_t)):
            block = src[:, h * HEAD : (h + 1) * HEAD]
            cat[h * rows : (h + 1) * rows, :] = block
            turned[:, h * rows : (h + 1) * rows] = block.astype(F32).T.astype(BF16)
    run_max[...] = jnp.full_like(run_max, START)
    run_sum[...] = jnp.zeros_like(run_sum)
    run_dot[...] = jnp.zeros_like(run_dot)
    dq_t[...] = jnp.zeros_like(dq_t)

    tiles = dkv_ref.shape[1] // tile
    first = lowest // tile
    last = ((own + 1) * rows) // tile
    whole_to = (own * rows) // tile
    whole_from = jnp.minimum((lowest + tile - 1) // tile, whole_to)

    def part(j):
        return pl.ds(pl.multiple_of(j * tile, tile), tile)

    def lanes(h):
        return pl.ds(h * rows, rows)

    def scores(j, h, masked):
        keys = kv_ref[0, part(j), :]
        value = jnp.dot(keys, q_t[:, lanes(h)], preferred_element_type=F32) * to_log2
        if masked:
            key_pos = j * tile + lax.broadcasted_iota(jnp.int32, (tile, rows), 0)
            query_pos = own * rows + lax.broadcasted_iota(jnp.int32, (tile, rows), 1)
            visible = (key_pos <= query_pos) & (key_pos >= seen_ref[...])
            value = jnp.where(visible, value, MASKED)
        return value

    def unseen(j, row, masked):
        return row if masked else jnp.where(seen_ref[...] > j * tile, -MASKED, row)

    def products(j, h):
        return jnp.dot(kv_ref[1, part(j), :], g_t[:, lanes(h)], preferred_element_type=F32)

    def stats(j, masked):
        for h in range(group):
            value = scores(j, h, masked).reshape(tile // 8, 8, rows)
            dprobs = products(j, h).reshape(tile // 8, 8, rows)
            before = run_max[:, lanes(h)]
            now = jnp.maximum(before, jnp.max(value, axis=0))
            if not masked:
                now = jnp.where(seen_ref[...] > j * tile, before, now)
            shrink = jnp.exp2(before - now)
            probs = jnp.exp2(value - unseen(j, now, masked)[None])
            run_max[:, lanes(h)] = now
            run_sum[:, lanes(h)] = run_sum[:, lanes(h)] * shrink + jnp.sum(probs, axis=0)
            run_dot[:, lanes(h)] = run_dot[:, lanes(h)] * shrink + jnp.sum(probs * dprobs, axis=0)

    def grads(j, masked):
        keys = kv_ref[0, part(j), :]
        for h in range(group):
            value = scores(j, h, masked)
            probs = jnp.exp2(value - unseen(j, run_max[0:1, lanes(h)], masked))
            p_all[:, lanes(h)] = probs.astype(BF16)
            d_all[:, lanes(h)] = (probs * (products(j, h) - run_dot[0:1, lanes(h)])).astype(BF16)
        dkv_ref[1, part(j), :] = jnp.dot(p_all[...], g_cat[...], preferred_element_type=F32).astype(BF16)
        dkv_ref[0, part(j), :] = (
            jnp.dot(d_all[...], q_cat[...], preferred_element_type=F32) * scale
        ).astype(BF16)
        dq_t[...] += contract_rows(keys, d_all[...])

    def sweep(body):
        lax.fori_loop(first, whole_from, lambda j, _: (body(j, True), 0)[1], 0)
        lax.fori_loop(jnp.maximum(whole_from, first), whole_to, lambda j, _: (body(j, False), 0)[1], 0)
        lax.fori_loop(jnp.maximum(whole_to, first), last, lambda j, _: (body(j, True), 0)[1], 0)

    sweep(stats)
    peak = jnp.max(run_max[...], axis=0, keepdims=True)
    factor = jnp.exp2(run_max[...] - peak)
    total = jnp.sum(run_sum[...] * factor, axis=0, keepdims=True)
    delta = jnp.sum(run_dot[...] * factor, axis=0, keepdims=True) / total
    run_max[0:1, :] = peak + jnp.log(total) * LOG2E
    run_dot[0:1, :] = delta

    def clear(j, _):
        dkv_ref[:, part(j), :] = jnp.zeros((2, tile, HEAD), BF16)
        return 0

    lax.fori_loop(0, first, clear, 0)
    lax.fori_loop(last, tiles, clear, 0)
    sweep(grads)
    for h in range(group):
        dq_ref[:, h * HEAD : (h + 1) * HEAD] = (dq_t[:, lanes(h)] * scale).T.astype(BF16)


def attention(query, out_grad, kv, visible_from, tile=512):
    rows, width = query.shape
    group = width // HEAD
    cat = VMEM((group * rows, HEAD), BF16)
    turned = VMEM((HEAD, group * rows), BF16)
    stat = VMEM((8, group * rows), F32)
    return pl.pallas_call(
        functools.partial(attention_kernel, tile=tile, scale=1.0 / math.sqrt(HEAD)),
        name="attention",
        out_shape=(
            jax.ShapeDtypeStruct((rows, width), BF16),
            VMEM(kv.shape, BF16),
        ),
        in_specs=[pl.BlockSpec(memory_space=pltpu.SMEM)] + [pl.BlockSpec(memory_space=VMEM)] * 4,
        out_specs=(pl.BlockSpec(memory_space=VMEM),) * 2,
        scratch_shapes=[
            cat, cat, turned, turned, stat, stat, stat, VMEM((HEAD, group * rows), F32),
            VMEM((tile, group * rows), BF16), VMEM((tile, group * rows), BF16),
        ],
        compiler_params=pltpu.CompilerParams(vmem_limit_bytes=32_000_000),
    )(visible_from, visible_from.reshape(1, rows), query, out_grad, kv)


def write_kernel(*refs):
    count = len(refs) // 2
    sem = refs[-1]
    copies = []
    for k in range(count):
        src, dst = refs[k], refs[count + k]
        rows = src.shape[-2]
        for piece in range(2):
            span = pl.ds(piece * rows // 2, rows // 2)
            at = (span,) if len(src.shape) == 2 else (0, span)
            copies.append(pltpu.make_async_copy(src.at[at], dst.at[at], sem.at[2 * k + piece]))
    for copy in copies:
        copy.start()
    for copy in copies:
        copy.wait()


def write_out(arrays):
    return pl.pallas_call(
        write_kernel,
        name="write_out",
        out_shape=tuple(jax.ShapeDtypeStruct(a.shape, a.dtype) for a in arrays),
        in_specs=[pl.BlockSpec(memory_space=VMEM)] * len(arrays),
        out_specs=(pl.BlockSpec(memory_space=pl.ANY),) * len(arrays),
        scratch_shapes=[pltpu.SemaphoreType.DMA((2 * len(arrays),))],
        compiler_params=pltpu.CompilerParams(vmem_limit_bytes=8_000_000),
    )(*[pltpu.with_memory_space_constraint(a, VMEM) for a in arrays])


def on_device(
    query, keys, values, out_grad, visible_from, kv_input, residual_grad, ffn_input,
    kv_gain, ffn_gain, w_key, w_value, w_gate, w_up, w_down,
):
    rows = query.shape[0]
    every = gather_first(keys, values)
    blocks = every.shape[1]
    query_grad, dkv = attention(query, out_grad, every.reshape(2, blocks * rows, HEAD), visible_from)
    rest = tail(
        dkv.reshape(2, blocks, rows, HEAD), ffn_input, kv_input, residual_grad, kv_gain, ffn_gain,
        w_key, w_value, w_gate, w_up, w_down,
    )
    return (query_grad, *write_out(rest))


def solution(mesh):
    finer = Mesh(
        mesh.devices.reshape(4, 2, 2, mesh.shape["kvh"], mesh.shape["section"]),
        (*BLK, *FEAT),
    )
    tokens = P(BLK, FEAT)
    placed = (
        tokens, tokens, tokens, tokens, P(BLK), tokens, tokens, tokens, P(), P(),
        P(FEAT, None), P(FEAT, None), P(None, FEAT), P(None, FEAT), P(FEAT, None),
    )
    return jax.shard_map(
        on_device,
        mesh=finer,
        in_specs=placed,
        out_specs=(
            tokens,
            tokens,
            P(BLK, FEAT, None),
            P(BLK, FEAT, None),
            P(BLK, None, FEAT),
            P(BLK, None, FEAT),
            P(BLK, FEAT, None),
        ),
        check_vma=False,
    )
```

```python
import functools
import math

import jax
import jax.numpy as jnp
from jax import lax
from jax.experimental import pallas as pl
from jax.experimental.pallas import tpu as pltpu
from jax.sharding import Mesh
from jax.sharding import PartitionSpec as P

HEAD = 128
BLK = ("bx", "bz", "bc")
FEAT = ("kvh", "section")
MESH = pl.DeviceIdType.MESH
LOG2E = 1.4426950408889634
VMEM = pltpu.VMEM
F32 = jnp.float32
BF16 = jnp.bfloat16

epsilon = 1e-06


def contract_rows(left, right):
    return lax.dot_general(left, right, (((0,), (0,)), ((), ())), preferred_element_type=F32)


def contract_cols(left, right):
    return lax.dot_general(left, right, (((1,), (1,)), ((), ())), preferred_element_type=F32)


def run_all(*plans):
    live = list(plans)
    while live:
        for plan in list(live):
            try:
                next(plan)
            except StopIteration:
                live.remove(plan)


def run_some(plan):
    try:
        next(plan)
    except StopIteration:
        pass


def run_first(main, *others):
    for _ in main:
        for other in others:
            run_some(other)


def chain(*plans):
    for plan in plans:
        yield from plan


def meet(peers):
    barrier = pltpu.get_barrier_semaphore()
    for peer in peers:
        pl.semaphore_signal(barrier, inc=1, device_id=peer, device_id_type=MESH)
    pl.semaphore_wait(barrier, len(peers))


class Wire:
    def __init__(self, send_sem, recv_sem):
        self.send_sem, self.recv_sem, self.sent = send_sem, recv_sem, []

    def send(self, i, src, dst, peer):
        copy = pltpu.make_async_remote_copy(
            src_ref=src,
            dst_ref=dst,
            send_sem=self.send_sem.at[i],
            recv_sem=self.recv_sem.at[i],
            device_id=peer,
            device_id_type=MESH,
        )
        copy.start()
        self.sent.append(copy)

    def got(self, i, dst, peer):
        pltpu.make_async_remote_copy(
            src_ref=dst,
            dst_ref=dst,
            send_sem=self.send_sem.at[i],
            recv_sem=self.recv_sem.at[i],
            device_id=peer,
            device_id_type=MESH,
        ).wait_recv()

    def finish(self):
        for copy in self.sent:
            copy.wait_send()


def feat_place():
    y, z = lax.axis_index("kvh"), lax.axis_index("section")
    return y, lax.rem(y + 1, 4), lax.rem(y + 3, 4), lax.rem(y + 2, 4), z, 1 - z


def feat_peers():
    y, yp, ym, y2, z, zo = feat_place()
    return [{"kvh": yp}, {"kvh": ym}, {"section": zo}]


def feat_others():
    y, yp, ym, y2, z, zo = feat_place()
    others = [{"section": zo}]
    for other in (yp, ym, y2):
        others.append({"kvh": other})
        others.append({"kvh": other, "section": zo})
    return others


def blk_place():
    x, z, c = lax.axis_index("bx"), lax.axis_index("bz"), lax.axis_index("bc")
    return x, lax.rem(x + 1, 4), lax.rem(x + 3, 4), lax.rem(x + 2, 4), z, 1 - z, c, 1 - c


def blk_peers():
    x, xp, xm, x2, z, zo, c, co = blk_place()
    return [{"bx": xp}, {"bx": xm}, {"bz": zo}, {"bc": co}]


GATHER8 = 18


def tree(place, rows, cut, own, on, got):
    y, yp, ym, y2, z, zo = place
    rest = rows - cut
    full_a, low_a, high_a = (0, cut), (0, cut // 2), (cut // 2, cut // 2)
    full_b, low_b, high_b = (cut, rest), (cut, rest // 2), (cut + rest // 2, rest // 2)
    own(0, full_a, "o")
    own(1, full_a, "p")
    own(2, full_a, "m")
    own(3, full_b, "p")
    own(4, full_b, "m")
    own(5, full_b, "o")
    yield
    got(0, y, zo, full_a)
    on(6, y, zo, full_a, "p")
    on(7, y, zo, full_a, "m")
    yield
    got(1, ym, z, full_a)
    on(8, ym, z, low_a, "p")
    yield
    got(2, yp, z, full_a)
    on(9, yp, z, high_a, "m")
    yield
    got(3, ym, z, full_b)
    on(10, ym, z, low_b, "p")
    on(12, ym, z, full_b, "o")
    yield
    got(4, yp, z, full_b)
    on(11, yp, z, high_b, "m")
    on(13, yp, z, full_b, "o")
    yield
    got(5, y, zo, full_b)
    yield y, False
    got(6, ym, zo, full_a)
    on(14, ym, zo, low_a, "p")
    yield
    got(7, yp, zo, full_a)
    on(15, yp, zo, high_a, "m")
    yield
    got(10, y2, z, low_b)
    on(16, y2, z, low_b, "o")
    yield
    got(11, y2, z, high_b)
    on(17, y2, z, high_b, "o")
    yield
    got(12, ym, zo, full_b)
    yield ym, False
    got(13, yp, zo, full_b)
    yield yp, False
    got(8, y2, z, low_a)
    got(9, y2, z, high_a)
    got(14, y2, zo, low_a)
    got(15, y2, zo, high_a)
    got(16, y2, zo, low_b)
    got(17, y2, zo, high_b)
    yield y2, True


def gather8(wire, x_ref, out_ref, cut):
    place = y, yp, ym, y2, z, zo = feat_place()
    rows, cols = x_ref.shape
    peers = {"p": {"kvh": yp}, "m": {"kvh": ym}, "o": {"section": zo}}

    def at(sy, sz, part):
        start = pl.multiple_of((sy * 2 + sz) * cols, cols)
        return out_ref.at[pl.ds(part[0], part[1]), pl.ds(start, cols)]

    def own(i, part, way):
        wire.send(i, x_ref.at[pl.ds(part[0], part[1]), :], at(y, z, part), peers[way])

    def on(i, sy, sz, part, way):
        wire.send(i, at(sy, sz, part), at(sy, sz, part), peers[way])

    def got(i, sy, sz, part):
        wire.got(i, at(sy, sz, part), peers["o"])

    for stage in tree(place, rows, cut, own, on, got):
        if stage is not None and stage[1]:
            wire.finish()
        yield stage


GATHER16 = 2 * GATHER8 + 1


def gather16(wire, kv_ref, out_ref, cut):
    x, xp, xm, x2, z, zo, c, co = blk_place()
    rows = kv_ref.shape[1]
    peers = {"p": {"bx": xp}, "m": {"bx": xm}, "o": {"bz": zo}}
    twin = {"bc": co}
    arrived = []

    def at(sx, sz, part, sc):
        return out_ref.at[:, sx * 4 + sz * 2 + sc, pl.ds(part[0], part[1]), :]

    def own(i, part, way):
        wire.send(i, kv_ref.at[:, pl.ds(part[0], part[1]), :], at(x, z, part, c), peers[way])

    def on(i, sx, sz, part, way):
        wire.send(i, at(sx, sz, part, c), at(sx, sz, part, c), peers[way])

    def got(i, sx, sz, part):
        wire.got(i, at(sx, sz, part, c), peers["o"])
        wire.send(GATHER8 + i, at(sx, sz, part, c), at(sx, sz, part, c), twin)
        arrived.append((GATHER8 + i, sx, sz, part))

    first = True
    for _ in tree((x, xp, xm, x2, z, zo), rows, cut, own, on, got):
        if first:
            wire.send(2 * GATHER8, kv_ref, at(x, z, (0, rows), c), twin)
            arrived.append((2 * GATHER8, x, z, (0, rows)))
            first = False
        yield
    for i, sx, sz, part in arrived:
        wire.got(i, at(sx, sz, part, co), twin)
    wire.finish()


def first_kernel(key_ref, value_ref, ffn_ref, kv_out, ffn_out, own, own_ffn, s0, r0, s1, r1, local):
    x, xp, xm, x2, z, zo, c, co = blk_place()
    y, yp, ym, y2, sz, szo = feat_place()
    rows, cols = own_ffn.shape
    loads = [
        pltpu.make_async_copy(key_ref, own.at[0], local.at[0]),
        pltpu.make_async_copy(value_ref, own.at[1], local.at[1]),
        pltpu.make_async_copy(ffn_ref.at[pl.ds(0, rows), :], own_ffn, local.at[2]),
    ]
    for load in loads:
        load.start()
    meet(blk_peers() + feat_peers())
    for load in loads:
        load.wait()
    keeps = [
        pltpu.make_async_copy(own, kv_out.at[:, x * 4 + z * 2 + c], local.at[3]),
        pltpu.make_async_copy(
            own_ffn,
            ffn_out.at[:, pl.ds(pl.multiple_of((y * 2 + sz) * cols, cols), cols)],
            local.at[4],
        ),
    ]
    kv_plan = gather16(Wire(s0, r0), own, kv_out, own.shape[1] * 3 // 4)
    ffn_plan = gather8(Wire(s1, r1), own_ffn, ffn_out, rows * 7 // 8)
    next(kv_plan)
    next(ffn_plan)
    for keep in keeps:
        keep.start()
    run_all(kv_plan, ffn_plan)
    for keep in keeps:
        keep.wait()


def gather_first(keys, values, ffn):
    rows, width = keys.shape
    half, cols = ffn.shape[0] // 2, ffn.shape[1]
    dma = pltpu.SemaphoreType.DMA
    return pl.pallas_call(
        first_kernel,
        name="gather_first",
        out_shape=(
            VMEM((2, 16, rows, width), keys.dtype),
            VMEM((half, 8 * cols), ffn.dtype),
        ),
        in_specs=[pl.BlockSpec(memory_space=pltpu.HBM)] * 3,
        out_specs=(pl.BlockSpec(memory_space=VMEM),) * 2,
        scratch_shapes=[
            VMEM((2, rows, width), keys.dtype),
            VMEM((half, cols), ffn.dtype),
            dma((GATHER16,)), dma((GATHER16,)), dma((GATHER8,)), dma((GATHER8,)), dma((5,)),
        ],
        compiler_params=pltpu.CompilerParams(
            collective_id=1, has_side_effects=True, vmem_limit_bytes=16_000_000
        ),
    )(*[pltpu.with_memory_space_constraint(a, pltpu.HBM) for a in (keys, values, ffn)])


def add(*terms):
    total = terms[0].astype(F32)
    for term in terms[1:]:
        total = total + term.astype(F32)
    return total


class Ring:
    SIZE = 6

    def __init__(self, wire, first, terms, halves, near, far, p, m):
        self.wire, self.first, self.p, self.m = wire, first, p, m
        self.far, self.plus, self.minus, self.own = terms
        self.low, self.high = halves
        self.near_p, self.near_m = near
        self.far_p, self.far_m = far

    def send_far(self):
        self.wire.send(self.first, self.high(self.far), self.high(self.far_m), self.p)
        self.wire.send(self.first + 1, self.low(self.far), self.low(self.far_p), self.m)

    def send_plus(self):
        self.wire.send(self.first + 2, self.low(self.plus), self.low(self.near_m), self.p)

    def send_minus(self):
        self.wire.send(self.first + 3, self.high(self.minus), self.high(self.near_p), self.m)

    def relay_plus(self):
        self.wire.got(self.first, self.high(self.far_m), self.p)
        ref = self.high(self.plus)
        ref[...] = add(ref[...], self.high(self.far_m)[...]).astype(BF16)
        self.wire.send(self.first + 4, ref, self.high(self.near_m), self.p)

    def relay_minus(self):
        self.wire.got(self.first + 1, self.low(self.far_p), self.p)
        ref = self.low(self.minus)
        ref[...] = add(ref[...], self.low(self.far_p)[...]).astype(BF16)
        self.wire.send(self.first + 5, ref, self.low(self.near_p), self.m)

    def collect(self):
        self.wire.got(self.first + 2, self.low(self.near_m), self.p)
        self.wire.got(self.first + 3, self.high(self.near_p), self.p)
        self.wire.got(self.first + 4, self.high(self.near_m), self.p)
        self.wire.got(self.first + 5, self.low(self.near_p), self.p)
        return add(self.own[...], self.near_p[...], self.near_m[...])


SCATTER16 = 8 + 4 + 3 * Ring.SIZE + 1


def scatter16(wire, part_ref, out_ref, acc, zbuf, near, far, zsend, zrecv):
    x, xp, xm, x2, z, zo, c, co = blk_place()
    rows = part_ref.shape[2]
    rest = zbuf.shape[2]
    cut = rows - rest
    across = {"bz": zo}
    turn = (x2, xp, xm, x)
    for p, tz in enumerate((zo, z)):
        for i, tx in enumerate(turn):
            wire.send(4 * p + i, part_ref.at[:, tx * 4 + tz * 2 + co], acc.at[p, i], {"bc": co})

    def merge(p, i):
        wire.got(4 * p + i, acc.at[p, i], {"bc": co})
        mine = part_ref[:, turn[i] * 4 + (zo, z)[p] * 2 + c]
        acc[p, i] = add(mine, acc[p, i]).astype(BF16)

    def term(p, i, first, size):
        return acc.at[p, i, :, pl.ds(first, size), :]

    def ring(k, p, first, size):
        return Ring(
            wire,
            12 + k * Ring.SIZE,
            [term(p, i, first, size) for i in range(4)],
            (
                lambda ref: ref.at[:, pl.ds(0, size // 2), :],
                lambda ref: ref.at[:, pl.ds(size // 2, size // 2), :],
            ),
            [near.at[k, n, :, pl.ds(0, size), :] for n in range(2)],
            [far.at[k, n, :, pl.ds(0, size), :] for n in range(2)],
            {"bx": xp},
            {"bx": xm},
        )

    outer, inner, last = ring(0, 0, 0, cut), ring(1, 1, 0, cut), ring(2, 1, cut, rest)

    def blend(i):
        wire.got(8 + i, zbuf.at[i], across)
        ref = term(1, i, cut, rest)
        ref[...] = add(ref[...], zbuf[i]).astype(BF16)

    def put(first, total):
        size = total.shape[1]
        out_ref[pl.ds(first, size), :] = total[0].astype(BF16)
        out_ref[pl.ds(rows + first, size), :] = total[1].astype(BF16)

    yield
    for p, one in enumerate((outer, inner)):
        for i in range(4):
            merge(p, i)
            if p == 0:
                wire.send(8 + i, term(0, i, cut, rest), zbuf.at[i], across)
            (one.send_far, one.send_plus, one.send_minus, lambda: None)[i]()
            yield
        if p == 0:
            outer.relay_plus()
            outer.relay_minus()
            yield
    blend(0)
    last.send_far()
    yield
    inner.relay_plus()
    inner.relay_minus()
    yield
    blend(1)
    last.send_plus()
    blend(2)
    last.send_minus()
    yield
    zsend[...] = outer.collect().astype(BF16)
    wire.send(SCATTER16 - 1, zsend, zrecv, across)
    yield
    last.relay_plus()
    last.relay_minus()
    yield
    blend(3)
    total = inner.collect()
    yield
    put(cut, last.collect())
    yield
    wire.got(SCATTER16 - 1, zrecv, across)
    put(0, total + zrecv[...].astype(F32))
    wire.finish()


SCATTER8 = 4 + 3 * Ring.SIZE + 1


def fold(value):
    total = value[:, :HEAD]
    for k in range(1, value.shape[1] // HEAD):
        total = total + value[:, k * HEAD : (k + 1) * HEAD]
    return total


def to_row(folded):
    return jnp.sum(folded.T, axis=0, keepdims=True)


def to_column(row):
    return jnp.broadcast_to(row, (HEAD, row.shape[1])).T


def wide(column, width):
    return jnp.concatenate([column] * (width // HEAD), axis=1)


def tail_kernel(
    dkv_ref, half_ref, ffn_ref, kv_ref, res_ref, kv_gain, ffn_gain, wk_ref, wv_ref, wg_ref, wu_ref, wd_ref,
    input_grad, key_grad, value_grad, gate_grad, up_grad, down_grad,
    shard, ffn_own, heads, ffn, kv_in, res, wk, wv, wg, wu, wd,
    act, gate, upper, hidden_t, inv_col, kv_scaled, kv_n, y_own, y_full, hidden_grad, acts,
    row_acc, final, acc16, zbuf16, near16, far16, zsend16, zrecv16,
    stat_send, stat_slots, zbuf, near, far, zsend, zrecv,
    load_sem, ss, sr, fs, fr, hs, hr, ys, yr, rs, rr, ts, tr,
):
    y, yp, ym, y2, z, zo = feat_place()
    rows, cols = y_own.shape
    width = ffn.shape[1]
    pair = 2 * cols
    half = ffn_own.shape[0]
    others = feat_others()
    loads = [
        pltpu.make_async_copy(src, dst, load_sem.at[i])
        for i, (src, dst) in enumerate(
            (
                (ffn_ref.at[pl.ds(half, half), :], ffn_own), (kv_ref, kv_in),
                (half_ref, ffn.at[pl.ds(0, half), :]), (wg_ref, wg), (wu_ref, wu),
                (wk_ref, wk), (wv_ref, wv), (res_ref, res), (wd_ref, wd),
            )
        )
    ]
    for load in loads:
        load.start()
    meet(others + blk_peers())
    offset = pl.multiple_of((y * 2 + z) * cols, cols)
    stat_wire = Wire(ts, tr)

    def share(k, row):
        stat_send[k] = jnp.broadcast_to(row, (8, rows))
        for i, peer in enumerate(others):
            stat_wire.send(7 * k + i, stat_send.at[k], stat_slots.at[k, i], peer)

    def total_of(k):
        total = stat_send[k]
        for i, peer in enumerate(others):
            stat_wire.got(7 * k + i, stat_slots.at[k, i], peer)
            total = total + stat_slots[k, i]
        return total[0:1, :]

    def group(ref, i):
        return ref[:, pl.ds(pl.multiple_of(i * pair, pair), pair)]

    def forward():
        loads[1].wait()
        floats = kv_in[...].astype(F32)
        share(0, to_row(fold(floats * floats)))
        yield
        loads[2].wait()
        squares = jnp.zeros((rows, HEAD), F32)
        for i in range(4):
            floats = ffn[:, i * pair : (i + 1) * pair].astype(F32)
            squares = squares + fold(floats * floats)
        inverse = lax.rsqrt(jnp.sum(squares, axis=-1, keepdims=True) / width + epsilon)
        inv_col[...] = jnp.broadcast_to(inverse, (rows, HEAD))
        gate[...] = jnp.zeros_like(gate)
        upper[...] = jnp.zeros_like(upper)
        yield
        for i in range(4):
            span = slice(i * pair, (i + 1) * pair)
            scaled = ffn[:, span].astype(F32) * wide(inv_col[...], pair) * ffn_gain[:, span]
            act[:, span] = scaled.astype(BF16)
            yield
            if i == 0:
                loads[3].wait()
                loads[4].wait()
            gate[...] += jnp.dot(act[:, span], wg[span, :], preferred_element_type=F32)
            yield
            upper[...] += jnp.dot(act[:, span], wu[span, :], preferred_element_type=F32)
            yield

    loads[0].wait()
    kv_sums = scatter16(Wire(ss, sr), dkv_ref, shard, acc16, zbuf16, near16, far16, zsend16, zrecv16)
    ffn_plan = gather8(Wire(fs, fr), ffn_own, ffn.at[pl.ds(half, half), :], half * 7 // 8)
    ahead = forward()
    next(kv_sums)
    next(ffn_plan)
    ffn[pl.ds(half, half), pl.ds(offset, cols)] = ffn_own[...]
    next(ahead)
    run_first(kv_sums, ffn_plan)
    plan = gather8(Wire(hs, hr), shard, heads, rows * 9 // 8)
    next(plan)
    heads[:, pl.ds(pl.multiple_of((y * 2 + z) * HEAD, HEAD), HEAD)] = shard[...]
    run_all(plan, chain(ffn_plan, ahead))

    for load in loads[5:]:
        load.wait()
    normed = contract_cols(heads[:rows, :], wk[...]) + contract_cols(heads[rows:, :], wv[...])
    gain = kv_gain[:, pl.ds(offset, cols)]
    scaled = gain * normed.astype(BF16).astype(F32)
    kv_scaled[...] = scaled
    kv_floats = kv_in[...].astype(F32)
    share(1, to_row(fold(scaled * kv_floats)))
    kv_inv = wide(to_column(lax.rsqrt(total_of(0) / width + epsilon)), cols)
    kv_hat = kv_in[...].astype(F32) * kv_inv
    kv_n[...] = (kv_hat * kv_gain[:, pl.ds(offset, cols)]).astype(BF16)
    key_grad[0] = contract_rows(kv_n[...], heads[:rows, :]).astype(BF16)
    mean = wide(to_column(total_of(1) / width), cols) * kv_inv
    y_own[...] = (res[...].astype(F32) + kv_inv * (kv_scaled[...] - kv_hat * mean)).astype(BF16)

    plan = gather8(Wire(ys, yr), y_own, y_full, rows * 9 // 16)
    next(plan)
    y_full[:, pl.ds(offset, cols)] = y_own[...]
    hidden_grad[...] = jnp.zeros_like(hidden_grad)

    def other_kv():
        value_grad[0] = contract_rows(kv_n[...], heads[rows:, :]).astype(BF16)
        yield
        hidden_t[...] = (gate[...] * jax.nn.sigmoid(gate[...]) * upper[...]).T.astype(BF16)
        yield
        value = gate[...]
        sigmoid = jax.nn.sigmoid(value)
        gate[...] = upper[...] * sigmoid * (1.0 + value * (1.0 - sigmoid))
        upper[...] = value * sigmoid

    def down(i):
        down_grad[0, :, pl.ds(pl.multiple_of(i * pair, pair), pair)] = jnp.dot(
            hidden_t[...], group(y_full, i), preferred_element_type=F32
        ).astype(BF16)

    def back(i):
        hidden_grad[...] += contract_cols(group(y_full, i), group(wd, i))

    filler = other_kv()
    for stage in plan:
        if stage is None:
            run_some(filler)
            continue
        i, is_last = stage
        back(i)
        if not is_last:
            down(i)

    value = hidden_grad[...]
    hidden = gate.shape[1]
    acts[:, :hidden] = (value * gate[...]).astype(BF16)
    acts[:, hidden:] = (value * upper[...]).astype(BF16)
    cut = near.shape[2]
    rest = rows - cut
    wire = Wire(rs, rr)

    def term(i, tz, first, size):
        return wd.at[pl.ds(first, size), pl.ds(pl.multiple_of(i * pair + tz * cols, cols), cols)]

    def ring(plane, tz, first, size):
        return Ring(
            wire,
            4 + plane * Ring.SIZE,
            [term(i, tz, first, size) for i in range(4)],
            (
                lambda ref: ref.at[pl.ds(0, size // 2), :],
                lambda ref: ref.at[pl.ds(size // 2, size // 2), :],
            ),
            [near.at[plane, k, pl.ds(0, size), :] for k in range(2)],
            [far.at[plane, k, pl.ds(0, size), :] for k in range(2)],
            {"kvh": yp},
            {"kvh": ym},
        )

    outer, inner, last = ring(0, zo, 0, cut), ring(1, z, 0, cut), ring(2, z, cut, rest)
    row_acc[...] = jnp.zeros_like(row_acc)
    for i, ty in enumerate((y2, yp, ym, y)):
        span = pl.ds(pl.multiple_of(ty * pair, pair), pair)
        value = contract_cols(acts[:, :hidden], wg[span, :]) + contract_cols(acts[:, hidden:], wu[span, :])
        wd[:, i * pair : (i + 1) * pair] = value.astype(BF16)
        wire.send(i, term(i, zo, cut, rest), zbuf.at[i], {"section": zo})
        for one in (outer, inner):
            (one.send_far, one.send_plus, one.send_minus, lambda: None)[i]()
        row_acc[...] += fold(value * ffn[:, span].astype(F32) * ffn_gain[:, span])
    share(2, to_row(row_acc[...] * inv_col[...]))

    def weights():
        for i in range(4):
            span = slice(i * pair, (i + 1) * pair)
            value = contract_rows(act[:, span], acts[:, :hidden])
            gate_grad[0, span, :] = value.astype(BF16)
            yield
            value = contract_rows(act[:, span], acts[:, hidden:])
            up_grad[0, span, :] = value.astype(BF16)
            yield
        down(y2)

    def blend(i):
        wire.got(i, zbuf.at[i], {"section": zo})
        ref = term(i, z, cut, rest)
        ref[...] = add(ref[...], zbuf[i]).astype(BF16)

    def sums():
        outer.relay_plus()
        outer.relay_minus()
        yield
        blend(0)
        last.send_far()
        inner.relay_plus()
        inner.relay_minus()
        yield
        blend(1)
        last.send_plus()
        blend(2)
        last.send_minus()
        yield
        zsend[...] = outer.collect().astype(BF16)
        wire.send(SCATTER8 - 1, zsend, zrecv, {"section": zo})
        yield
        last.relay_plus()
        last.relay_minus()
        yield
        blend(3)
        final[pl.ds(0, cut), :] = inner.collect()
        yield
        final[pl.ds(cut, rest), :] = last.collect()
        yield
        wire.got(SCATTER8 - 1, zrecv, {"section": zo})
        final[pl.ds(0, cut), :] += zrecv[...].astype(F32)

    run_all(weights(), sums())
    inverse = wide(inv_col[...], cols)
    correction = wide(to_column(total_of(2) / width), cols)
    hat = ffn[:, pl.ds(offset, cols)].astype(F32) * inverse
    input_grad[...] = (
        y_own[...].astype(F32)
        + inverse * (ffn_gain[:, pl.ds(offset, cols)] * final[...] - hat * correction)
    ).astype(BF16)
    wire.finish()
    stat_wire.finish()


def tail(dkv, ffn_half, ffn_input, kv_input, residual, kv_gain, ffn_gain, w_key, w_value, w_gate, w_up, w_down):
    rows, cols = kv_input.shape
    width, hidden = w_gate.shape
    cut = rows * 9 // 16
    rest = rows - cut
    kv_cut = rows * 3 // 4
    any_space = pl.BlockSpec(memory_space=pl.ANY)
    in_vmem = pl.BlockSpec(memory_space=VMEM)
    dma = pltpu.SemaphoreType.DMA
    heads = w_key.shape[1]
    return pl.pallas_call(
        tail_kernel,
        name="tail",
        out_shape=(
            VMEM((rows, cols), BF16),
            VMEM((1, cols, heads), BF16),
            VMEM((1, cols, heads), BF16),
            VMEM((1, width, hidden), BF16),
            VMEM((1, width, hidden), BF16),
            VMEM((1, hidden, width), BF16),
        ),
        in_specs=[in_vmem] * 2 + [any_space] * 3 + [in_vmem] * 2 + [any_space] * 5,
        out_specs=(in_vmem,) * 6,
        scratch_shapes=[
            VMEM((2 * rows, HEAD), BF16),
            VMEM((rows // 2, cols), BF16),
            VMEM((2 * rows, heads), BF16),
            VMEM((rows, width), BF16),
            VMEM((rows, cols), BF16),
            VMEM((rows, cols), BF16),
            VMEM((cols, heads), BF16),
            VMEM((cols, heads), BF16),
            VMEM((width, hidden), BF16),
            VMEM((width, hidden), BF16),
            VMEM((hidden, width), BF16),
            VMEM((rows, width), BF16),
            VMEM((rows, hidden), F32),
            VMEM((rows, hidden), F32),
            VMEM((hidden, rows), BF16),
            VMEM((rows, HEAD), F32),
            VMEM((rows, cols), F32),
            VMEM((rows, cols), BF16),
            VMEM((rows, cols), BF16),
            VMEM((rows, width), BF16),
            VMEM((rows, hidden), F32),
            VMEM((rows, 2 * hidden), BF16),
            VMEM((rows, HEAD), F32),
            VMEM((rows, cols), F32),
            VMEM((2, 4, 2, rows, HEAD), BF16),
            VMEM((4, 2, rows - kv_cut, HEAD), BF16),
            VMEM((3, 2, 2, kv_cut, HEAD), BF16),
            VMEM((3, 2, 2, kv_cut, HEAD), BF16),
            VMEM((2, kv_cut, HEAD), BF16),
            VMEM((2, kv_cut, HEAD), BF16),
            VMEM((3, 8, rows), F32),
            VMEM((3, 7, 8, rows), F32),
            VMEM((4, rest, cols), BF16),
            VMEM((3, 2, cut, cols), BF16),
            VMEM((3, 2, cut, cols), BF16),
            VMEM((cut, cols), BF16),
            VMEM((cut, cols), BF16),
            dma((9,)), dma((SCATTER16,)), dma((SCATTER16,)), dma((GATHER8,)), dma((GATHER8,)),
            dma((GATHER8,)), dma((GATHER8,)), dma((GATHER8,)), dma((GATHER8,)),
            dma((SCATTER8,)), dma((SCATTER8,)), dma((21,)), dma((21,)),
        ],
        compiler_params=pltpu.CompilerParams(
            collective_id=3, has_side_effects=True, vmem_limit_bytes=44_000_000
        ),
    )(
        pltpu.with_memory_space_constraint(dkv, VMEM),
        pltpu.with_memory_space_constraint(ffn_half, VMEM),
        ffn_input, kv_input, residual, kv_gain.reshape(1, -1), ffn_gain.reshape(1, -1),
        w_key, w_value, w_gate, w_up, w_down,
    )


MASKED = -1e30
START = -1e29


def attention_kernel(
    bound_ref, seen_ref, q_ref, g_ref, kv_ref, dq_ref, dkv_ref,
    q_cat, g_cat, q_t, g_t, run_max, run_sum, run_dot, dq_t, p_all, d_all, *, tile, scale
):
    rows = q_ref.shape[0]
    group = q_ref.shape[1] // HEAD
    own = lax.axis_index(BLK)
    lowest = bound_ref[0]
    to_log2 = scale * LOG2E
    for h in range(group):
        for src, cat, turned in ((q_ref, q_cat, q_t), (g_ref, g_cat, g_t)):
            block = src[:, h * HEAD : (h + 1) * HEAD]
            cat[h * rows : (h + 1) * rows, :] = block
            turned[:, h * rows : (h + 1) * rows] = block.astype(F32).T.astype(BF16)
    run_max[...] = jnp.full_like(run_max, START)
    run_sum[...] = jnp.zeros_like(run_sum)
    run_dot[...] = jnp.zeros_like(run_dot)
    dq_t[...] = jnp.zeros_like(dq_t)

    tiles = dkv_ref.shape[1] // tile
    first = lowest // tile
    last = ((own + 1) * rows) // tile
    whole_to = (own * rows) // tile
    whole_from = jnp.minimum((lowest + tile - 1) // tile, whole_to)

    def part(j):
        return pl.ds(pl.multiple_of(j * tile, tile), tile)

    def lanes(h):
        return pl.ds(h * rows, rows)

    def scores(j, h, masked):
        keys = kv_ref[0, part(j), :]
        value = jnp.dot(keys, q_t[:, lanes(h)], preferred_element_type=F32) * to_log2
        if masked:
            key_pos = j * tile + lax.broadcasted_iota(jnp.int32, (tile, rows), 0)
            query_pos = own * rows + lax.broadcasted_iota(jnp.int32, (tile, rows), 1)
            visible = (key_pos <= query_pos) & (key_pos >= seen_ref[...])
            value = jnp.where(visible, value, MASKED)
        return value

    def unseen(j, row, masked):
        return row if masked else jnp.where(seen_ref[...] > j * tile, -MASKED, row)

    def products(j, h):
        return jnp.dot(kv_ref[1, part(j), :], g_t[:, lanes(h)], preferred_element_type=F32)

    def stats(j, masked):
        for h in range(group):
            value = scores(j, h, masked).reshape(tile // 8, 8, rows)
            dprobs = products(j, h).reshape(tile // 8, 8, rows)
            before = run_max[:, lanes(h)]
            now = jnp.maximum(before, jnp.max(value, axis=0))
            if not masked:
                now = jnp.where(seen_ref[...] > j * tile, before, now)
            shrink = jnp.exp2(before - now)
            probs = jnp.exp2(value - unseen(j, now, masked)[None])
            run_max[:, lanes(h)] = now
            run_sum[:, lanes(h)] = run_sum[:, lanes(h)] * shrink + jnp.sum(probs, axis=0)
            run_dot[:, lanes(h)] = run_dot[:, lanes(h)] * shrink + jnp.sum(probs * dprobs, axis=0)

    def grads(j, masked):
        keys = kv_ref[0, part(j), :]
        for h in range(group):
            value = scores(j, h, masked)
            probs = jnp.exp2(value - unseen(j, run_max[0:1, lanes(h)], masked))
            p_all[:, lanes(h)] = probs.astype(BF16)
            d_all[:, lanes(h)] = (probs * (products(j, h) - run_dot[0:1, lanes(h)])).astype(BF16)
        dkv_ref[1, part(j), :] = jnp.dot(p_all[...], g_cat[...], preferred_element_type=F32).astype(BF16)
        dkv_ref[0, part(j), :] = (
            jnp.dot(d_all[...], q_cat[...], preferred_element_type=F32) * scale
        ).astype(BF16)
        dq_t[...] += contract_rows(keys, d_all[...])

    def sweep(body):
        lax.fori_loop(first, whole_from, lambda j, _: (body(j, True), 0)[1], 0)
        lax.fori_loop(jnp.maximum(whole_from, first), whole_to, lambda j, _: (body(j, False), 0)[1], 0)
        lax.fori_loop(jnp.maximum(whole_to, first), last, lambda j, _: (body(j, True), 0)[1], 0)

    sweep(stats)
    peak = jnp.max(run_max[...], axis=0, keepdims=True)
    factor = jnp.exp2(run_max[...] - peak)
    total = jnp.sum(run_sum[...] * factor, axis=0, keepdims=True)
    delta = jnp.sum(run_dot[...] * factor, axis=0, keepdims=True) / total
    run_max[0:1, :] = peak + jnp.log(total) * LOG2E
    run_dot[0:1, :] = delta

    def clear(j, _):
        dkv_ref[:, part(j), :] = jnp.zeros((2, tile, HEAD), BF16)
        return 0

    lax.fori_loop(0, first, clear, 0)
    lax.fori_loop(last, tiles, clear, 0)
    sweep(grads)
    for h in range(group):
        dq_ref[:, h * HEAD : (h + 1) * HEAD] = (dq_t[:, lanes(h)] * scale).T.astype(BF16)


def attention(query, out_grad, kv, visible_from, tile=512):
    rows, width = query.shape
    group = width // HEAD
    cat = VMEM((group * rows, HEAD), BF16)
    turned = VMEM((HEAD, group * rows), BF16)
    stat = VMEM((8, group * rows), F32)
    return pl.pallas_call(
        functools.partial(attention_kernel, tile=tile, scale=1.0 / math.sqrt(HEAD)),
        name="attention",
        out_shape=(
            jax.ShapeDtypeStruct((rows, width), BF16),
            VMEM(kv.shape, BF16),
        ),
        in_specs=[pl.BlockSpec(memory_space=pltpu.SMEM)] + [pl.BlockSpec(memory_space=VMEM)] * 4,
        out_specs=(pl.BlockSpec(memory_space=VMEM),) * 2,
        scratch_shapes=[
            cat, cat, turned, turned, stat, stat, stat, VMEM((HEAD, group * rows), F32),
            VMEM((tile, group * rows), BF16), VMEM((tile, group * rows), BF16),
        ],
        compiler_params=pltpu.CompilerParams(vmem_limit_bytes=55_800_000),
    )(
        visible_from, visible_from.reshape(1, rows), query, out_grad,
        pltpu.with_memory_space_constraint(kv, VMEM),
    )


def write_kernel(*refs):
    count = len(refs) // 2
    sem = refs[-1]
    copies = []
    for k in range(count):
        src, dst = refs[k], refs[count + k]
        rows = src.shape[-2]
        for piece in range(2):
            span = pl.ds(piece * rows // 2, rows // 2)
            at = (span,) if len(src.shape) == 2 else (0, span)
            copies.append(pltpu.make_async_copy(src.at[at], dst.at[at], sem.at[2 * k + piece]))
    for copy in copies:
        copy.start()
    for copy in copies:
        copy.wait()


def write_out(arrays):
    return pl.pallas_call(
        write_kernel,
        name="write_out",
        out_shape=tuple(jax.ShapeDtypeStruct(a.shape, a.dtype) for a in arrays),
        in_specs=[pl.BlockSpec(memory_space=VMEM)] * len(arrays),
        out_specs=(pl.BlockSpec(memory_space=pl.ANY),) * len(arrays),
        scratch_shapes=[pltpu.SemaphoreType.DMA((2 * len(arrays),))],
        compiler_params=pltpu.CompilerParams(vmem_limit_bytes=8_000_000),
    )(*[pltpu.with_memory_space_constraint(a, VMEM) for a in arrays])


def on_device(
    query, keys, values, out_grad, visible_from, kv_input, residual_grad, ffn_input,
    kv_gain, ffn_gain, w_key, w_value, w_gate, w_up, w_down,
):
    rows = query.shape[0]
    every, ffn_half = gather_first(keys, values, ffn_input)
    blocks = every.shape[1]
    query_grad, dkv = attention(query, out_grad, every.reshape(2, blocks * rows, HEAD), visible_from)
    rest = tail(
        dkv.reshape(2, blocks, rows, HEAD), ffn_half, ffn_input, kv_input, residual_grad, kv_gain, ffn_gain,
        w_key, w_value, w_gate, w_up, w_down,
    )
    return (query_grad, *write_out(rest))


def solution(mesh):
    finer = Mesh(
        mesh.devices.reshape(4, 2, 2, mesh.shape["kvh"], mesh.shape["section"]),
        (*BLK, *FEAT),
    )
    tokens = P(BLK, FEAT)
    placed = (
        tokens, tokens, tokens, tokens, P(BLK), tokens, tokens, tokens, P(), P(),
        P(FEAT, None), P(FEAT, None), P(None, FEAT), P(None, FEAT), P(FEAT, None),
    )
    return jax.shard_map(
        on_device,
        mesh=finer,
        in_specs=placed,
        out_specs=(
            tokens,
            tokens,
            P(BLK, FEAT, None),
            P(BLK, FEAT, None),
            P(BLK, None, FEAT),
            P(BLK, None, FEAT),
            P(BLK, FEAT, None),
        ),
        check_vma=False,
    )
```

```python
import functools
import math

import jax
import jax.numpy as jnp
from jax import lax
from jax.experimental import pallas as pl
from jax.experimental.pallas import tpu as pltpu
from jax.sharding import Mesh
from jax.sharding import PartitionSpec as P

HEAD = 128
BLK = ("bx", "bz", "bc")
FEAT = ("kvh", "section")
MESH = pl.DeviceIdType.MESH
LOG2E = 1.4426950408889634
VMEM = pltpu.VMEM
F32 = jnp.float32
BF16 = jnp.bfloat16

epsilon = 1e-06


def contract_rows(left, right):
    return lax.dot_general(left, right, (((0,), (0,)), ((), ())), preferred_element_type=F32)


def contract_cols(left, right):
    return lax.dot_general(left, right, (((1,), (1,)), ((), ())), preferred_element_type=F32)


def run_all(*plans):
    live = list(plans)
    while live:
        for plan in list(live):
            try:
                next(plan)
            except StopIteration:
                live.remove(plan)


def run_some(plan):
    try:
        next(plan)
    except StopIteration:
        pass


def run_first(main, *others):
    for _ in main:
        for other in others:
            run_some(other)


def chain(*plans):
    for plan in plans:
        yield from plan


def meet(peers):
    barrier = pltpu.get_barrier_semaphore()
    for peer in peers:
        pl.semaphore_signal(barrier, inc=1, device_id=peer, device_id_type=MESH)
    pl.semaphore_wait(barrier, len(peers))


class Wire:
    def __init__(self, send_sem, recv_sem):
        self.send_sem, self.recv_sem, self.sent = send_sem, recv_sem, []

    def send(self, i, src, dst, peer):
        copy = pltpu.make_async_remote_copy(
            src_ref=src,
            dst_ref=dst,
            send_sem=self.send_sem.at[i],
            recv_sem=self.recv_sem.at[i],
            device_id=peer,
            device_id_type=MESH,
        )
        copy.start()
        self.sent.append(copy)

    def got(self, i, dst, peer):
        pltpu.make_async_remote_copy(
            src_ref=dst,
            dst_ref=dst,
            send_sem=self.send_sem.at[i],
            recv_sem=self.recv_sem.at[i],
            device_id=peer,
            device_id_type=MESH,
        ).wait_recv()

    def finish(self):
        for copy in self.sent:
            copy.wait_send()


def feat_place():
    y, z = lax.axis_index("kvh"), lax.axis_index("section")
    return y, lax.rem(y + 1, 4), lax.rem(y + 3, 4), lax.rem(y + 2, 4), z, 1 - z


def feat_peers():
    y, yp, ym, y2, z, zo = feat_place()
    return [{"kvh": yp}, {"kvh": ym}, {"section": zo}]


def feat_others():
    y, yp, ym, y2, z, zo = feat_place()
    others = [{"section": zo}]
    for other in (yp, ym, y2):
        others.append({"kvh": other})
        others.append({"kvh": other, "section": zo})
    return others


def blk_place():
    x, z, c = lax.axis_index("bx"), lax.axis_index("bz"), lax.axis_index("bc")
    return x, lax.rem(x + 1, 4), lax.rem(x + 3, 4), lax.rem(x + 2, 4), z, 1 - z, c, 1 - c


def blk_peers():
    x, xp, xm, x2, z, zo, c, co = blk_place()
    return [{"bx": xp}, {"bx": xm}, {"bz": zo}, {"bc": co}]


GATHER8 = 18


def tree(place, rows, cut, own, on, got):
    y, yp, ym, y2, z, zo = place
    rest = rows - cut
    full_a, low_a, high_a = (0, cut), (0, cut // 2), (cut // 2, cut // 2)
    full_b, low_b, high_b = (cut, rest), (cut, rest // 2), (cut + rest // 2, rest // 2)
    own(0, full_a, "o")
    own(1, full_a, "p")
    own(2, full_a, "m")
    own(3, full_b, "p")
    own(4, full_b, "m")
    own(5, full_b, "o")
    yield
    got(0, y, zo, full_a)
    on(6, y, zo, full_a, "p")
    on(7, y, zo, full_a, "m")
    yield
    got(1, ym, z, full_a)
    on(8, ym, z, low_a, "p")
    yield
    got(2, yp, z, full_a)
    on(9, yp, z, high_a, "m")
    yield
    got(3, ym, z, full_b)
    on(10, ym, z, low_b, "p")
    on(12, ym, z, full_b, "o")
    yield
    got(4, yp, z, full_b)
    on(11, yp, z, high_b, "m")
    on(13, yp, z, full_b, "o")
    yield
    got(5, y, zo, full_b)
    yield y, False
    got(6, ym, zo, full_a)
    on(14, ym, zo, low_a, "p")
    yield
    got(7, yp, zo, full_a)
    on(15, yp, zo, high_a, "m")
    yield
    got(10, y2, z, low_b)
    on(16, y2, z, low_b, "o")
    yield
    got(11, y2, z, high_b)
    on(17, y2, z, high_b, "o")
    yield
    got(12, ym, zo, full_b)
    yield ym, False
    got(13, yp, zo, full_b)
    yield yp, False
    got(8, y2, z, low_a)
    got(9, y2, z, high_a)
    got(14, y2, zo, low_a)
    got(15, y2, zo, high_a)
    got(16, y2, zo, low_b)
    got(17, y2, zo, high_b)
    yield y2, True


def gather8(wire, x_ref, out_ref, cut):
    place = y, yp, ym, y2, z, zo = feat_place()
    rows, cols = x_ref.shape
    peers = {"p": {"kvh": yp}, "m": {"kvh": ym}, "o": {"section": zo}}

    def at(sy, sz, part):
        start = pl.multiple_of((sy * 2 + sz) * cols, cols)
        return out_ref.at[pl.ds(part[0], part[1]), pl.ds(start, cols)]

    def own(i, part, way):
        wire.send(i, x_ref.at[pl.ds(part[0], part[1]), :], at(y, z, part), peers[way])

    def on(i, sy, sz, part, way):
        wire.send(i, at(sy, sz, part), at(sy, sz, part), peers[way])

    def got(i, sy, sz, part):
        wire.got(i, at(sy, sz, part), peers["o"])

    for stage in tree(place, rows, cut, own, on, got):
        if stage is not None and stage[1]:
            wire.finish()
        yield stage


GATHER16 = 2 * GATHER8 + 1


def gather16(wire, kv_ref, out_ref, cut):
    x, xp, xm, x2, z, zo, c, co = blk_place()
    rows = kv_ref.shape[1]
    peers = {"p": {"bx": xp}, "m": {"bx": xm}, "o": {"bz": zo}}
    twin = {"bc": co}
    arrived = []

    def at(sx, sz, part, sc):
        return out_ref.at[:, sx * 4 + sz * 2 + sc, pl.ds(part[0], part[1]), :]

    def own(i, part, way):
        wire.send(i, kv_ref.at[:, pl.ds(part[0], part[1]), :], at(x, z, part, c), peers[way])

    def on(i, sx, sz, part, way):
        wire.send(i, at(sx, sz, part, c), at(sx, sz, part, c), peers[way])

    def got(i, sx, sz, part):
        wire.got(i, at(sx, sz, part, c), peers["o"])
        wire.send(GATHER8 + i, at(sx, sz, part, c), at(sx, sz, part, c), twin)
        arrived.append((GATHER8 + i, sx, sz, part))

    first = True
    for _ in tree((x, xp, xm, x2, z, zo), rows, cut, own, on, got):
        if first:
            wire.send(2 * GATHER8, kv_ref, at(x, z, (0, rows), c), twin)
            arrived.append((2 * GATHER8, x, z, (0, rows)))
            first = False
        yield
    for i, sx, sz, part in arrived:
        wire.got(i, at(sx, sz, part, co), twin)
    wire.finish()


def first_kernel(key_ref, value_ref, ffn_ref, kv_out, ffn_out, own, own_ffn, s0, r0, s1, r1, local):
    x, xp, xm, x2, z, zo, c, co = blk_place()
    y, yp, ym, y2, sz, szo = feat_place()
    rows, cols = own_ffn.shape
    loads = [
        pltpu.make_async_copy(key_ref, own.at[0], local.at[0]),
        pltpu.make_async_copy(value_ref, own.at[1], local.at[1]),
        pltpu.make_async_copy(ffn_ref.at[pl.ds(0, rows), :], own_ffn, local.at[2]),
    ]
    for load in loads:
        load.start()
    meet(blk_peers() + feat_peers())
    for load in loads:
        load.wait()
    keeps = [
        pltpu.make_async_copy(own, kv_out.at[:, x * 4 + z * 2 + c], local.at[3]),
        pltpu.make_async_copy(
            own_ffn,
            ffn_out.at[:, pl.ds(pl.multiple_of((y * 2 + sz) * cols, cols), cols)],
            local.at[4],
        ),
    ]
    kv_plan = gather16(Wire(s0, r0), own, kv_out, own.shape[1] * 7 // 8)
    ffn_plan = gather8(Wire(s1, r1), own_ffn, ffn_out, rows // 2)
    next(kv_plan)
    next(ffn_plan)
    for keep in keeps:
        keep.start()
    run_all(kv_plan, ffn_plan)
    for keep in keeps:
        keep.wait()


def gather_first(keys, values, ffn):
    rows, width = keys.shape
    half, cols = ffn.shape[0] // 2, ffn.shape[1]
    dma = pltpu.SemaphoreType.DMA
    return pl.pallas_call(
        first_kernel,
        name="gather_first",
        out_shape=(
            VMEM((2, 16, rows, width), keys.dtype),
            VMEM((half, 8 * cols), ffn.dtype),
        ),
        in_specs=[pl.BlockSpec(memory_space=pltpu.HBM)] * 3,
        out_specs=(pl.BlockSpec(memory_space=VMEM),) * 2,
        scratch_shapes=[
            VMEM((2, rows, width), keys.dtype),
            VMEM((half, cols), ffn.dtype),
            dma((GATHER16,)), dma((GATHER16,)), dma((GATHER8,)), dma((GATHER8,)), dma((5,)),
        ],
        compiler_params=pltpu.CompilerParams(
            collective_id=1, has_side_effects=True, vmem_limit_bytes=16_000_000
        ),
    )(*[pltpu.with_memory_space_constraint(a, pltpu.HBM) for a in (keys, values, ffn)])


def add(*terms):
    total = terms[0].astype(F32)
    for term in terms[1:]:
        total = total + term.astype(F32)
    return total


class Ring:
    SIZE = 6

    def __init__(self, wire, first, terms, halves, near, far, p, m):
        self.wire, self.first, self.p, self.m = wire, first, p, m
        self.far, self.plus, self.minus, self.own = terms
        self.low, self.high = halves
        self.near_p, self.near_m = near
        self.far_p, self.far_m = far

    def send_far(self):
        self.wire.send(self.first, self.high(self.far), self.high(self.far_m), self.p)
        self.wire.send(self.first + 1, self.low(self.far), self.low(self.far_p), self.m)

    def send_plus(self):
        self.wire.send(self.first + 2, self.low(self.plus), self.low(self.near_m), self.p)

    def send_minus(self):
        self.wire.send(self.first + 3, self.high(self.minus), self.high(self.near_p), self.m)

    def relay_plus(self):
        self.wire.got(self.first, self.high(self.far_m), self.p)
        ref = self.high(self.plus)
        ref[...] = add(ref[...], self.high(self.far_m)[...]).astype(BF16)
        self.wire.send(self.first + 4, ref, self.high(self.near_m), self.p)

    def relay_minus(self):
        self.wire.got(self.first + 1, self.low(self.far_p), self.p)
        ref = self.low(self.minus)
        ref[...] = add(ref[...], self.low(self.far_p)[...]).astype(BF16)
        self.wire.send(self.first + 5, ref, self.low(self.near_p), self.m)

    def collect(self):
        self.wire.got(self.first + 2, self.low(self.near_m), self.p)
        self.wire.got(self.first + 3, self.high(self.near_p), self.p)
        self.wire.got(self.first + 4, self.high(self.near_m), self.p)
        self.wire.got(self.first + 5, self.low(self.near_p), self.p)
        return add(self.own[...], self.near_p[...], self.near_m[...])


SCATTER16 = 8 + 4 + 3 * Ring.SIZE + 1


def scatter16(wire, part_ref, out_ref, acc, zbuf, near, far, zsend, zrecv):
    x, xp, xm, x2, z, zo, c, co = blk_place()
    rows = part_ref.shape[2]
    rest = zbuf.shape[2]
    cut = rows - rest
    across = {"bz": zo}
    turn = (x2, xp, xm, x)
    for p, tz in enumerate((zo, z)):
        for i, tx in enumerate(turn):
            wire.send(4 * p + i, part_ref.at[:, tx * 4 + tz * 2 + co], acc.at[p, i], {"bc": co})

    def merge(p, i):
        wire.got(4 * p + i, acc.at[p, i], {"bc": co})
        mine = part_ref[:, turn[i] * 4 + (zo, z)[p] * 2 + c]
        acc[p, i] = add(mine, acc[p, i]).astype(BF16)

    def term(p, i, first, size):
        return acc.at[p, i, :, pl.ds(first, size), :]

    def ring(k, p, first, size):
        return Ring(
            wire,
            12 + k * Ring.SIZE,
            [term(p, i, first, size) for i in range(4)],
            (
                lambda ref: ref.at[:, pl.ds(0, size // 2), :],
                lambda ref: ref.at[:, pl.ds(size // 2, size // 2), :],
            ),
            [near.at[k, n, :, pl.ds(0, size), :] for n in range(2)],
            [far.at[k, n, :, pl.ds(0, size), :] for n in range(2)],
            {"bx": xp},
            {"bx": xm},
        )

    outer, inner, last = ring(0, 0, 0, cut), ring(1, 1, 0, cut), ring(2, 1, cut, rest)

    def blend(i):
        wire.got(8 + i, zbuf.at[i], across)
        ref = term(1, i, cut, rest)
        ref[...] = add(ref[...], zbuf[i]).astype(BF16)

    def put(first, total):
        size = total.shape[1]
        out_ref[pl.ds(first, size), :] = total[0].astype(BF16)
        out_ref[pl.ds(rows + first, size), :] = total[1].astype(BF16)

    yield
    for p, one in enumerate((outer, inner)):
        for i in range(4):
            merge(p, i)
            if p == 0:
                wire.send(8 + i, term(0, i, cut, rest), zbuf.at[i], across)
            (one.send_far, one.send_plus, one.send_minus, lambda: None)[i]()
            yield
        if p == 0:
            outer.relay_plus()
            outer.relay_minus()
            yield
    blend(0)
    last.send_far()
    yield
    inner.relay_plus()
    inner.relay_minus()
    yield
    blend(1)
    last.send_plus()
    blend(2)
    last.send_minus()
    yield
    zsend[...] = outer.collect().astype(BF16)
    wire.send(SCATTER16 - 1, zsend, zrecv, across)
    yield
    last.relay_plus()
    last.relay_minus()
    yield
    blend(3)
    total = inner.collect()
    yield
    put(cut, last.collect())
    yield
    wire.got(SCATTER16 - 1, zrecv, across)
    put(0, total + zrecv[...].astype(F32))
    wire.finish()


SCATTER8 = 4 + 3 * Ring.SIZE + 1


def fold(value):
    total = value[:, :HEAD]
    for k in range(1, value.shape[1] // HEAD):
        total = total + value[:, k * HEAD : (k + 1) * HEAD]
    return total


def to_row(folded):
    return jnp.sum(folded.T, axis=0, keepdims=True)


def to_column(row):
    return jnp.broadcast_to(row, (HEAD, row.shape[1])).T


def wide(column, width):
    return jnp.concatenate([column] * (width // HEAD), axis=1)


def tail_kernel(
    dkv_ref, half_ref, ffn_ref, kv_ref, res_ref, kv_gain, ffn_gain, wk_ref, wv_ref, wg_ref, wu_ref, wd_ref,
    input_grad, key_grad, value_grad, gate_grad, up_grad, down_grad,
    shard, ffn_own, heads, ffn, kv_in, res, wk, wv, wg, wu, wd,
    act, gate, upper, hidden_t, inv_col, kv_scaled, kv_n, y_own, y_full, hidden_grad, acts,
    row_acc, final, acc16, zbuf16, near16, far16, zsend16, zrecv16,
    stat_send, stat_slots, zbuf, near, far, zsend, zrecv,
    load_sem, ss, sr, fs, fr, hs, hr, ys, yr, rs, rr, ts, tr,
):
    y, yp, ym, y2, z, zo = feat_place()
    rows, cols = y_own.shape
    width = ffn.shape[1]
    pair = 2 * cols
    half = ffn_own.shape[0]
    others = feat_others()
    loads = [
        pltpu.make_async_copy(src, dst, load_sem.at[i])
        for i, (src, dst) in enumerate(
            (
                (ffn_ref.at[pl.ds(half, half), :], ffn_own), (kv_ref, kv_in),
                (half_ref, ffn.at[pl.ds(0, half), :]), (wg_ref, wg), (wu_ref, wu),
                (wk_ref, wk), (wv_ref, wv), (res_ref, res), (wd_ref, wd),
            )
        )
    ]
    for load in loads:
        load.start()
    meet(others + blk_peers())
    offset = pl.multiple_of((y * 2 + z) * cols, cols)
    stat_wire = Wire(ts, tr)

    def share(k, row):
        stat_send[k] = jnp.broadcast_to(row, (8, rows))
        for i, peer in enumerate(others):
            stat_wire.send(7 * k + i, stat_send.at[k], stat_slots.at[k, i], peer)

    def total_of(k):
        total = stat_send[k]
        for i, peer in enumerate(others):
            stat_wire.got(7 * k + i, stat_slots.at[k, i], peer)
            total = total + stat_slots[k, i]
        return total[0:1, :]

    def group(ref, i):
        return ref[:, pl.ds(pl.multiple_of(i * pair, pair), pair)]

    def forward():
        loads[1].wait()
        floats = kv_in[...].astype(F32)
        share(0, to_row(fold(floats * floats)))
        yield
        loads[2].wait()
        squares = jnp.zeros((rows, HEAD), F32)
        for i in range(4):
            floats = ffn[:, i * pair : (i + 1) * pair].astype(F32)
            squares = squares + fold(floats * floats)
        inverse = lax.rsqrt(jnp.sum(squares, axis=-1, keepdims=True) / width + epsilon)
        inv_col[...] = jnp.broadcast_to(inverse, (rows, HEAD))
        gate[...] = jnp.zeros_like(gate)
        upper[...] = jnp.zeros_like(upper)
        yield
        for i in range(4):
            span = slice(i * pair, (i + 1) * pair)
            scaled = ffn[:, span].astype(F32) * wide(inv_col[...], pair) * ffn_gain[:, span]
            act[:, span] = scaled.astype(BF16)
            yield
            if i == 0:
                loads[3].wait()
                loads[4].wait()
            gate[...] += jnp.dot(act[:, span], wg[span, :], preferred_element_type=F32)
            yield
            upper[...] += jnp.dot(act[:, span], wu[span, :], preferred_element_type=F32)
            yield

    loads[0].wait()
    kv_sums = scatter16(Wire(ss, sr), dkv_ref, shard, acc16, zbuf16, near16, far16, zsend16, zrecv16)
    ffn_plan = gather8(Wire(fs, fr), ffn_own, ffn.at[pl.ds(half, half), :], half * 7 // 8)
    ahead = forward()
    next(kv_sums)
    next(ffn_plan)
    ffn[pl.ds(half, half), pl.ds(offset, cols)] = ffn_own[...]
    next(ahead)
    run_first(kv_sums, ffn_plan)
    plan = gather8(Wire(hs, hr), shard, heads, rows * 9 // 8)
    next(plan)
    heads[:, pl.ds(pl.multiple_of((y * 2 + z) * HEAD, HEAD), HEAD)] = shard[...]
    run_all(plan, chain(ffn_plan, ahead))

    for load in loads[5:]:
        load.wait()
    normed = contract_cols(heads[:rows, :], wk[...]) + contract_cols(heads[rows:, :], wv[...])
    gain = kv_gain[:, pl.ds(offset, cols)]
    scaled = gain * normed.astype(BF16).astype(F32)
    kv_scaled[...] = scaled
    kv_floats = kv_in[...].astype(F32)
    share(1, to_row(fold(scaled * kv_floats)))
    kv_inv = wide(to_column(lax.rsqrt(total_of(0) / width + epsilon)), cols)
    kv_hat = kv_in[...].astype(F32) * kv_inv
    kv_n[...] = (kv_hat * kv_gain[:, pl.ds(offset, cols)]).astype(BF16)
    key_grad[0] = contract_rows(kv_n[...], heads[:rows, :]).astype(BF16)
    mean = wide(to_column(total_of(1) / width), cols) * kv_inv
    y_own[...] = (res[...].astype(F32) + kv_inv * (kv_scaled[...] - kv_hat * mean)).astype(BF16)

    plan = gather8(Wire(ys, yr), y_own, y_full, rows * 9 // 16)
    next(plan)
    y_full[:, pl.ds(offset, cols)] = y_own[...]
    hidden_grad[...] = jnp.zeros_like(hidden_grad)

    def other_kv():
        value_grad[0] = contract_rows(kv_n[...], heads[rows:, :]).astype(BF16)
        yield
        hidden_t[...] = (gate[...] * jax.nn.sigmoid(gate[...]) * upper[...]).T.astype(BF16)
        yield
        value = gate[...]
        sigmoid = jax.nn.sigmoid(value)
        gate[...] = upper[...] * sigmoid * (1.0 + value * (1.0 - sigmoid))
        upper[...] = value * sigmoid

    def down(i):
        down_grad[0, :, pl.ds(pl.multiple_of(i * pair, pair), pair)] = jnp.dot(
            hidden_t[...], group(y_full, i), preferred_element_type=F32
        ).astype(BF16)

    def back(i):
        hidden_grad[...] += contract_cols(group(y_full, i), group(wd, i))

    filler = other_kv()
    for stage in plan:
        if stage is None:
            run_some(filler)
            continue
        i, is_last = stage
        back(i)
        if not is_last:
            down(i)

    value = hidden_grad[...]
    hidden = gate.shape[1]
    acts[:, :hidden] = (value * gate[...]).astype(BF16)
    acts[:, hidden:] = (value * upper[...]).astype(BF16)
    cut = near.shape[2]
    rest = rows - cut
    wire = Wire(rs, rr)

    def term(i, tz, first, size):
        return wd.at[pl.ds(first, size), pl.ds(pl.multiple_of(i * pair + tz * cols, cols), cols)]

    def ring(plane, tz, first, size):
        return Ring(
            wire,
            4 + plane * Ring.SIZE,
            [term(i, tz, first, size) for i in range(4)],
            (
                lambda ref: ref.at[pl.ds(0, size // 2), :],
                lambda ref: ref.at[pl.ds(size // 2, size // 2), :],
            ),
            [near.at[plane, k, pl.ds(0, size), :] for k in range(2)],
            [far.at[plane, k, pl.ds(0, size), :] for k in range(2)],
            {"kvh": yp},
            {"kvh": ym},
        )

    outer, inner, last = ring(0, zo, 0, cut), ring(1, z, 0, cut), ring(2, z, cut, rest)
    row_acc[...] = jnp.zeros_like(row_acc)
    for i, ty in enumerate((y2, yp, ym, y)):
        span = pl.ds(pl.multiple_of(ty * pair, pair), pair)
        value = contract_cols(acts[:, :hidden], wg[span, :]) + contract_cols(acts[:, hidden:], wu[span, :])
        wd[:, i * pair : (i + 1) * pair] = value.astype(BF16)
        wire.send(i, term(i, zo, cut, rest), zbuf.at[i], {"section": zo})
        for one in (outer, inner):
            (one.send_far, one.send_plus, one.send_minus, lambda: None)[i]()
        row_acc[...] += fold(value * ffn[:, span].astype(F32) * ffn_gain[:, span])
    share(2, to_row(row_acc[...] * inv_col[...]))

    def weights():
        for i in range(4):
            span = slice(i * pair, (i + 1) * pair)
            value = contract_rows(act[:, span], acts[:, :hidden])
            gate_grad[0, span, :] = value.astype(BF16)
            yield
            value = contract_rows(act[:, span], acts[:, hidden:])
            up_grad[0, span, :] = value.astype(BF16)
            yield
        down(y2)

    def blend(i):
        wire.got(i, zbuf.at[i], {"section": zo})
        ref = term(i, z, cut, rest)
        ref[...] = add(ref[...], zbuf[i]).astype(BF16)

    def sums():
        outer.relay_plus()
        outer.relay_minus()
        yield
        blend(0)
        last.send_far()
        inner.relay_plus()
        inner.relay_minus()
        yield
        blend(1)
        last.send_plus()
        blend(2)
        last.send_minus()
        yield
        zsend[...] = outer.collect().astype(BF16)
        wire.send(SCATTER8 - 1, zsend, zrecv, {"section": zo})
        yield
        last.relay_plus()
        last.relay_minus()
        yield
        blend(3)
        final[pl.ds(0, cut), :] = inner.collect()
        yield
        final[pl.ds(cut, rest), :] = last.collect()
        yield
        wire.got(SCATTER8 - 1, zrecv, {"section": zo})
        final[pl.ds(0, cut), :] += zrecv[...].astype(F32)

    run_all(weights(), sums())
    inverse = wide(inv_col[...], cols)
    correction = wide(to_column(total_of(2) / width), cols)
    hat = ffn[:, pl.ds(offset, cols)].astype(F32) * inverse
    input_grad[...] = (
        y_own[...].astype(F32)
        + inverse * (ffn_gain[:, pl.ds(offset, cols)] * final[...] - hat * correction)
    ).astype(BF16)
    wire.finish()
    stat_wire.finish()


def tail(dkv, ffn_half, ffn_input, kv_input, residual, kv_gain, ffn_gain, w_key, w_value, w_gate, w_up, w_down):
    rows, cols = kv_input.shape
    width, hidden = w_gate.shape
    cut = rows * 9 // 16
    rest = rows - cut
    kv_cut = rows * 3 // 4
    any_space = pl.BlockSpec(memory_space=pl.ANY)
    in_vmem = pl.BlockSpec(memory_space=VMEM)
    dma = pltpu.SemaphoreType.DMA
    heads = w_key.shape[1]
    return pl.pallas_call(
        tail_kernel,
        name="tail",
        out_shape=(
            VMEM((rows, cols), BF16),
            VMEM((1, cols, heads), BF16),
            VMEM((1, cols, heads), BF16),
            VMEM((1, width, hidden), BF16),
            VMEM((1, width, hidden), BF16),
            VMEM((1, hidden, width), BF16),
        ),
        in_specs=[in_vmem] * 2 + [any_space] * 3 + [in_vmem] * 2 + [any_space] * 5,
        out_specs=(in_vmem,) * 6,
        scratch_shapes=[
            VMEM((2 * rows, HEAD), BF16),
            VMEM((rows // 2, cols), BF16),
            VMEM((2 * rows, heads), BF16),
            VMEM((rows, width), BF16),
            VMEM((rows, cols), BF16),
            VMEM((rows, cols), BF16),
            VMEM((cols, heads), BF16),
            VMEM((cols, heads), BF16),
            VMEM((width, hidden), BF16),
            VMEM((width, hidden), BF16),
            VMEM((hidden, width), BF16),
            VMEM((rows, width), BF16),
            VMEM((rows, hidden), F32),
            VMEM((rows, hidden), F32),
            VMEM((hidden, rows), BF16),
            VMEM((rows, HEAD), F32),
            VMEM((rows, cols), F32),
            VMEM((rows, cols), BF16),
            VMEM((rows, cols), BF16),
            VMEM((rows, width), BF16),
            VMEM((rows, hidden), F32),
            VMEM((rows, 2 * hidden), BF16),
            VMEM((rows, HEAD), F32),
            VMEM((rows, cols), F32),
            VMEM((2, 4, 2, rows, HEAD), BF16),
            VMEM((4, 2, rows - kv_cut, HEAD), BF16),
            VMEM((3, 2, 2, kv_cut, HEAD), BF16),
            VMEM((3, 2, 2, kv_cut, HEAD), BF16),
            VMEM((2, kv_cut, HEAD), BF16),
            VMEM((2, kv_cut, HEAD), BF16),
            VMEM((3, 8, rows), F32),
            VMEM((3, 7, 8, rows), F32),
            VMEM((4, rest, cols), BF16),
            VMEM((3, 2, cut, cols), BF16),
            VMEM((3, 2, cut, cols), BF16),
            VMEM((cut, cols), BF16),
            VMEM((cut, cols), BF16),
            dma((9,)), dma((SCATTER16,)), dma((SCATTER16,)), dma((GATHER8,)), dma((GATHER8,)),
            dma((GATHER8,)), dma((GATHER8,)), dma((GATHER8,)), dma((GATHER8,)),
            dma((SCATTER8,)), dma((SCATTER8,)), dma((21,)), dma((21,)),
        ],
        compiler_params=pltpu.CompilerParams(
            collective_id=3, has_side_effects=True, vmem_limit_bytes=44_000_000
        ),
    )(
        pltpu.with_memory_space_constraint(dkv, VMEM),
        pltpu.with_memory_space_constraint(ffn_half, VMEM),
        ffn_input, kv_input, residual, kv_gain.reshape(1, -1), ffn_gain.reshape(1, -1),
        w_key, w_value, w_gate, w_up, w_down,
    )


MASKED = -1e30
START = -1e29


def attention_kernel(
    bound_ref, seen_ref, q_ref, g_ref, kv_ref, dq_ref, dkv_ref,
    q_cat, g_cat, q_t, g_t, run_max, run_sum, run_dot, dq_t, p_all, d_all, *, tile, scale
):
    rows = q_ref.shape[0]
    group = q_ref.shape[1] // HEAD
    own = lax.axis_index(BLK)
    lowest = bound_ref[0]
    to_log2 = scale * LOG2E
    for h in range(group):
        for src, cat, turned in ((q_ref, q_cat, q_t), (g_ref, g_cat, g_t)):
            block = src[:, h * HEAD : (h + 1) * HEAD]
            cat[h * rows : (h + 1) * rows, :] = block
            turned[:, h * rows : (h + 1) * rows] = block.astype(F32).T.astype(BF16)
    run_max[...] = jnp.full_like(run_max, START)
    run_sum[...] = jnp.zeros_like(run_sum)
    run_dot[...] = jnp.zeros_like(run_dot)
    dq_t[...] = jnp.zeros_like(dq_t)

    tiles = dkv_ref.shape[1] // tile
    first = lowest // tile
    last = ((own + 1) * rows) // tile
    whole_to = (own * rows) // tile
    whole_from = jnp.minimum((lowest + tile - 1) // tile, whole_to)

    def part(j):
        return pl.ds(pl.multiple_of(j * tile, tile), tile)

    def lanes(h):
        return pl.ds(h * rows, rows)

    def scores(j, h, masked):
        keys = kv_ref[0, part(j), :]
        value = jnp.dot(keys, q_t[:, lanes(h)], preferred_element_type=F32) * to_log2
        if masked:
            key_pos = j * tile + lax.broadcasted_iota(jnp.int32, (tile, rows), 0)
            query_pos = own * rows + lax.broadcasted_iota(jnp.int32, (tile, rows), 1)
            visible = (key_pos <= query_pos) & (key_pos >= seen_ref[...])
            value = jnp.where(visible, value, MASKED)
        return value

    def unseen(j, row, masked):
        return row if masked else jnp.where(seen_ref[...] > j * tile, -MASKED, row)

    def products(j, h):
        return jnp.dot(kv_ref[1, part(j), :], g_t[:, lanes(h)], preferred_element_type=F32)

    def stats(j, masked):
        for h in range(group):
            value = scores(j, h, masked).reshape(tile // 8, 8, rows)
            dprobs = products(j, h).reshape(tile // 8, 8, rows)
            before = run_max[:, lanes(h)]
            now = jnp.maximum(before, jnp.max(value, axis=0))
            if not masked:
                now = jnp.where(seen_ref[...] > j * tile, before, now)
            shrink = jnp.exp2(before - now)
            probs = jnp.exp2(value - unseen(j, now, masked)[None])
            run_max[:, lanes(h)] = now
            run_sum[:, lanes(h)] = run_sum[:, lanes(h)] * shrink + jnp.sum(probs, axis=0)
            run_dot[:, lanes(h)] = run_dot[:, lanes(h)] * shrink + jnp.sum(probs * dprobs, axis=0)

    def grads(j, masked):
        keys = kv_ref[0, part(j), :]
        for h in range(group):
            value = scores(j, h, masked)
            probs = jnp.exp2(value - unseen(j, run_max[0:1, lanes(h)], masked))
            p_all[:, lanes(h)] = probs.astype(BF16)
            d_all[:, lanes(h)] = (probs * (products(j, h) - run_dot[0:1, lanes(h)])).astype(BF16)
        dkv_ref[1, part(j), :] = jnp.dot(p_all[...], g_cat[...], preferred_element_type=F32).astype(BF16)
        dkv_ref[0, part(j), :] = (
            jnp.dot(d_all[...], q_cat[...], preferred_element_type=F32) * scale
        ).astype(BF16)
        dq_t[...] += contract_rows(keys, d_all[...])

    def sweep(body):
        lax.fori_loop(first, whole_from, lambda j, _: (body(j, True), 0)[1], 0)
        lax.fori_loop(jnp.maximum(whole_from, first), whole_to, lambda j, _: (body(j, False), 0)[1], 0)
        lax.fori_loop(jnp.maximum(whole_to, first), last, lambda j, _: (body(j, True), 0)[1], 0)

    sweep(stats)
    peak = jnp.max(run_max[...], axis=0, keepdims=True)
    factor = jnp.exp2(run_max[...] - peak)
    total = jnp.sum(run_sum[...] * factor, axis=0, keepdims=True)
    delta = jnp.sum(run_dot[...] * factor, axis=0, keepdims=True) / total
    run_max[0:1, :] = peak + jnp.log(total) * LOG2E
    run_dot[0:1, :] = delta

    def clear(j, _):
        dkv_ref[:, part(j), :] = jnp.zeros((2, tile, HEAD), BF16)
        return 0

    lax.fori_loop(0, first, clear, 0)
    lax.fori_loop(last, tiles, clear, 0)
    sweep(grads)
    for h in range(group):
        dq_ref[:, h * HEAD : (h + 1) * HEAD] = (dq_t[:, lanes(h)] * scale).T.astype(BF16)


def attention(query, out_grad, kv, visible_from, tile=512):
    rows, width = query.shape
    group = width // HEAD
    cat = VMEM((group * rows, HEAD), BF16)
    turned = VMEM((HEAD, group * rows), BF16)
    stat = VMEM((8, group * rows), F32)
    return pl.pallas_call(
        functools.partial(attention_kernel, tile=tile, scale=1.0 / math.sqrt(HEAD)),
        name="attention",
        out_shape=(
            jax.ShapeDtypeStruct((rows, width), BF16),
            VMEM(kv.shape, BF16),
        ),
        in_specs=[pl.BlockSpec(memory_space=pltpu.SMEM)] + [pl.BlockSpec(memory_space=VMEM)] * 4,
        out_specs=(pl.BlockSpec(memory_space=VMEM),) * 2,
        scratch_shapes=[
            cat, cat, turned, turned, stat, stat, stat, VMEM((HEAD, group * rows), F32),
            VMEM((tile, group * rows), BF16), VMEM((tile, group * rows), BF16),
        ],
        compiler_params=pltpu.CompilerParams(vmem_limit_bytes=55_800_000),
    )(
        visible_from, visible_from.reshape(1, rows), query, out_grad,
        pltpu.with_memory_space_constraint(kv, VMEM),
    )


def write_kernel(*refs):
    count = len(refs) // 2
    sem = refs[-1]
    copies = []
    for k in range(count):
        src, dst = refs[k], refs[count + k]
        rows = src.shape[-2]
        for piece in range(2):
            span = pl.ds(piece * rows // 2, rows // 2)
            at = (span,) if len(src.shape) == 2 else (0, span)
            copies.append(pltpu.make_async_copy(src.at[at], dst.at[at], sem.at[2 * k + piece]))
    for copy in copies:
        copy.start()
    for copy in copies:
        copy.wait()


def write_out(arrays):
    return pl.pallas_call(
        write_kernel,
        name="write_out",
        out_shape=tuple(jax.ShapeDtypeStruct(a.shape, a.dtype) for a in arrays),
        in_specs=[pl.BlockSpec(memory_space=VMEM)] * len(arrays),
        out_specs=(pl.BlockSpec(memory_space=pl.ANY),) * len(arrays),
        scratch_shapes=[pltpu.SemaphoreType.DMA((2 * len(arrays),))],
        compiler_params=pltpu.CompilerParams(vmem_limit_bytes=8_000_000),
    )(*[pltpu.with_memory_space_constraint(a, VMEM) for a in arrays])


def on_device(
    query, keys, values, out_grad, visible_from, kv_input, residual_grad, ffn_input,
    kv_gain, ffn_gain, w_key, w_value, w_gate, w_up, w_down,
):
    rows = query.shape[0]
    every, ffn_half = gather_first(keys, values, ffn_input)
    blocks = every.shape[1]
    query_grad, dkv = attention(query, out_grad, every.reshape(2, blocks * rows, HEAD), visible_from)
    rest = tail(
        dkv.reshape(2, blocks, rows, HEAD), ffn_half, ffn_input, kv_input, residual_grad, kv_gain, ffn_gain,
        w_key, w_value, w_gate, w_up, w_down,
    )
    return (query_grad, *write_out(rest))


def solution(mesh):
    finer = Mesh(
        mesh.devices.reshape(4, 2, 2, mesh.shape["kvh"], mesh.shape["section"]),
        (*BLK, *FEAT),
    )
    tokens = P(BLK, FEAT)
    placed = (
        tokens, tokens, tokens, tokens, P(BLK), tokens, tokens, tokens, P(), P(),
        P(FEAT, None), P(FEAT, None), P(None, FEAT), P(None, FEAT), P(FEAT, None),
    )
    return jax.shard_map(
        on_device,
        mesh=finer,
        in_specs=placed,
        out_specs=(
            tokens,
            tokens,
            P(BLK, FEAT, None),
            P(BLK, FEAT, None),
            P(BLK, None, FEAT),
            P(BLK, None, FEAT),
            P(BLK, FEAT, None),
        ),
        check_vma=False,
    )
```
